32 devices in a mesh: dp: 8 (over y, x, core), ctx: 4 (over z).
Axes of the slice: x: 2, y: 2, z: 4, core: 2. Of those that a mesh axis runs over, the one named last changes fastest.
Arguments:
- inputs: bfloat16 [2, 8192, 768], P(None, ('dp', 'ctx')), may hold values from -6 to 6
- cotangent: bfloat16 [2, 8192, 768], P(None, ('dp', 'ctx')), may hold values from -6 to 6
- lengths: int32 [2, 8, 4], P(None, 'dp'), may hold values from 1 to 896, 1024 in all within a row
- send_order: int32 [2, 32, 256], P(None, ('dp', 'ctx')), may hold values from 0 to 255, each once within a row
- norm1_gain: bfloat16 [768], P(('dp', 'ctx')), may hold values from 0.099609375 to 1.8984375
- qkv_weight: bfloat16 [768, 2304], P(('dp', 'ctx')), may hold values from -0.3125 to 0.3125
- out_weight: bfloat16 [768, 768], P(('dp', 'ctx')), may hold values from -1.25 to 1.25
- norm2_gain: bfloat16 [768], P(('dp', 'ctx')), may hold values from 0.099609375 to 1.8984375
- gate_weight: bfloat16 [768, 2048], P(('dp', 'ctx')), may hold values from -0.21875 to 0.21875
- up_weight: bfloat16 [768, 2048], P(('dp', 'ctx')), may hold values from -0.21875 to 0.21875
- down_weight: bfloat16 [2048, 768], P(('dp', 'ctx')), may hold values from -0.1875 to 0.1875
Outputs:
- layer_out: bfloat16 [2, 8192, 768], P(None, ('dp', 'ctx'))
- input_grad: bfloat16 [2, 8192, 768], P(None, ('dp', 'ctx'))
- norm1_grad: float32 [768], P(('dp', 'ctx'))
- qkv_grad: float32 [768, 2304], P(('dp', 'ctx'))
- out_grad: float32 [768, 768], P(('dp', 'ctx'))
- norm2_grad: float32 [768], P(('dp', 'ctx'))
- gate_grad: float32 [768, 2048], P(('dp', 'ctx'))
- up_grad: float32 [768, 2048], P(('dp', 'ctx'))
- down_grad: float32 [2048, 768], P(('dp', 'ctx'))
The draws below stay inside these ranges and needn't reach their ends.
Inputs may be any that keep to these rules, and one draw needn't show every extreme that they name: Each pack's 4 lengths sum to 1024, and the longest of each pack has 896. `send_order`: each row of 256 entries holds every number of 0 to 255 once.
All inputs are finite; a program needn't handle non-finite values.
Results may differ from the reference program's by a relative error of at most 0.015.
The reference program's roundings to bfloat16 on the way count: a program that leaves them out, or rounds other values in their place, can miss the bound.
Values may be sent and summed in bfloat16 or wider, within the bound.
A program may use at most 192 MiB of HBM per device.

```python
import math
import jax
import jax.numpy as jnp
import numpy as np
from jax import lax

D = 768
HEADS = 12
HEAD_DIM = 64
FF = 2048
TOK_DEV = 256
MICRO = 2
SEQS = 4
TOKENS = 8192
GROUP = 1024
MAXLEN = 896
N_DP = 8
N_CTX = 4


def strengthened(values, stream_key, source, target, parts, factor):
    owner, partner = [(jnp.arange(values.shape[dim]) // (values.shape[dim] // parts)).reshape([-1 if axis == dim else 1 for axis in range(values.ndim)]) for dim in (source, target)]
    chosen = jax.random.permutation(stream_key, parts)[partner]
    strong = (owner == chosen) | (owner == (partner + parts // 2) % parts)
    return jnp.where(strong, factor * values, values)


def level_of(stream_key, dims, split, smallest, largest):
    def one(dim, shards_of):
        draws = jax.random.uniform(jax.random.fold_in(jax.random.fold_in(stream_key, 6), dim), (shards_of,), jnp.float32, smallest / len(split), largest / len(split))
        return jnp.repeat(jnp.exp(draws), dims[dim] // shards_of).reshape((-1,) + (1,) * (len(dims) - dim - 1))

    level = one(*split[0])
    for cut in split[1:]:
        level = level * one(*cut)
    return level


def split_up(number_of, total, limit, lean):
    loads = [(1 << 20) // math.isqrt(grade ** lean) + 1 for grade in range(2, number_of + 1)]
    surplus, counts = total - limit - (number_of - 1), [1] * (number_of - 1)
    while surplus > 0:
        candidates = [i for i in range(number_of - 1) if counts[i] < limit]
        whole, remaining = sum([loads[i] for i in candidates]), surplus
        for i in candidates:
            addition = min(limit - counts[i], max(1, remaining * loads[i] // whole), surplus)
            counts[i] = counts[i] + addition
            surplus = surplus - addition
    return np.array([limit] + counts)


def uneven_parts(key, number_of, total, bound, lean):
    if number_of == 2:
        one = jax.random.randint(key, (), max(1, total - bound), min(bound, total - 1) + 1)
        return jnp.stack([one, total - one])
    sizes = jnp.asarray(split_up(number_of, total, bound, lean), jnp.int32)
    twos = (number_of - 1) // 2
    donor, taker = sizes[1:1 + 2 * twos:2], sizes[2:2 + 2 * twos:2]
    margin = jnp.minimum(donor - 1, bound - taker)
    moved = jax.random.randint(jax.random.fold_in(key, 1), (twos,), 0, 1 << 20) % (margin + 1)
    sizes = sizes.at[1:1 + 2 * twos:2].set(donor - moved).at[2:2 + 2 * twos:2].set(taker + moved)
    return sizes[jax.random.permutation(jax.random.fold_in(key, 2), number_of)]


def scatter_about(own_key, dims, width, bound, pieces=(), held_as=jnp.bfloat16):
    entries = jax.random.normal(own_key, dims, jnp.float32) * width
    if len(pieces) > 0:
        entries = level_of(own_key, dims, pieces, -0.22, 0.18) * entries
    return jnp.clip(entries, min=-bound, max=bound).astype(held_as)


def noise_with(own_key, dims, spread, limit, pieces, heavy, kind=jnp.bfloat16):
    values = spread * jax.random.normal(own_key, dims, jnp.float32)
    if pieces:
        values = values * level_of(own_key, dims, pieces, -0.22, 0.18)
    return jnp.clip(strengthened(values, jax.random.fold_in(own_key, 3), *heavy), -limit, limit).astype(kind)


def setup_inputs(seed: int = 0) -> dict:
    key_list = jax.random.split(jax.random.key(seed), 12)
    inputs = noise_with(key_list[0], (MICRO, TOKENS, D), 1.0, 6.0, ((1, 32),), (1, 2, 32, 2.75))
    cotangent = scatter_about(key_list[1], (MICRO, TOKENS, D), 1.0, 6.0, ((1, 32),))
    lengths = jax.vmap(lambda own: uneven_parts(own, SEQS, GROUP, MAXLEN, 2))(jax.random.split(key_list[2], MICRO * N_DP)).reshape((MICRO, N_DP, SEQS)).astype(jnp.int32)
    send_order = jax.vmap(lambda own: jax.random.permutation(own, TOK_DEV))(jax.random.split(key_list[3], MICRO * (N_DP * N_CTX))).reshape((MICRO, N_DP * N_CTX, TOK_DEV)).astype(jnp.int32)
    norm1_gain = jnp.clip(1.0 + 0.18 * jax.random.normal(key_list[4], (D,), jnp.float32), 0.099609375, 1.8984375).astype(jnp.bfloat16)
    qkv_weight = scatter_about(key_list[5], (D, 3 * D), (D // 2) ** -0.5, 0.3125, ((0, 32),))
    out_weight = scatter_about(key_list[6], (D, D), (D // 32) ** -0.5, 1.25, ((0, 32),))
    norm2_gain = jnp.clip(1.0 + 0.18 * jax.random.normal(key_list[7], (D,), jnp.float32), 0.099609375, 1.8984375).astype(jnp.bfloat16)
    gate_weight = scatter_about(key_list[8], (D, FF), D ** -0.5, 0.21875, ((0, 32),))
    up_weight = scatter_about(key_list[9], (D, FF), D ** -0.5, 0.21875, ((0, 32),))
    down_weight = scatter_about(key_list[10], (FF, D), (FF // 2) ** -0.5, 0.1875, ((0, 32),))
    return dict(inputs=inputs, cotangent=cotangent, lengths=lengths, send_order=send_order, norm1_gain=norm1_gain, qkv_weight=qkv_weight, out_weight=out_weight, norm2_gain=norm2_gain, gate_weight=gate_weight, up_weight=up_weight, down_weight=down_weight)


eps_norm = 1e-05
rope_base = 10000.0

@jax.custom_vjp
def low(v):
    return lax.optimization_barrier(v.astype(jnp.bfloat16)).astype(jnp.float32)

@jax.custom_vjp
def low_back(v):
    return v

def low_keep(v):
    return (low(v), None)

def low_pass(kept, grad):
    return (grad,)

def back_keep(v):
    return (v, None)

def back_low(kept, grad):
    return (low(grad),)
low.defvjp(low_keep, low_pass)
low_back.defvjp(back_keep, back_low)

def matmul_high(left, right):
    return jnp.dot(left, right, precision=lax.Precision.HIGHEST)

def scaled_norm(values, gain):
    inverse = lax.rsqrt(lax.optimization_barrier(jnp.mean(values * values, axis=-1, keepdims=True)) + eps_norm)
    return values * inverse * gain

def pack_layout(seq_lengths, row_ids):
    seq_ends = jnp.cumsum(seq_lengths).astype(jnp.int32)
    passed = (row_ids[:, None] >= seq_ends[None, :]).astype(jnp.int32)
    segment = lax.optimization_barrier(jnp.sum(passed, axis=1)).astype(jnp.int32)
    seq_start = lax.optimization_barrier(jnp.sum(passed * seq_lengths[None, :], axis=1)).astype(jnp.int32)
    return (segment, row_ids - seq_start)

def rope_tables(position, head_size):
    half_dim = head_size // 2
    frequency = rope_base ** (-(jnp.arange(half_dim, dtype=jnp.float32) * 2.0 / head_size))
    angles = position.astype(jnp.float32)[:, None] * frequency[None, :]
    return (jnp.cos(angles), jnp.sin(angles))

def rotate(values, cosine, sine, head_count):
    shaped = values.reshape(values.shape[0], head_count, -1)
    half_dim = shaped.shape[-1] // 2
    first_half = shaped[..., :half_dim]
    second_half = shaped[..., half_dim:]
    cos_wide = cosine[:, None, :]
    sin_wide = sine[:, None, :]
    turned = jnp.concatenate([first_half * cos_wide - second_half * sin_wide, second_half * cos_wide + first_half * sin_wide], axis=-1)
    return turned.reshape(values.shape)

def layer_forward(params, block_x, seq_lengths):
    gain1, wqkv, wout, gain2, wgate, wup, wdown = params
    row_ids = jnp.arange(GROUP, dtype=jnp.int32)
    segment, position = pack_layout(seq_lengths, row_ids)
    cosine, sine = rope_tables(position, HEAD_DIM)
    normed1 = low(scaled_norm(block_x, gain1))
    qkv = low_back(matmul_high(normed1, wqkv))
    queries = low(rotate(qkv[:, :D], cosine, sine, HEADS))
    keys = low(rotate(qkv[:, D:2 * D], cosine, sine, HEADS))
    values = low(qkv[:, 2 * D:])
    block_rows = min(512, GROUP)
    block_count = GROUP // block_rows
    query_blocks = queries.reshape(block_count, block_rows, HEADS, HEAD_DIM)
    keys_three = keys.reshape(GROUP, HEADS, HEAD_DIM)
    values_three = values.reshape(GROUP, HEADS, HEAD_DIM)
    score_scale = HEAD_DIM ** (-0.5)

    def attend(member):
        block_q, block_index = member
        start = block_index * block_rows
        q_rows = start + jnp.arange(block_rows, dtype=jnp.int32)
        q_segment = lax.dynamic_slice_in_dim(segment, start, block_rows)
        allowed = (q_segment[:, None] == segment[None, :]) & (row_ids[None, :] <= q_rows[:, None])
        scores = jnp.einsum('qhd,khd->hqk', block_q, keys_three, precision=lax.Precision.HIGHEST)
        scores = jnp.where(allowed[None], low_back(scores * score_scale), -jnp.inf)
        soft_probs = low(jax.nn.softmax(scores, axis=-1))
        mixture = jnp.einsum('hqk,khd->qhd', soft_probs, values_three, precision=lax.Precision.HIGHEST)
        return mixture.reshape(block_rows, D)
    mixed = lax.map(jax.checkpoint(attend), (query_blocks, jnp.arange(block_count, dtype=jnp.int32)))
    attended = low(low_back(mixed.reshape(GROUP, D)))
    hidden = block_x + low_back(matmul_high(attended, wout))
    normed2 = low(scaled_norm(hidden, gain2))
    gate_value = low_back(matmul_high(normed2, wgate))
    up_value = low_back(matmul_high(normed2, wup))
    inner_act = low(jax.nn.silu(gate_value) * up_value)
    return hidden + low_back(matmul_high(inner_act, wdown))

def reference(inputs, cotangent, lengths, send_order, norm1_gain, qkv_weight, out_weight, norm2_gain, gate_weight, up_weight, down_weight):
    params = (norm1_gain.astype(jnp.float32), qkv_weight.astype(jnp.float32), out_weight.astype(jnp.float32), norm2_gain.astype(jnp.float32), gate_weight.astype(jnp.float32), up_weight.astype(jnp.float32), down_weight.astype(jnp.float32))
    slot_rows = TOK_DEV // N_DP
    row_order = send_order.reshape(MICRO, N_DP, N_CTX, TOK_DEV).astype(jnp.int32)

    def to_groups(array):
        natural = array.reshape(MICRO, N_DP, N_CTX, TOK_DEV, D)
        sent_rows = jnp.take_along_axis(natural, row_order[..., None], axis=3)
        sent_rows = sent_rows.reshape(MICRO, N_DP, N_CTX, N_DP, slot_rows, D)
        placed = jnp.transpose(sent_rows, (0, 3, 2, 1, 4, 5))
        return placed.reshape(MICRO * N_DP, GROUP, D)

    def from_groups(array):
        placed = array.reshape(MICRO, N_DP, N_CTX, N_DP, slot_rows, D)
        sent_rows = jnp.transpose(placed, (0, 3, 2, 1, 4, 5)).reshape(MICRO, N_DP, N_CTX, TOK_DEV, D)
        inverse = jnp.argsort(row_order, axis=-1).astype(jnp.int32)
        natural = jnp.take_along_axis(sent_rows, inverse[..., None], axis=3)
        return natural.reshape(MICRO, TOKENS, D)
    groups_x = to_groups(inputs.astype(jnp.float32))
    groups_dy = to_groups(cotangent.astype(jnp.float32))
    group_lengths = lengths.reshape(MICRO * N_DP, SEQS).astype(jnp.int32)

    def one_group(running, member):
        block_x, block_dy, block_lengths = member
        block_out, pullback = jax.vjp(lambda weights, rows_in: layer_forward(weights, rows_in, block_lengths), params, block_x)
        grad_params, grad_rows = pullback(block_dy)
        running = jax.tree.map(lambda first_sum, second_sum: first_sum + second_sum, running, grad_params)
        return (running, (block_out, grad_rows))
    zero_grads = tuple((jnp.zeros(weight.shape, jnp.float32) for weight in params))
    totals, (outs_all, grads_all) = lax.scan(one_group, zero_grads, (groups_x, groups_dy, group_lengths))
    return (from_groups(outs_all).astype(jnp.bfloat16), from_groups(grads_all).astype(jnp.bfloat16), totals[0], totals[1], totals[2], totals[3], totals[4], totals[5], totals[6])
```

```python
import functools

import jax
import jax.numpy as jnp
from jax import lax
from jax.experimental import pallas as pl
from jax.experimental.pallas import tpu as pltpu
from jax.sharding import PartitionSpec as P

HEADS = 12
BLK = 256
SLOTS = 8
eps_norm = 1e-05
rope_base = 10000.0
MESH = pl.DeviceIdType.MESH
F32, BF16 = jnp.float32, jnp.bfloat16
NT = (((1,), (1,)), ((), ()))
TN = (((0,), (0,)), ((), ()))
ANY = pl.BlockSpec(memory_space=pl.ANY)
VM = pl.BlockSpec(memory_space=pltpu.VMEM)
SM = pl.BlockSpec(memory_space=pltpu.SMEM)


class Place:
    def __init__(self, ndp, nctx):
        self.ndp, self.nctx = ndp, nctx
        self.nb = 2
        self.na = ndp // 4
        self.g = nctx // 2
        self.gz = nctx // 4
        self.dp = lax.axis_index("dp")
        self.ctx = lax.axis_index("ctx")
        self.k, self.core = self.dp // 2, self.dp % 2
        self.ya, self.xb = self.k // self.nb, self.k % self.nb
        self.me = self.dp * nctx + self.ctx
        self.pack = self.ctx // self.gz
        self.j = self.core * self.gz + self.ctx % self.gz

    def member(self, j):
        return (self.k * 2 + j // self.gz, self.pack * self.gz + j % self.gz)

    def holder(self, m, d, c):
        j = jnp.where(c < self.g, c, 2 * self.g - 1 - c)
        return ((d // 2) * 2 + j // self.gz, (m * 2 + d % 2) * self.gz + j % self.gz)

    def dp_of(self, ya, xb, core):
        return (ya * self.nb + xb) * 2 + core


def entry_barrier(pc):
    total = pc.ndp * pc.nctx
    barrier = pltpu.get_barrier_semaphore()

    def greet(i, carry):
        other = (pc.me + i) % total
        pl.semaphore_signal(
            barrier, inc=1, device_id=(other // pc.nctx, other % pc.nctx), device_id_type=MESH
        )
        return carry

    lax.fori_loop(1, total, greet, 0)
    pl.semaphore_wait(barrier, total - 1)


def remote(src, dst, ss, rs, dev):
    return pltpu.make_async_remote_copy(
        src_ref=src, dst_ref=dst, send_sem=ss, recv_sem=rs, device_id=dev, device_id_type=MESH
    )


def gather_kernel(ndp, nctx, nt, x_ref, dy_ref, order_ref, len_ref, *refs):
    shards = refs[:nt]
    gx_ref, gdy_ref, plen_ref = refs[nt : nt + 3]
    full = refs[nt + 3 : nt + 3 + nt]
    (
        perm, tok_ss, tok_rs, len_ss, len_rs, own_sem,
        z_ss, z_rs, x_ss, x_rs, y_ss, y_rs, fa_ss, fa_rs, fb_ss, fb_rs, c_ss, c_rs,
    ) = refs[nt + 3 + nt :]
    pc = Place(ndp, nctx)
    na, nb = pc.na, pc.nb
    slot = BLK // ndp
    entry_barrier(pc)

    def block(t, dp, part=None):
        if part is None:
            return full[t].at[pl.ds(dp * nctx, nctx)]
        return full[t].at[pl.ds(dp * nctx + part * (nctx // 2), nctx // 2)]

    pending = []

    def z_copies(t):
        out = []
        for d in range(1, nctx):
            out.append(
                remote(
                    shards[t],
                    full[t].at[pc.me],
                    z_ss.at[t, d - 1],
                    z_rs.at[t, d - 1],
                    (pc.dp, (pc.ctx + d) % nctx),
                )
            )
        return out

    def own_copy(t):
        return pltpu.make_async_copy(shards[t], full[t].at[pc.me], own_sem.at[t])

    def x_copies(t):
        return [
            remote(
                block(t, pc.dp), block(t, pc.dp), x_ss.at[t, d - 1], x_rs.at[t, d - 1],
                (pc.dp_of(pc.ya, (pc.xb + d) % nb, pc.core), pc.ctx),
            )
            for d in range(1, nb)
        ]

    def y_copies(t):
        return [
            remote(
                block(t, pc.dp), block(t, pc.dp), y_ss.at[t, d - 1], y_rs.at[t, d - 1],
                (pc.dp_of((pc.ya + d) % na, pc.xb, pc.core), pc.ctx),
            )
            for d in range(1, na)
        ]

    def forward_copies(t):
        out = []
        for dx in range(1, nb):
            for dy in range(1, na):
                src = pc.dp_of(pc.ya, (pc.xb + nb - dx) % nb, pc.core)
                out.append(
                    remote(
                        block(t, src, 0), block(t, src, 0),
                        fa_ss.at[t, dx - 1, dy - 1], fa_rs.at[t, dx - 1, dy - 1],
                        (pc.dp_of((pc.ya + dy) % na, pc.xb, pc.core), pc.ctx),
                    )
                )
                src = pc.dp_of((pc.ya + na - dy) % na, pc.xb, pc.core)
                out.append(
                    remote(
                        block(t, src, 1), block(t, src, 1),
                        fb_ss.at[t, dx - 1, dy - 1], fb_rs.at[t, dx - 1, dy - 1],
                        (pc.dp_of(pc.ya, (pc.xb + dx) % nb, pc.core), pc.ctx),
                    )
                )
        return out

    def core_copy(t, dy, dx):
        src = pc.dp_of((pc.ya + na - dy) % na, (pc.xb + nb - dx) % nb, pc.core)
        return remote(
            block(t, src), block(t, src), c_ss.at[t, dy, dx], c_rs.at[t, dy, dx],
            (pc.k * 2 + 1 - pc.core, pc.ctx),
        )

    def start(copies):
        for cp in copies:
            cp.start()
            pending.append(cp)

    def token_copies(t, m, d):
        dp_to, ctx_to = pc.holder(m, d, pc.ctx)
        half = jnp.where(pc.ctx < pc.g, 0, 1)
        src = perm.at[t, m, pl.ds(pl.multiple_of(d * slot, slot), slot)]
        dst = (gx_ref, gdy_ref)[t].at[
            pl.ds(pl.multiple_of(half * BLK + pc.dp * slot, slot), slot)
        ]
        rs = tok_rs.at[t, half, pc.dp]
        same = (dp_to == pc.dp) & (ctx_to == pc.ctx)
        return (
            same,
            pltpu.make_async_copy(src, dst, rs),
            remote(src, dst, tok_ss.at[t, m, d], rs, (dp_to, ctx_to)),
        )

    def send_tokens(t, source):
        for m in range(2):
            order = order_ref[m]
            hot = (lax.broadcasted_iota(jnp.int32, (BLK, BLK), 1) == order).astype(BF16)
            perm[t, m] = jnp.dot(hot, source[m], preferred_element_type=F32).astype(BF16)

            def one(d, carry):
                same, near, far = token_copies(t, m, d)

                @pl.when(same)
                def _():
                    near.start()

                @pl.when(jnp.logical_not(same))
                def _():
                    far.start()

                return carry

            lax.fori_loop(0, ndp, one, 0)

    for t in range(nt):
        own_copy(t).start()
    start(z_copies(0))
    send_tokens(0, x_ref)
    len_copy = remote(len_ref, plen_ref, len_ss, len_rs, (pc.k * 2 + 1 - pc.core, pc.ctx))
    len_copy.start()
    start(z_copies(1))

    def got_xy(t):
        for cp in x_copies(t) + y_copies(t):
            cp.wait_recv()
        start(forward_copies(t))
        start([core_copy(t, 0, dx) for dx in range(1, nb)])
        start([core_copy(t, dy, 0) for dy in range(1, na)])

    def got_forward(t):
        for cp in forward_copies(t):
            cp.wait_recv()
        start([core_copy(t, dy, dx) for dy in range(1, na) for dx in range(1, nb)])

    for t in range(nt + 2):
        if t < nt:
            own_copy(t).wait()
            for cp in z_copies(t):
                cp.wait_recv()
            start(x_copies(t) + y_copies(t))
            start([core_copy(t, 0, 0)])
            if t + 2 < nt:
                start(z_copies(t + 2))
            if t + 2 == nt:
                send_tokens(1, dy_ref)
        if 1 <= t <= nt:
            got_xy(t - 1)
        if t >= 2:
            got_forward(t - 2)

    for t in range(nt):
        for dy in range(na):
            for dx in range(nb):
                core_copy(t, dy, dx).wait_recv()
    for cp in pending:
        cp.wait_send()
    len_copy.wait()
    for t in range(2):
        for m in range(2):

            def sent(d, carry):
                same, _near, far = token_copies(t, m, d)

                @pl.when(jnp.logical_not(same))
                def _():
                    far.wait_send()

                return carry

            lax.fori_loop(0, ndp, sent, 0)
        for half in range(2):

            def arrived(b, carry):
                dst = (gx_ref, gdy_ref)[t].at[
                    pl.ds(pl.multiple_of(half * BLK + b * slot, slot), slot)
                ]
                pltpu.make_async_copy(dst, dst, tok_rs.at[t, half, b]).wait()
                return carry

            lax.fori_loop(0, ndp, arrived, 0)


def gather_all(ndp, nctx, x, dy, order, lens, shards):
    nt = len(shards)
    n_all = ndp * nctx
    na, nb = ndp // 4, 2
    width = x.shape[-1]
    dma = pltpu.SemaphoreType.DMA
    return pl.pallas_call(
        functools.partial(gather_kernel, ndp, nctx, nt),
        out_shape=[
            jax.ShapeDtypeStruct((2 * BLK, width), BF16),
            jax.ShapeDtypeStruct((2 * BLK, width), BF16),
            jax.ShapeDtypeStruct(lens.shape, lens.dtype),
        ]
        + [jax.ShapeDtypeStruct((n_all,) + s.shape, s.dtype) for s in shards],
        in_specs=[VM, VM, VM, ANY] + [ANY] * nt,
        out_specs=[ANY] * (3 + nt),
        scratch_shapes=[
            pltpu.VMEM((2, 2, BLK, width), BF16),
            dma((2, 2, ndp)), dma((2, 2, ndp)), dma, dma, dma((nt,)),
            dma((nt, nctx - 1)), dma((nt, nctx - 1)),
            dma((nt, nb - 1)), dma((nt, nb - 1)),
            dma((nt, na - 1)), dma((nt, na - 1)),
            dma((nt, nb - 1, na - 1)), dma((nt, nb - 1, na - 1)),
            dma((nt, nb - 1, na - 1)), dma((nt, nb - 1, na - 1)),
            dma((nt, na, nb)), dma((nt, na, nb)),
        ],
        compiler_params=pltpu.CompilerParams(
            collective_id=0, has_side_effects=True, vmem_limit_bytes=32 << 20
        ),
        name="gather_all",
    )(x, dy, order, lens, *shards)


def scatter_kernel(ndp, nctx, nt, out_ref, gin_ref, order_ref, *refs):
    grads = refs[:nt]
    fin_out, fin_gin = refs[nt : nt + 2]
    shares = refs[nt + 2 : nt + 2 + nt]
    rest = refs[nt + 2 + nt :]
    from_core, diag_a, diag_b, from_x, from_y, own, zsend, zrecv = (
        rest[i * nt : (i + 1) * nt] for i in range(8)
    )
    h = nctx // 2
    (
        tok, tok_ss, tok_rs, c_ss, c_rs, da_ss, da_rs, db_ss, db_rs,
        x_ss, x_rs, y_ss, y_rs, z_ss, z_rs,
    ) = rest[8 * nt :]
    pc = Place(ndp, nctx)
    na, nb = pc.na, pc.nb
    slot = BLK // ndp
    entry_barrier(pc)
    pending = []

    def start(copies):
        for cp in copies:
            cp.start()
            pending.append(cp)

    def token_copies(t, half, b):
        c = jnp.where(half == 0, pc.j, 2 * pc.g - 1 - pc.j)
        d = pc.k * 2 + pc.pack % 2
        m = pc.pack // 2
        src = (out_ref, gin_ref)[t].at[
            pl.ds(pl.multiple_of(half * BLK + b * slot, slot), slot)
        ]
        dst = tok.at[t, m, pl.ds(pl.multiple_of(d * slot, slot), slot)]
        rs = tok_rs.at[t, m, d]
        same = (b == pc.dp) & (c == pc.ctx)
        return (
            same,
            pltpu.make_async_copy(src, dst, rs),
            remote(src, dst, tok_ss.at[t, half, b], rs, (b, c)),
        )

    def send_tokens(t):
        for half in range(2):

            def one(b, carry):
                same, near, far = token_copies(t, half, b)

                @pl.when(same)
                def _():
                    near.start()

                @pl.when(jnp.logical_not(same))
                def _():
                    far.start()

                return carry

            lax.fori_loop(0, ndp, one, 0)

    def place_tokens(t, fin):
        for half in range(2):

            def sent(b, carry):
                same, near, far = token_copies(t, half, b)

                @pl.when(jnp.logical_not(same))
                def _():
                    far.wait_send()

                return carry

            lax.fori_loop(0, ndp, sent, 0)
        for m in range(2):

            def arrived(d, carry):
                dst = tok.at[t, m, pl.ds(pl.multiple_of(d * slot, slot), slot)]
                pltpu.make_async_copy(dst, dst, tok_rs.at[t, m, d]).wait()
                return carry

            lax.fori_loop(0, ndp, arrived, 0)
            order = order_ref[m]
            hot = (lax.broadcasted_iota(jnp.int32, (BLK, BLK), 0) == order).astype(BF16)
            fin[m] = jnp.dot(hot, tok[t, m], preferred_element_type=F32).astype(BF16)

    def core_copy(t, dy, dx):
        k = ((pc.ya + dy) % na) * nb + (pc.xb + dx) % nb
        src = grads[t].at[pl.ds((k * 2 + 1 - pc.core) * nctx, nctx)]
        return remote(
            src, from_core[t].at[dy, dx], c_ss.at[t, dy, dx], c_rs.at[t, dy, dx],
            (pc.k * 2 + 1 - pc.core, pc.ctx),
        )

    def add_core(t, dy, dx):
        k = ((pc.ya + dy) % na) * nb + (pc.xb + dx) % nb
        mine = grads[t][pl.ds((k * 2 + pc.core) * nctx, nctx)].astype(F32)
        both = mine + from_core[t][dy, dx].astype(F32)
        if dy == 0 and dx == 0:
            own[t][...] = both
        else:
            from_core[t][dy, dx] = both.astype(BF16)

    def diag_copies(t):
        out = []
        for dy in range(1, na):
            for dx in range(1, nb):
                out.append(
                    remote(
                        from_core[t].at[dy, dx, pl.ds(0, h)], diag_a[t].at[dy - 1, dx - 1],
                        da_ss.at[t, dy - 1, dx - 1], da_rs.at[t, dy - 1, dx - 1],
                        (pc.dp_of((pc.ya + dy) % na, pc.xb, pc.core), pc.ctx),
                    )
                )
                out.append(
                    remote(
                        from_core[t].at[dy, dx, pl.ds(h, h)], diag_b[t].at[dy - 1, dx - 1],
                        db_ss.at[t, dy - 1, dx - 1], db_rs.at[t, dy - 1, dx - 1],
                        (pc.dp_of(pc.ya, (pc.xb + dx) % nb, pc.core), pc.ctx),
                    )
                )
        return out

    def add_diag(t):
        for dx in range(1, nb):
            part = from_core[t][0, dx, pl.ds(0, h)].astype(F32)
            for dy in range(1, na):
                part = part + diag_a[t][dy - 1, dx - 1].astype(F32)
            from_core[t][0, dx, pl.ds(0, h)] = part.astype(BF16)
        for dy in range(1, na):
            part = from_core[t][dy, 0, pl.ds(h, h)].astype(F32)
            for dx in range(1, nb):
                part = part + diag_b[t][dy - 1, dx - 1].astype(F32)
            from_core[t][dy, 0, pl.ds(h, h)] = part.astype(BF16)

    def xy_copies(t):
        out = []
        for dx in range(1, nb):
            out.append(
                remote(
                    from_core[t].at[0, dx], from_x[t].at[dx - 1],
                    x_ss.at[t, dx - 1], x_rs.at[t, dx - 1],
                    (pc.dp_of(pc.ya, (pc.xb + dx) % nb, pc.core), pc.ctx),
                )
            )
        for dy in range(1, na):
            out.append(
                remote(
                    from_core[t].at[dy, 0], from_y[t].at[dy - 1],
                    y_ss.at[t, dy - 1], y_rs.at[t, dy - 1],
                    (pc.dp_of((pc.ya + dy) % na, pc.xb, pc.core), pc.ctx),
                )
            )
        return out

    def add_xy(t):
        total = own[t][...]
        for i in range(nb - 1):
            total = total + from_x[t][i].astype(F32)
        for i in range(na - 1):
            total = total + from_y[t][i].astype(F32)
        own[t][...] = total
        zsend[t][...] = total.astype(BF16)

    def z_copies(t):
        return [
            remote(
                zsend[t].at[(pc.ctx + d) % nctx], zrecv[t].at[d - 1],
                z_ss.at[t, d - 1], z_rs.at[t, d - 1], (pc.dp, (pc.ctx + d) % nctx),
            )
            for d in range(1, nctx)
        ]

    def add_z(t):
        total = own[t][pc.ctx]
        for i in range(nctx - 1):
            total = total + zrecv[t][i].astype(F32)
        shares[t][...] = total

    order_yx = [(dy, dx) for dy in range(1, na) for dx in range(1, nb)]
    order_yx += [(0, dx) for dx in range(1, nb)] + [(dy, 0) for dy in range(1, na)] + [(0, 0)]

    send_tokens(0)
    for t in range(nt):
        start([core_copy(t, dy, dx) for dy, dx in order_yx])
    for t in range(nt + 3):
        if t < nt:
            for dy, dx in order_yx:
                core_copy(t, dy, dx).wait_recv()
                add_core(t, dy, dx)
            start(diag_copies(t))
        if 1 <= t <= nt:
            for cp in diag_copies(t - 1):
                cp.wait_recv()
            add_diag(t - 1)
            start(xy_copies(t - 1))
        if 2 <= t <= nt + 1:
            for cp in xy_copies(t - 2):
                cp.wait_recv()
            add_xy(t - 2)
            start(z_copies(t - 2))
        if t == 1:
            send_tokens(1)
        if t == 3:
            place_tokens(0, fin_out)
        if t >= 3:
            for cp in z_copies(t - 3):
                cp.wait_recv()
            add_z(t - 3)
    place_tokens(1, fin_gin)
    for cp in pending:
        cp.wait_send()


def scatter_all(ndp, nctx, out, gin, order, grads):
    nt = len(grads)
    na, nb = ndp // 4, 2
    width = out.shape[-1]
    dma = pltpu.SemaphoreType.DMA
    scratch = []
    spec = [g.shape[1:] for g in grads]
    scratch += [pltpu.VMEM((na, nb, nctx) + s, BF16) for s in spec]
    scratch += [pltpu.VMEM((na - 1, nb - 1, nctx // 2) + s, BF16) for s in spec]
    scratch += [pltpu.VMEM((na - 1, nb - 1, nctx // 2) + s, BF16) for s in spec]
    scratch += [pltpu.VMEM((nb - 1, nctx) + s, BF16) for s in spec]
    scratch += [pltpu.VMEM((na - 1, nctx) + s, BF16) for s in spec]
    scratch += [pltpu.VMEM((nctx,) + s, F32) for s in spec]
    scratch += [pltpu.VMEM((nctx,) + s, BF16) for s in spec]
    scratch += [pltpu.VMEM((nctx - 1,) + s, BF16) for s in spec]
    scratch += [
        pltpu.VMEM((2, 2, BLK, width), BF16),
        dma((2, 2, ndp)), dma((2, 2, ndp)),
        dma((nt, na, nb)), dma((nt, na, nb)),
        dma((nt, na - 1, nb - 1)), dma((nt, na - 1, nb - 1)),
        dma((nt, na - 1, nb - 1)), dma((nt, na - 1, nb - 1)),
        dma((nt, nb - 1)), dma((nt, nb - 1)),
        dma((nt, na - 1)), dma((nt, na - 1)),
        dma((nt, nctx - 1)), dma((nt, nctx - 1)),
    ]
    return pl.pallas_call(
        functools.partial(scatter_kernel, ndp, nctx, nt),
        out_shape=[jax.ShapeDtypeStruct((2, BLK, width), BF16)] * 2
        + [jax.ShapeDtypeStruct(s, F32) for s in spec],
        in_specs=[VM] * (3 + nt),
        out_specs=[VM] * (2 + nt),
        scratch_shapes=scratch,
        compiler_params=pltpu.CompilerParams(
            collective_id=1, has_side_effects=True, vmem_limit_bytes=60 << 20
        ),
        name="scatter_all",
    )(out, gin, order, *grads)


def group_barrier(pc):
    barrier = pltpu.get_barrier_semaphore()
    for o in range(1, pc.g):
        pl.semaphore_signal(
            barrier, inc=1, device_id=pc.member((pc.j + o) % pc.g), device_id_type=MESH
        )
    pl.semaphore_wait(barrier, pc.g - 1)


def block_at(ref, index, size=BLK):
    return ref.at[pl.ds(pl.multiple_of(index * size, size), size)]


def kv_kernel(ndp, nctx, kv_ref, all_ref, own_sem, ss, rs):
    pc = Place(ndp, nctx)
    group_barrier(pc)
    copies = []
    for half in range(2):
        where = pc.j if half == 0 else 2 * pc.g - 1 - pc.j
        src, dst = block_at(kv_ref, half), block_at(all_ref, where)
        for o in range(1, pc.g):
            copies.append(
                remote(src, dst, ss.at[half, o - 1], rs.at[half, o - 1], pc.member((pc.j + o) % pc.g))
            )
        copies.append(pltpu.make_async_copy(src, dst, own_sem.at[half]))
    for cp in copies:
        cp.start()
    for cp in copies:
        cp.wait()


def share_kv(ndp, nctx, kv):
    g = nctx // 2
    dma = pltpu.SemaphoreType.DMA
    return pl.pallas_call(
        functools.partial(kv_kernel, ndp, nctx),
        out_shape=jax.ShapeDtypeStruct((g * kv.shape[0], kv.shape[1]), kv.dtype),
        in_specs=[ANY],
        out_specs=ANY,
        scratch_shapes=[dma((2,)), dma((2, g - 1)), dma((2, g - 1))],
        compiler_params=pltpu.CompilerParams(
            collective_id=2, has_side_effects=True, vmem_limit_bytes=16 << 20
        ),
        name="share_kv",
    )(kv)


def dkv_kernel(ndp, nctx, part_ref, sum_ref, got, ss, rs):
    pc = Place(ndp, nctx)
    group_barrier(pc)
    copies = []
    for o in range(1, pc.g):
        to = (pc.j + o) % pc.g
        for half in range(2):
            where = to if half == 0 else 2 * pc.g - 1 - to
            copies.append(
                remote(
                    block_at(part_ref, where), got.at[o - 1, half],
                    ss.at[half, o - 1], rs.at[half, o - 1], pc.member(to),
                )
            )
    for cp in copies:
        cp.start()
    for cp in copies:
        cp.wait()
    for half in range(2):
        where = pc.j if half == 0 else 2 * pc.g - 1 - pc.j
        total = part_ref[pl.ds(pl.multiple_of(where * BLK, BLK), BLK)].astype(F32)
        for o in range(1, pc.g):
            total = total + got[o - 1, half].astype(F32)
        sum_ref[half * BLK : (half + 1) * BLK] = total


def sum_dkv(ndp, nctx, part):
    g = nctx // 2
    width = part.shape[1]
    dma = pltpu.SemaphoreType.DMA
    return pl.pallas_call(
        functools.partial(dkv_kernel, ndp, nctx),
        out_shape=jax.ShapeDtypeStruct((2 * BLK, width), F32),
        in_specs=[VM],
        out_specs=VM,
        scratch_shapes=[
            pltpu.VMEM((g - 1, 2, BLK, width), BF16), dma((2, g - 1)), dma((2, g - 1)),
        ],
        compiler_params=pltpu.CompilerParams(
            collective_id=3, has_side_effects=True, vmem_limit_bytes=32 << 20
        ),
        name="sum_dkv",
    )(part)


NEG = -1e30


def lane_mask(h):
    lanes = lax.broadcasted_iota(jnp.int32, (1, 128), 1)
    return (lanes < 64) if h == 0 else (lanes >= 64)


def fill_bias(qi, nk, blk, segk_ref, segq_ref, bias):
    segq = segq_ref[:, qi * BLK : (qi + 1) * BLK]
    qrow = blk * BLK + lax.broadcasted_iota(jnp.int32, (BLK, BLK), 1)

    def one(kb, carry):
        segk = segk_ref[pl.ds(pl.multiple_of(kb * BLK, BLK), BLK)]
        krow = kb * BLK + lax.broadcasted_iota(jnp.int32, (BLK, BLK), 0)
        bias[kb] = jnp.where((segk == segq) & (krow <= qrow), 0.0, NEG)
        return carry

    lax.fori_loop(0, nk, one, 0)


def tile(ref, kb, col):
    return ref[pl.ds(pl.multiple_of(kb * BLK, BLK), BLK), pl.ds(pl.multiple_of(col, 128), 128)]


def attend_kernel(blk_ref, q_ref, kv_ref, segk_ref, segq_ref, o_ref, lse_ref, bias, sbuf):
    width = q_ref.shape[1]
    for qi in range(2):
        blk = blk_ref[qi]
        nk = blk + 1
        fill_bias(qi, nk, blk, segk_ref, segq_ref, bias)

        def pair(hp, carry):
            qp = q_ref[qi * BLK : (qi + 1) * BLK, pl.ds(pl.multiple_of(hp * 128, 128), 128)]
            outs = []
            for h in range(2):
                qm = jnp.where(lane_mask(h), qp, 0) * 0.125
                qm = qm.astype(BF16)

                def score(kb, top):
                    s = lax.dot_general(
                        tile(kv_ref, kb, hp * 128), qm, NT, preferred_element_type=F32
                    )
                    s = s + bias[kb]
                    sbuf[kb] = s
                    return jnp.maximum(top, jnp.max(s, axis=0, keepdims=True))

                top = lax.fori_loop(0, nk, score, jnp.full((1, BLK), NEG, F32))

                def expo(kb, total):
                    p = jnp.exp(sbuf[kb] - top)
                    sbuf[kb] = p
                    return total + jnp.sum(p, axis=0, keepdims=True)

                total = lax.fori_loop(0, nk, expo, jnp.zeros((1, BLK), F32))
                inv = 1.0 / total

                def mix(kb, acc):
                    p = (sbuf[kb] * inv).astype(BF16)
                    return acc + lax.dot_general(
                        tile(kv_ref, kb, width + hp * 128), p, TN, preferred_element_type=F32
                    )

                acc = lax.fori_loop(0, nk, mix, jnp.zeros((128, BLK), F32))
                outs.append(acc)
                lse_ref[hp, h : h + 1, qi * BLK : (qi + 1) * BLK] = top + jnp.log(total)
            sub = lax.broadcasted_iota(jnp.int32, (128, BLK), 0)
            o = jnp.where(sub < 64, outs[0], outs[1])
            o_ref[qi * BLK : (qi + 1) * BLK, pl.ds(pl.multiple_of(hp * 128, 128), 128)] = (
                o.T.astype(BF16)
            )
            return carry

        lax.fori_loop(0, HEADS // 2, pair, 0)


def attend(blk, q, kv, segk, segq):
    group, width = kv.shape[0], q.shape[1]
    nb = group // BLK
    return pl.pallas_call(
        attend_kernel,
        out_shape=[
            jax.ShapeDtypeStruct((2 * BLK, width), BF16),
            jax.ShapeDtypeStruct((HEADS // 2, 2, 2 * BLK), F32),
        ],
        in_specs=[SM, VM, VM, VM, VM],
        out_specs=[VM, VM],
        scratch_shapes=[pltpu.VMEM((nb, BLK, BLK), F32), pltpu.VMEM((nb, BLK, BLK), F32)],
        compiler_params=pltpu.CompilerParams(vmem_limit_bytes=48 << 20),
        name="attend",
    )(blk, q, kv, segk, segq)


def attend_back_kernel(
    blk_ref, q_ref, kv_ref, do_ref, lse_ref, segk_ref, segq_ref, dq_ref, dkv_ref,
    bias, pbuf, dpbuf, dkv_acc,
):
    width = q_ref.shape[1]
    dkv_acc[...] = jnp.zeros_like(dkv_acc)
    for qi in range(2):
        blk = blk_ref[qi]
        nk = blk + 1
        fill_bias(qi, nk, blk, segk_ref, segq_ref, bias)
        rows = slice(qi * BLK, (qi + 1) * BLK)

        def pair(hp, carry):
            cols = pl.ds(pl.multiple_of(hp * 128, 128), 128)
            qp, dop = q_ref[rows, cols], do_ref[rows, cols]
            dqs = []
            for h in range(2):
                qm = (jnp.where(lane_mask(h), qp, 0) * 0.125).astype(BF16)
                dom = jnp.where(lane_mask(h), dop, 0).astype(BF16)
                lse = lse_ref[hp, h : h + 1, rows]

                def first(kb, weighted):
                    s = lax.dot_general(
                        tile(kv_ref, kb, hp * 128), qm, NT, preferred_element_type=F32
                    )
                    p = jnp.exp(s + bias[kb] - lse)
                    dp = lax.dot_general(
                        tile(kv_ref, kb, width + hp * 128), dom, NT, preferred_element_type=F32
                    )
                    pbuf[kb] = p
                    dpbuf[kb] = dp
                    return weighted + jnp.sum(p * dp, axis=0, keepdims=True)

                weighted = lax.fori_loop(0, nk, first, jnp.zeros((1, BLK), F32))

                def second(kb, acc):
                    p = pbuf[kb]
                    ds = (p * (dpbuf[kb] - weighted)).astype(BF16)
                    krows = pl.ds(pl.multiple_of(kb * BLK, BLK), BLK)
                    dkv_acc[krows, cols] += jnp.dot(ds, qm, preferred_element_type=F32)
                    vcols = pl.ds(pl.multiple_of(width + hp * 128, 128), 128)
                    dkv_acc[krows, vcols] += jnp.dot(
                        p.astype(BF16), dom, preferred_element_type=F32
                    )
                    return acc + lax.dot_general(
                        tile(kv_ref, kb, hp * 128), ds, TN, preferred_element_type=F32
                    )

                dqs.append(lax.fori_loop(0, nk, second, jnp.zeros((128, BLK), F32)))
            sub = lax.broadcasted_iota(jnp.int32, (128, BLK), 0)
            dq = jnp.where(sub < 64, dqs[0], dqs[1]) * 0.125
            dq_ref[rows, cols] = dq.T
            return carry

        lax.fori_loop(0, HEADS // 2, pair, 0)
    dkv_ref[...] = dkv_acc[...].astype(BF16)


def attend_back(blk, q, kv, do, lse, segk, segq):
    group, width = kv.shape[0], q.shape[1]
    nb = group // BLK
    return pl.pallas_call(
        attend_back_kernel,
        out_shape=[
            jax.ShapeDtypeStruct((2 * BLK, width), F32),
            jax.ShapeDtypeStruct((group, 2 * width), BF16),
        ],
        in_specs=[SM] + [VM] * 6,
        out_specs=[VM, VM],
        scratch_shapes=[pltpu.VMEM((nb, BLK, BLK), F32)] * 3
        + [pltpu.VMEM((group, 2 * width), F32)],
        compiler_params=pltpu.CompilerParams(vmem_limit_bytes=56 << 20),
        name="attend_back",
    )(blk, q, kv, do, lse, segk, segq)


def inverse_rms(values):
    return lax.rsqrt(jnp.mean(values * values, axis=-1, keepdims=True) + eps_norm)


def norm_back(grad, values, inverse, gain):
    scaled = grad * gain
    mean = jnp.mean(scaled * values, axis=-1, keepdims=True)
    return (
        inverse * scaled - values * (inverse * inverse * inverse) * mean,
        jnp.sum(grad * values * inverse, axis=0),
    )


def swap_halves(values):
    lane = lax.broadcasted_iota(jnp.int32, values.shape, 1) % 64
    return jnp.where(lane < 32, jnp.roll(values, -32, axis=1), jnp.roll(values, 32, axis=1))


def dot(a, b):
    return jnp.dot(a, b, preferred_element_type=F32)


def dot_nt(a, b):
    return lax.dot_general(a, b, NT, preferred_element_type=F32)


def dot_tn(a, b):
    return lax.dot_general(a, b, TN, preferred_element_type=F32)


def per_device(
    inputs, cotangent, lengths, send_order,
    norm1_gain, qkv_weight, out_weight, norm2_gain, gate_weight, up_weight, down_weight,
):
    ndp, nctx = lax.axis_size("dp"), lax.axis_size("ctx")
    n_all = ndp * nctx
    width = inputs.shape[2]
    head = width // HEADS
    pc = Place(ndp, nctx)
    share = norm1_gain.shape[0]
    pad = jnp.zeros((SLOTS, 128), BF16).at[0, :share].set(norm1_gain).at[1, :share].set(norm2_gain)
    lens = jnp.zeros((8, 128), jnp.int32).at[:2, : lengths.shape[2]].set(lengths[:, 0])
    order_row = send_order
    order_col = jnp.swapaxes(send_order, 1, 2)
    x, dy, partner_lens, wqkv, wout, gains, wgate, wup, wdown = gather_all(
        ndp, nctx, inputs, cotangent, order_col, lens,
        [qkv_weight, out_weight, pad, gate_weight, up_weight, down_weight],
    )
    wqkv, wout, wgate, wup, wdown = (
        w.reshape(-1, w.shape[2]) for w in (wqkv, wout, wgate, wup, wdown)
    )
    gain1 = gains[:, 0, :share].reshape(1, width).astype(F32)
    gain2 = gains[:, 1, :share].reshape(1, width).astype(F32)

    both = jnp.where(pc.pack % 2 == pc.core, lens, partner_lens)
    seq_lengths = lax.dynamic_index_in_dim(both, pc.pack // 2, 0, keepdims=False)[: lengths.shape[2]]
    blocks = jnp.stack([pc.j, 2 * pc.g - 1 - pc.j]).astype(jnp.int32)
    rows = (blocks[:, None] * BLK + jnp.arange(BLK, dtype=jnp.int32)[None, :]).reshape(-1)
    ends = jnp.cumsum(seq_lengths)
    passed = (rows[:, None] >= ends[None, :]).astype(jnp.int32)
    segq = jnp.sum(passed, axis=1)
    position = rows - jnp.sum(passed * seq_lengths[None, :], axis=1)
    key_rows = jnp.arange(pc.g * 2 * BLK, dtype=jnp.int32)
    segk = jnp.sum((key_rows[:, None] >= ends[None, :]).astype(jnp.int32), axis=1)
    segq, segk = segq[None, :], segk[:, None]
    half = head // 2
    frequency = rope_base ** (-(jnp.arange(half, dtype=F32) * 2.0 / head))
    angles = position.astype(F32)[:, None] * frequency[None, :]
    cosine, sine = jnp.cos(angles), jnp.sin(angles)
    cos_all = jnp.tile(jnp.concatenate([cosine, cosine], 1), (1, HEADS))
    sin_all = jnp.tile(jnp.concatenate([-sine, sine], 1), (1, HEADS))

    xin, grad_out = x.astype(F32), dy.astype(F32)
    r1 = inverse_rms(xin)
    normed1 = (xin * r1 * gain1).astype(BF16)
    qkv = dot(normed1, wqkv)
    q_raw, k_raw = qkv[:, :width], qkv[:, width : 2 * width]
    queries = (q_raw * cos_all + swap_halves(q_raw) * sin_all).astype(BF16)
    keys = (k_raw * cos_all + swap_halves(k_raw) * sin_all).astype(BF16)
    kv = jnp.concatenate([keys, qkv[:, 2 * width :].astype(BF16)], axis=1)
    kv_all = share_kv(ndp, nctx, kv)
    attended, lse = attend(blocks, queries, kv_all, segk, segq)
    hidden = xin + dot(attended, wout)
    r2 = inverse_rms(hidden)
    normed2 = (hidden * r2 * gain2).astype(BF16)
    gate, up = dot(normed2, wgate), dot(normed2, wup)
    sig = 1.0 / (1.0 + jnp.exp(-gate))
    act = gate * sig
    inner = (act * up).astype(BF16)
    layer_out = (hidden + dot(inner, wdown)).astype(BF16)

    d_down = dot_tn(inner, dy).astype(BF16)
    grad_inner = dot_nt(dy, wdown)
    g_gate = (grad_inner * up * (sig * (1.0 + gate * (1.0 - sig)))).astype(BF16)
    g_up = (grad_inner * act).astype(BF16)
    d_gate = dot_tn(normed2, g_gate).astype(BF16)
    d_up = dot_tn(normed2, g_up).astype(BF16)
    grad_normed2 = dot_nt(g_gate, wgate) + dot_nt(g_up, wup)
    grad_hidden, d_gain2 = norm_back(grad_normed2, hidden, r2, gain2)
    grad_hidden = grad_out + grad_hidden
    g_branch = grad_hidden.astype(BF16)
    d_out = dot_tn(attended, g_branch).astype(BF16)
    grad_attended = dot_nt(g_branch, wout).astype(BF16)
    dq, dkv_part = attend_back(blocks, queries, kv_all, grad_attended, lse, segk, segq)
    dkv = sum_dkv(ndp, nctx, dkv_part)
    dk = dkv[:, :width]
    grad_qkv = jnp.concatenate(
        [
            dq * cos_all - swap_halves(dq) * sin_all,
            dk * cos_all - swap_halves(dk) * sin_all,
            dkv[:, width:],
        ],
        axis=1,
    ).astype(BF16)
    d_qkv = dot_tn(normed1, grad_qkv).astype(BF16)
    grad_normed1 = dot_nt(grad_qkv, wqkv)
    grad_x, d_gain1 = norm_back(grad_normed1, xin, r1, gain1)
    input_grad = (grad_hidden + grad_x).astype(BF16)

    d_gains = jnp.zeros((n_all, SLOTS, 128), BF16)
    d_gains = d_gains.at[:, 0, :share].set(d_gain1.reshape(n_all, share).astype(BF16))
    d_gains = d_gains.at[:, 1, :share].set(d_gain2.reshape(n_all, share).astype(BF16))
    fin_out, fin_gin, s_down, s_gate, s_up, s_out, s_qkv, s_gains = scatter_all(
        ndp, nctx, layer_out, input_grad, order_row,
        [d.reshape(n_all, -1, d.shape[1]) for d in (d_down, d_gate, d_up, d_out, d_qkv)] + [d_gains],
    )
    return (
        fin_out, fin_gin, s_gains[0, :share], s_qkv, s_out, s_gains[1, :share],
        s_gate, s_up, s_down,
    )


def solution(mesh):
    both = ("dp", "ctx")
    in_specs = (
        P(None, both, None), P(None, both, None), P(None, "dp", None), P(None, both, None),
        P(both), P(both, None), P(both, None), P(both), P(both, None), P(both, None), P(both, None),
    )
    out_specs = (
        P(None, both, None), P(None, both, None),
        P(both), P(both, None), P(both, None), P(both), P(both, None), P(both, None), P(both, None),
    )
    return jax.shard_map(
        per_device, mesh=mesh, in_specs=in_specs, out_specs=out_specs, check_vma=False
    )
```

```python
import functools

import jax
import jax.numpy as jnp
from jax import lax
from jax.experimental import pallas as pl
from jax.experimental.pallas import tpu as pltpu
from jax.sharding import PartitionSpec as P

HEADS = 12
BLK = 256
SLOTS = 8
eps_norm = 1e-05
rope_base = 10000.0
MESH = pl.DeviceIdType.MESH
F32, BF16 = jnp.float32, jnp.bfloat16
NT = (((1,), (1,)), ((), ()))
TN = (((0,), (0,)), ((), ()))
ANY = pl.BlockSpec(memory_space=pl.ANY)
VM = pl.BlockSpec(memory_space=pltpu.VMEM)
SM = pl.BlockSpec(memory_space=pltpu.SMEM)


class Place:
    def __init__(self, ndp, nctx, pre=1):
        self.ndp, self.nctx, self.pre = ndp, nctx, pre
        self.nz = nctx // pre
        self.nb = 2
        self.na = ndp // 4
        self.g = nctx // 2
        self.gz = nctx // 4
        self.dp = lax.axis_index("dp")
        self.ctx = lax.axis_index("ctx")
        self.k, self.core = self.dp // 2, self.dp % 2
        self.ya, self.xb = self.k // self.nb, self.k % self.nb
        self.me = self.dp * nctx + self.ctx
        self.zi = self.ctx // pre
        self.pack = self.ctx // self.gz
        self.j = self.core * self.gz + self.ctx % self.gz

    def member(self, j):
        return (self.k * 2 + j // self.gz, self.pack * self.gz + j % self.gz)

    def holder(self, m, d, c):
        j = jnp.where(c < self.g, c, 2 * self.g - 1 - c)
        return ((d // 2) * 2 + j // self.gz, (m * 2 + d % 2) * self.gz + j % self.gz)

    def dp_of(self, ya, xb, core):
        return (ya * self.nb + xb) * 2 + core


def entry_barrier(pc):
    total = pc.ndp * pc.nctx
    barrier = pltpu.get_barrier_semaphore()

    def greet(i, carry):
        other = (pc.me + i) % total
        pl.semaphore_signal(
            barrier, inc=1, device_id=(other // pc.nctx, other % pc.nctx), device_id_type=MESH
        )
        return carry

    lax.fori_loop(1, total, greet, 0)
    pl.semaphore_wait(barrier, total - 1)


def remote(src, dst, ss, rs, dev):
    return pltpu.make_async_remote_copy(
        src_ref=src, dst_ref=dst, send_sem=ss, recv_sem=rs, device_id=dev, device_id_type=MESH
    )


class Gather:
    def __init__(self, pc, shards, full, chunks, sems):
        self.pc, self.shards, self.full, self.chunks = pc, shards, full, chunks
        (
            self.own_sem, self.z_ss, self.z_rs, self.x_ss, self.x_rs, self.y_ss, self.y_rs,
            self.fa_ss, self.fa_rs, self.fb_ss, self.fb_rs, self.c_ss, self.c_rs,
        ) = sems

    def cut(self, ref, t, start, count):
        _, c0, cw = self.chunks[t]
        return ref.at[pl.ds(pl.multiple_of(start, 8), count), pl.ds(c0, cw)]

    def rows(self, t):
        return self.shards[self.chunks[t][0]].shape[0]

    def mine(self, t):
        a, c0, cw = self.chunks[t]
        return self.shards[a].at[:, pl.ds(c0, cw)]

    def place(self, t):
        r = self.rows(t)
        return self.cut(self.full[self.chunks[t][0]], t, (self.pc.dp * self.pc.nz + self.pc.zi) * r, r)

    def block(self, t, dp, part=None):
        n = self.pc.nz * self.rows(t)
        ref = self.full[self.chunks[t][0]]
        if part is None:
            return self.cut(ref, t, dp * n, n)
        return self.cut(ref, t, dp * n + part * (n // 2), n // 2)

    def own_copy(self, t):
        return pltpu.make_async_copy(self.mine(t), self.place(t), self.own_sem.at[t])

    def z_copies(self, t):
        pc = self.pc
        return [
            remote(
                self.mine(t), self.place(t), self.z_ss.at[t, d - 1], self.z_rs.at[t, d - 1],
                (pc.dp, (pc.ctx + d * pc.pre) % pc.nctx),
            )
            for d in range(1, pc.nz)
        ]

    def xy_copies(self, t):
        pc = self.pc
        out = []
        for d in range(1, pc.nb):
            to = (pc.dp_of(pc.ya, (pc.xb + d) % pc.nb, pc.core), pc.ctx)
            out.append(
                remote(
                    self.block(t, pc.dp), self.block(t, pc.dp),
                    self.x_ss.at[t, d - 1], self.x_rs.at[t, d - 1], to,
                )
            )
        for d in range(1, pc.na):
            to = (pc.dp_of((pc.ya + d) % pc.na, pc.xb, pc.core), pc.ctx)
            out.append(
                remote(
                    self.block(t, pc.dp), self.block(t, pc.dp),
                    self.y_ss.at[t, d - 1], self.y_rs.at[t, d - 1], to,
                )
            )
        return out

    def forward_copies(self, t):
        pc = self.pc
        out = []
        for dx in range(1, pc.nb):
            for dy in range(1, pc.na):
                src = pc.dp_of(pc.ya, (pc.xb + pc.nb - dx) % pc.nb, pc.core)
                out.append(
                    remote(
                        self.block(t, src, 0), self.block(t, src, 0),
                        self.fa_ss.at[t, dx - 1, dy - 1], self.fa_rs.at[t, dx - 1, dy - 1],
                        (pc.dp_of((pc.ya + dy) % pc.na, pc.xb, pc.core), pc.ctx),
                    )
                )
                src = pc.dp_of((pc.ya + pc.na - dy) % pc.na, pc.xb, pc.core)
                out.append(
                    remote(
                        self.block(t, src, 1), self.block(t, src, 1),
                        self.fb_ss.at[t, dx - 1, dy - 1], self.fb_rs.at[t, dx - 1, dy - 1],
                        (pc.dp_of(pc.ya, (pc.xb + dx) % pc.nb, pc.core), pc.ctx),
                    )
                )
        return out

    def core_copy(self, t, dy, dx):
        pc = self.pc
        src = pc.dp_of((pc.ya + pc.na - dy) % pc.na, (pc.xb + pc.nb - dx) % pc.nb, pc.core)
        return remote(
            self.block(t, src), self.block(t, src), self.c_ss.at[t, dy, dx], self.c_rs.at[t, dy, dx],
            (pc.k * 2 + 1 - pc.core, pc.ctx),
        )

    def core_copies(self, t, which):
        pc = self.pc
        pairs = {
            "own": [(0, 0)],
            "xy": [(0, dx) for dx in range(1, pc.nb)] + [(dy, 0) for dy in range(1, pc.na)],
            "diag": [(dy, dx) for dy in range(1, pc.na) for dx in range(1, pc.nb)],
        }[which]
        return [self.core_copy(t, dy, dx) for dy, dx in pairs]

    def step(self, t, stage):
        if stage == 0:
            start_all(self.z_copies(t))
        elif stage == 1:
            self.own_copy(t).wait()
            wait_arrived(self.z_copies(t))
            start_all(self.xy_copies(t) + self.core_copies(t, "own"))
        elif stage == 2:
            wait_arrived(self.xy_copies(t))
            start_all(self.forward_copies(t) + self.core_copies(t, "xy"))
        elif stage == 3:
            wait_arrived(self.forward_copies(t))
            start_all(self.core_copies(t, "diag"))
        else:
            wait_arrived([cp for w in ("own", "xy", "diag") for cp in self.core_copies(t, w)])

    def wait_sent(self):
        for t in range(len(self.chunks)):
            for cp in self.z_copies(t) + self.xy_copies(t) + self.forward_copies(t):
                cp.wait_send()
            for w in ("own", "xy", "diag"):
                for cp in self.core_copies(t, w):
                    cp.wait_send()


def start_all(copies):
    for cp in copies:
        cp.start()


def wait_arrived(copies):
    for cp in copies:
        cp.wait_recv()


class Steps:
    def __init__(self):
        self.todo = []
        self.done = set()

    def add(self, name, fn):
        self.todo.append((name, fn))

    def run(self, count=1):
        for _ in range(count):
            if self.todo:
                name, fn = self.todo.pop(0)
                fn()
                self.done.add(name)

    def until(self, name):
        while name not in self.done:
            self.run()

    def take(self, count):
        out, self.todo = self.todo[:count], self.todo[count:]
        for name, _ in out:
            self.done.add(name)
        return [fn for _, fn in out]


def loop_with_steps(n, body, groups):
    def one(i, carry):
        body(i)
        for at, group in enumerate(groups):
            if group:

                @pl.when(i == at)
                def _():
                    for fn in group:
                        fn()

        return carry

    lax.fori_loop(0, n, one, 0)


def lane_swap(u):
    lane = lax.broadcasted_iota(jnp.int32, (1, 128), 1) % 64
    return jnp.where(lane < 32, pltpu.roll(u, 96, 1), pltpu.roll(u, 32, 1))


def turned(u, cos_t, sin_t):
    parts = []
    for i in range(u.shape[1] // 128):
        v = u[:, i * 128 : (i + 1) * 128]
        parts.append(v * cos_t + lane_swap(v) * sin_t)
    return jnp.concatenate(parts, axis=1)


def cols(i, size=256):
    return pl.ds(pl.multiple_of(i * size, size), size)


def layer_rows(pc, half):
    return pc.j if half == 0 else 2 * pc.g - 1 - pc.j


def gain_row(tiles, which, share, width):
    lane = lax.broadcasted_iota(jnp.int32, (128, width), 0)
    col = lax.broadcasted_iota(jnp.int32, (128, width), 1)
    spread = (lane == col % share).astype(BF16)
    wide = jnp.dot(tiles, spread, preferred_element_type=F32)
    row = lax.broadcasted_iota(jnp.int32, wide.shape, 0)
    col = lax.broadcasted_iota(jnp.int32, wide.shape, 1)
    keep = row == SLOTS * (col // share) + which
    return jnp.sum(jnp.where(keep, wide, 0.0), axis=0, keepdims=True)


KF_OUT = (
    "dy", "x", "n1_t", "q", "kv", "lse", "att_t", "hidden", "n2_t", "slope", "act", "inner_t", "out",
    "rope", "bias", "gain",
)


def forward_kernel(ndp, nctx, pre, share, nt, chunks, x_ref, dy_ref, order_ref, len_ref, freq_ref, *refs):
    shards, refs = refs[:nt], refs[nt:]
    full, refs = refs[:nt], refs[nt:]
    out, refs = dict(zip(KF_OUT, refs[: len(KF_OUT)])), refs[len(KF_OUT) :]
    weights, refs = refs[:nt], refs[nt:]
    (
        perm, plen, x_v, n1_v, q_v, kv_v, lse_v, att_v, hid_v, n2_v, slope_v, act_v, inner_v, out_v,
        rope_v, bias_v, gain_v, n1_t, att_t, n2_t, inner_t,
        tok_ss, tok_rs, len_ss, len_rs, kv_ss, kv_rs, load_sem, save_sem, *sems,
    ) = refs
    pc = Place(ndp, nctx, pre)
    width = x_v.shape[1]
    slot = BLK // ndp
    nch = len(chunks)
    gather = Gather(pc, shards, full, chunks, sems)
    for t in range(nch):
        gather.own_copy(t).start()
    hots = []
    entry_barrier(pc)

    def token_copies(t, m, d):
        dp_to, ctx_to = pc.holder(m, d, pc.ctx)
        half = jnp.where(pc.ctx < pc.g, 0, 1)
        src = perm.at[t, m, pl.ds(pl.multiple_of(d * slot, slot), slot)]
        dst = (x_v, out["dy"])[t].at[pl.ds(pl.multiple_of(half * BLK + pc.dp * slot, slot), slot)]
        rs = tok_rs.at[t, half, pc.dp]
        same = (dp_to == pc.dp) & (ctx_to == pc.ctx)
        return (
            same,
            pltpu.make_async_copy(src, dst, rs),
            remote(src, dst, tok_ss.at[t, m, d], rs, (dp_to, ctx_to)),
        )

    def send_tokens(t, source):
        for m in range(2):
            order = order_ref[m]
            hot = (lax.broadcasted_iota(jnp.int32, (BLK, BLK), 1) == order).astype(BF16)
            perm[t, m] = jnp.dot(hot, source[m], preferred_element_type=F32).astype(BF16)

            def one(d, carry):
                same, near, far = token_copies(t, m, d)

                @pl.when(same)
                def _():
                    near.start()

                @pl.when(jnp.logical_not(same))
                def _():
                    far.start()

                return carry

            lax.fori_loop(0, ndp, one, 0)

    def tokens_sent(t):
        for m in range(2):

            def sent(d, carry):
                same, _near, far = token_copies(t, m, d)

                @pl.when(jnp.logical_not(same))
                def _():
                    far.wait_send()

                return carry

            lax.fori_loop(0, ndp, sent, 0)

    def tokens_arrived(t):
        for half in range(2):

            def arrived(b, carry):
                dst = (x_v, out["dy"])[t].at[
                    pl.ds(pl.multiple_of(half * BLK + b * slot, slot), slot)
                ]
                pltpu.make_async_copy(dst, dst, tok_rs.at[t, half, b]).wait()
                return carry

            lax.fori_loop(0, ndp, arrived, 0)

    saves = []

    def save(name, src):
        cp = pltpu.make_async_copy(src, out[name], save_sem.at[len(saves)])
        cp.start()
        saves.append(cp)

    def load(a):
        return pltpu.make_async_copy(full[a], weights[a], load_sem.at[a])

    steps = Steps()
    last_of = {a: max(t for t in range(nch) if chunks[t][0] == a) for a in range(nt)}

    def final(t):
        gather.step(t, 4)
        if last_of[chunks[t][0]] == t:
            load(chunks[t][0]).start()

    for i in range(nch + 3):
        if i < nch:
            steps.add(("z", i), functools.partial(gather.step, i, 1))
            if i + 2 < nch:
                steps.add(("start", i + 2), functools.partial(gather.step, i + 2, 0))
            if i == nch - 4:
                steps.add("dy", functools.partial(send_tokens, 1, dy_ref))
        if 1 <= i <= nch:
            steps.add(("xy", i - 1), functools.partial(gather.step, i - 1, 2))
        if 2 <= i <= nch + 1:
            steps.add(("f", i - 2), functools.partial(gather.step, i - 2, 3))
        if i >= 3:
            steps.add(("c", i - 3), functools.partial(final, i - 3))

    gather.step(0, 0)
    gather.step(1, 0)
    len_copy = remote(len_ref, plen, len_ss, len_rs, (pc.k * 2 + 1 - pc.core, pc.ctx))
    len_copy.start()
    send_tokens(0, x_ref)
    steps.run(6)

    len_copy.wait_recv()
    lens = jnp.where(pc.pack % 2 == pc.core, len_ref[...], plen[...]).astype(F32)
    lens = jnp.where(pc.pack // 2 == 0, lens[0:1], lens[1:2])
    lane = lax.broadcasted_iota(jnp.int32, (1, 128), 1)
    ends = [jnp.sum(jnp.where(lane <= i, lens, 0.0), axis=1, keepdims=True) for i in range(4)]
    sizes = [jnp.sum(jnp.where(lane == i, lens, 0.0), axis=1, keepdims=True) for i in range(4)]

    def segment(rows):
        seg = jnp.zeros(rows.shape, F32)
        start = jnp.zeros(rows.shape, F32)
        for end, size in zip(ends, sizes):
            passed = (rows >= end).astype(F32)
            seg = seg + passed
            start = start + passed * size
        return seg, start

    def index(shape, axis):
        return lax.broadcasted_iota(jnp.int32, shape, axis).astype(F32)

    sign = jnp.where(lane % 64 < 32, -1.0, 1.0)
    at = 0
    for half in range(2):
        base = (layer_rows(pc, half) * BLK).astype(F32)
        rows = base + index((BLK, 128), 0)
        _, start = segment(rows)
        angle = (rows - start) * freq_ref[0:1]
        rope_v[half * BLK : (half + 1) * BLK, 0:128] = jnp.cos(angle)
        rope_v[half * BLK : (half + 1) * BLK, 128:256] = jnp.sin(angle) * sign
        qrow = base + index((1, BLK), 1)
        segq, _ = segment(qrow)
        for kb in range((half + 1) * pc.g):
            krow = kb * BLK + index((BLK, BLK), 0)
            segk, _ = segment(kb * BLK + index((BLK, 1), 0))
            bias_v[at : at + BLK] = jnp.where((segk == segq) & (krow <= qrow), 0.0, NEG)
            at += BLK
    save("rope", rope_v)
    save("bias", bias_v)
    steps.until(("c", 0))
    load(0).wait()
    gain_v[0:1] = gain_row(weights[0][...], 0, share, width)
    gain_v[1:2] = gain_row(weights[0][...], 1, share, width)
    gain_v[2:8] = jnp.zeros((6, width), F32)
    save("gain", gain_v)
    tokens_arrived(0)
    save("x", x_v)
    x = x_v[...].astype(F32)
    n1_v[...] = (x * inverse_rms(x) * gain_v[0:1]).astype(BF16)
    n1_t[...] = n1_v[...].T
    save("n1_t", n1_t)

    wqkv = weights[1]
    cos_t, sin_t = rope_v[:, 0:128], rope_v[:, 128:256]

    def kv_copies(part):
        copies = []
        for half in range(2):
            ref = kv_v.at[
                pl.ds(pl.multiple_of(layer_rows(pc, half) * BLK, BLK), BLK),
                pl.ds(part * width, width),
            ]
            for o in range(1, pc.g):
                copies.append(
                    remote(
                        ref, ref, kv_ss.at[part, half, o - 1], kv_rs.at[part, half, o - 1],
                        pc.member((pc.j + o) % pc.g),
                    )
                )
        return copies

    def project(base, to, rope):
        def one(i, carry):
            u = jnp.dot(
                n1_v[...], wqkv[:, pl.ds(pl.multiple_of(base + i * 256, 256), 256)],
                preferred_element_type=F32,
            )
            if rope:
                u = turned(u, cos_t, sin_t)
            to(i, u.astype(BF16))
            return carry

        lax.fori_loop(0, width // 256, one, 0)

    def to_kv(part):
        def put(i, u):
            for half in range(2):
                kv_v[
                    pl.ds(pl.multiple_of(layer_rows(pc, half) * BLK, BLK), BLK),
                    pl.ds(pl.multiple_of(part * width + i * 256, 256), 256),
                ] = u[half * BLK : (half + 1) * BLK]

        return put

    def to_q(i, u):
        q_v[:, cols(i)] = u

    steps.until(("c", last_of[1]))
    load(1).wait()
    project(width, to_kv(0), True)
    start_all(kv_copies(0))
    steps.run(1)
    project(2 * width, to_kv(1), False)
    start_all(kv_copies(1))
    steps.run(1)
    project(0, to_q, True)
    save("q", q_v)
    steps.run(2)
    wait_arrived(kv_copies(0) + kv_copies(1))
    save("kv", kv_v)

    def pair(hp):
        hc = cols(hp, 128)
        vc = pl.ds(pl.multiple_of(width + hp * 128, 128), 128)
        at = 0
        for half in range(2):
            nk = (half + 1) * pc.g * BLK
            rows = slice(half * BLK, (half + 1) * BLK)
            qp = q_v[rows, hc]
            both = []
            for h in range(2):
                qm = (jnp.where(lane_mask(h), qp, 0) * 0.125).astype(BF16)
                s = lax.dot_general(kv_v[0:nk, hc], qm, NT, preferred_element_type=F32)
                s = s + bias_v[at : at + nk]
                top = jnp.max(s, axis=0, keepdims=True)
                p = jnp.exp(s - top)
                total = jnp.sum(p, axis=0, keepdims=True)
                p = (p * (1.0 / total)).astype(BF16)
                both.append(
                    lax.dot_general(kv_v[0:nk, vc], p, TN, preferred_element_type=F32)
                )
                lse_v[hp, h : h + 1, rows] = top + jnp.log(total)
            sub = lax.broadcasted_iota(jnp.int32, (128, BLK), 0)
            o = jnp.where(sub < 64, both[0], both[1])
            att_v[rows, hc] = o.T.astype(BF16)
            att_t[hc, rows] = o.astype(BF16)
            at += nk

    loop_with_steps(HEADS // 2, pair, [steps.take(2) for _ in range(HEADS // 2)])
    save("lse", lse_v)
    save("att_t", att_t)

    steps.until(("c", last_of[2]))
    load(2).wait()
    hid = x_v[...].astype(F32) + jnp.dot(att_v[...], weights[2][...], preferred_element_type=F32)
    hid_v[...] = hid
    n2_v[...] = (hid * inverse_rms(hid) * gain_v[1:2]).astype(BF16)
    save("hidden", hid_v)
    n2_t[...] = n2_v[...].T
    save("n2_t", n2_t)
    steps.until(("c", last_of[3]))
    load(3).wait()
    steps.until(("c", last_of[4]))
    load(4).wait()

    def ffn(c):
        g = jnp.dot(n2_v[...], weights[3][:, cols(c)], preferred_element_type=F32)
        u = jnp.dot(n2_v[...], weights[4][:, cols(c)], preferred_element_type=F32)
        sig = 1.0 / (1.0 + jnp.exp(-g))
        act = g * sig
        act_v[:, cols(c)] = act.astype(BF16)
        inner = (act * u).astype(BF16)
        inner_v[:, cols(c)] = inner
        inner_t[cols(c), :] = inner.T
        slope_v[:, cols(c)] = (u * (sig * (1.0 + g * (1.0 - sig)))).astype(BF16)

    n_ff = act_v.shape[1] // 256
    loop_with_steps(n_ff, ffn, [[]] + [steps.take(1) for _ in range(n_ff - 1)])
    save("act", act_v)
    save("slope", slope_v)
    save("inner_t", inner_t)
    steps.until(("c", last_of[5]))
    load(5).wait()

    def down(i, carry):
        u = jnp.dot(inner_v[...], weights[5][:, cols(i)], preferred_element_type=F32)
        out_v[:, cols(i)] = (hid_v[:, cols(i)] + u).astype(BF16)
        return carry

    lax.fori_loop(0, width // 256, down, 0)
    save("out", out_v)
    while steps.todo:
        steps.run()
    tokens_arrived(1)
    tokens_sent(0)
    tokens_sent(1)
    len_copy.wait_send()
    for cp in kv_copies(0) + kv_copies(1):
        cp.wait_send()
    gather.wait_sent()
    for cp in saves:
        cp.wait()


def forward(ndp, nctx, pre, share, x, dy, order, lens, freq, shards):
    nt = len(shards)
    nz, na, nb, g = nctx // pre, ndp // 4, 2, nctx // 2
    n_blocks = ndp * nz
    width = x.shape[-1]
    ff = shards[3].shape[1]
    rows = 2 * BLK
    dma = pltpu.SemaphoreType.DMA
    chunks = [(0, 0, 128)]
    chunks += [(1, width, width), (1, 2 * width, width), (1, 0, width), (2, 0, width)]
    for a in (3, 4):
        chunks += [(a, 0, ff // 2), (a, ff // 2, ff // 2)]
    chunks += [(5, 0, width // 2), (5, width // 2, width // 2)]
    n = len(chunks)
    full = [jax.ShapeDtypeStruct((n_blocks * s.shape[0], s.shape[1]), BF16) for s in shards]
    shape = dict(
        dy=((rows, width), BF16), x=((rows, width), BF16), n1=((rows, width), BF16),
        q=((rows, width), BF16), kv=((g * rows, 2 * width), BF16),
        lse=((HEADS // 2, 2, rows), F32), att=((rows, width), BF16), hidden=((rows, width), F32),
        n2=((rows, width), BF16), slope=((rows, ff), BF16), act=((rows, ff), BF16),
        inner=((rows, ff), BF16), out=((rows, width), BF16), rope=((rows, 256), F32),
        bias=((3 * g * BLK, BLK), F32), gain=((8, width), F32),
        n1_t=((width, rows), BF16), att_t=((width, rows), BF16), n2_t=((width, rows), BF16),
        inner_t=((ff, rows), BF16),
    )
    kept = {k: jax.ShapeDtypeStruct(*v) for k, v in shape.items()}
    v = {k: pltpu.VMEM(*sd) for k, sd in shape.items()}
    order_v = (
        "x", "n1", "q", "kv", "lse", "att", "hidden", "n2", "slope", "act", "inner", "out",
        "rope", "bias", "gain", "n1_t", "att_t", "n2_t", "inner_t",
    )
    scratch = [pltpu.VMEM(f.shape, BF16) for f in full]
    scratch += [pltpu.VMEM((2, 2, BLK, width), BF16), pltpu.VMEM(lens.shape, lens.dtype)]
    scratch += [v[k] for k in order_v]
    scratch += [
        dma((2, 2, ndp)), dma((2, 2, ndp)), dma, dma, dma((2, 2, g - 1)), dma((2, 2, g - 1)),
        dma((nt,)), dma((len(KF_OUT),)),
        dma((n,)), dma((n, nz - 1)), dma((n, nz - 1)),
        dma((n, nb - 1)), dma((n, nb - 1)), dma((n, na - 1)), dma((n, na - 1)),
        dma((n, nb - 1, na - 1)), dma((n, nb - 1, na - 1)),
        dma((n, nb - 1, na - 1)), dma((n, nb - 1, na - 1)),
        dma((n, na, nb)), dma((n, na, nb)),
    ]
    res = pl.pallas_call(
        functools.partial(forward_kernel, ndp, nctx, pre, share, nt, chunks),
        out_shape=full + [kept[k] for k in KF_OUT],
        in_specs=[VM] * 5 + [ANY] * nt,
        out_specs=[ANY] * (nt + len(KF_OUT)),
        scratch_shapes=scratch,
        compiler_params=pltpu.CompilerParams(
            collective_id=0, has_side_effects=True, vmem_limit_bytes=60 << 20
        ),
        name="forward",
    )(x, dy, order, lens, freq, *shards)
    return res[:nt], dict(zip(KF_OUT, res[nt:]))


class Scatter:
    def __init__(self, pc, grads, shares, bufs, sems):
        self.pc, self.grads, self.shares = pc, grads, shares
        self.core_in, self.diag_a, self.diag_b, self.x_in, self.y_in, self.z_in = bufs
        (
            self.c_ss, self.c_rs, self.da_ss, self.da_rs, self.db_ss, self.db_rs,
            self.x_ss, self.x_rs, self.y_ss, self.y_rs, self.z_ss, self.z_rs,
        ) = sems
        self.yx = [(dy, dx) for dy in range(1, pc.na) for dx in range(1, pc.nb)]
        self.yx += [(0, dx) for dx in range(1, pc.nb)] + [(dy, 0) for dy in range(1, pc.na)]
        self.yx += [(0, 0)]

    def first(self, dy, dx, core):
        pc = self.pc
        k = ((pc.ya + dy) % pc.na) * pc.nb + (pc.xb + dx) % pc.nb
        return (k * 2 + core) * pc.nz

    def core_copies(self, t):
        pc = self.pc
        return [
            remote(
                self.grads[t].at[pl.ds(self.first(dy, dx, 1 - pc.core), pc.nz)],
                self.core_in[t].at[dy, dx], self.c_ss.at[t, dy, dx], self.c_rs.at[t, dy, dx],
                (pc.k * 2 + 1 - pc.core, pc.ctx),
            )
            for dy, dx in self.yx
        ]

    def diag_copies(self, t):
        pc = self.pc
        h = pc.nz // 2
        out = []
        for dy in range(1, pc.na):
            for dx in range(1, pc.nb):
                out.append(
                    remote(
                        self.core_in[t].at[dy, dx, pl.ds(0, h)], self.diag_a[t].at[dy - 1, dx - 1],
                        self.da_ss.at[t, dy - 1, dx - 1], self.da_rs.at[t, dy - 1, dx - 1],
                        (pc.dp_of((pc.ya + dy) % pc.na, pc.xb, pc.core), pc.ctx),
                    )
                )
                out.append(
                    remote(
                        self.core_in[t].at[dy, dx, pl.ds(h, h)], self.diag_b[t].at[dy - 1, dx - 1],
                        self.db_ss.at[t, dy - 1, dx - 1], self.db_rs.at[t, dy - 1, dx - 1],
                        (pc.dp_of(pc.ya, (pc.xb + dx) % pc.nb, pc.core), pc.ctx),
                    )
                )
        return out

    def xy_copies(self, t):
        pc = self.pc
        out = []
        for dx in range(1, pc.nb):
            out.append(
                remote(
                    self.core_in[t].at[0, dx], self.x_in[t].at[dx - 1],
                    self.x_ss.at[t, dx - 1], self.x_rs.at[t, dx - 1],
                    (pc.dp_of(pc.ya, (pc.xb + dx) % pc.nb, pc.core), pc.ctx),
                )
            )
        for dy in range(1, pc.na):
            out.append(
                remote(
                    self.core_in[t].at[dy, 0], self.y_in[t].at[dy - 1],
                    self.y_ss.at[t, dy - 1], self.y_rs.at[t, dy - 1],
                    (pc.dp_of((pc.ya + dy) % pc.na, pc.xb, pc.core), pc.ctx),
                )
            )
        return out

    def z_copies(self, t):
        pc = self.pc
        return [
            remote(
                self.core_in[t].at[0, 0, (pc.zi + d) % pc.nz], self.z_in[t].at[d - 1],
                self.z_ss.at[t, d - 1], self.z_rs.at[t, d - 1],
                (pc.dp, (pc.ctx + d * pc.pre) % pc.nctx),
            )
            for d in range(1, pc.nz)
        ]

    def step(self, t, stage):
        pc = self.pc
        h = pc.nz // 2
        if stage == 0:
            start_all(self.core_copies(t))
        elif stage == 1:
            wait_arrived(self.core_copies(t))
            for dy, dx in self.yx:
                first = self.first(dy, dx, pc.core)
                self.accumulate(t, dy, dx, 0, pc.nz, [lambda z, f=first: self.grads[t][f + z]])
            start_all(self.diag_copies(t))
        elif stage == 2:
            for cp in self.core_copies(t):
                cp.wait_send()
            wait_arrived(self.diag_copies(t))
            for dx in range(1, pc.nb):
                self.accumulate(
                    t, 0, dx, 0, h,
                    [lambda z, dy=dy: self.diag_a[t][dy - 1, dx - 1, z] for dy in range(1, pc.na)],
                )
            for dy in range(1, pc.na):
                self.accumulate(
                    t, dy, 0, h, h,
                    [lambda z, dx=dx: self.diag_b[t][dy - 1, dx - 1, z] for dx in range(1, pc.nb)],
                )
            start_all(self.xy_copies(t))
        elif stage == 3:
            wait_arrived(self.xy_copies(t))
            self.accumulate(
                t, 0, 0, 0, pc.nz,
                [lambda z, i=i: self.x_in[t][i, z] for i in range(pc.nb - 1)]
                + [lambda z, i=i: self.y_in[t][i, z] for i in range(pc.na - 1)],
            )
            start_all(self.z_copies(t))
        else:
            wait_arrived(self.z_copies(t))
            total = self.core_in[t][0, 0, pc.zi].astype(F32)
            for i in range(pc.nz - 1):
                total = total + self.z_in[t][i].astype(F32)
            self.shares[t][...] = total

    def accumulate(self, t, dy, dx, z0, count, others):
        ref = self.core_in[t]

        def one(z, carry):
            total = ref[dy, dx, z0 + z].astype(F32)
            for other in others:
                total = total + other(z).astype(F32)
            ref[dy, dx, z0 + z] = total.astype(BF16)
            return carry

        lax.fori_loop(0, count, one, 0)

    def wait_sent(self):
        for t in range(len(self.grads)):
            for cp in self.diag_copies(t) + self.xy_copies(t) + self.z_copies(t):
                cp.wait_send()


class Rounds(Steps):
    def __init__(self, scatter, stages):
        super().__init__()
        self.scatter, self.stages = scatter, stages

    def begin(self, t):
        self.scatter.step(t, 0)
        self.todo.append((t, 1))

    def take(self, count):
        out = []
        for _ in range(count):
            if self.todo:
                t, stage = self.todo.pop(0)
                out.append(functools.partial(self.scatter.step, t, stage))
                if stage + 1 < self.stages:
                    self.todo.append((t, stage + 1))
        return out

    def run(self, count=1):
        for fn in self.take(count):
            fn()


def block_at(ref, index, size=BLK):
    return ref.at[pl.ds(pl.multiple_of(index * size, size), size)]


KB_IN = (
    "dy", "x", "n1_t", "q", "kv", "lse", "att_t", "hidden", "n2_t", "slope", "act", "inner_t", "out",
    "rope", "bias", "gain",
)
CHUNKS = ("down0", "down1", "down2", "gate0", "up0", "gate1", "up1", "out", "q", "k", "v", "gain")


def backward_kernel(ndp, nctx, pre, share, nt, order_ref, *refs):
    kept, refs = dict(zip(KB_IN, refs[: len(KB_IN)])), refs[len(KB_IN) :]
    (wqkv_h, wout_h, wgate_h, wup_h, wdown_h), refs = refs[:5], refs[5:]
    fin, refs = refs[:2], refs[2:]
    (s_qkv, s_out, s_gate, s_up, s_down, s_gain), refs = refs[:6], refs[6:]
    grad_bufs, refs = refs[:9], refs[9:]
    nch = len(CHUNKS)
    bufs = [refs[i * nch : (i + 1) * nch] for i in range(6)]
    refs = refs[6 * nch :]
    (
        tok, dkv_in, dy_v, hid_v, att_t, wout, gb_v, gatt_v, gain_v, dg_v,
        tok_ss, tok_rs, dkv_ss, dkv_rs, load_sem, *sems,
    ) = refs
    pc = Place(ndp, nctx, pre)
    rows, width = dy_v.shape
    slot = BLK // ndp
    ff = s_gate.shape[1]
    n_blocks = ndp * pc.nz
    b_down0, b_down1, b_down2, b_gate0, b_up0, b_gate1, b_up1, b_out, b_gain = grad_bufs
    narrow = slice(0, width)
    grads = [
        b_down0, b_down1, b_down2, b_gate0, b_up0, b_gate1, b_up1, b_out,
        b_gate0.at[:, :, narrow], b_up0.at[:, :, narrow], b_gate1.at[:, :, narrow], b_gain,
    ]
    half_ff = ff // 2
    third = width // 3
    shares = [s_down.at[:, pl.ds(i * third, third)] for i in range(3)]
    shares += [s_gate.at[:, pl.ds(0, half_ff)], s_up.at[:, pl.ds(0, half_ff)]]
    shares += [s_gate.at[:, pl.ds(half_ff, half_ff)], s_up.at[:, pl.ds(half_ff, half_ff)], s_out]
    shares += [s_qkv.at[:, pl.ds(i * width, width)] for i in range(3)] + [s_gain]
    scatter = Scatter(pc, grads, shares, bufs, sems)
    rounds = Rounds(scatter, 5)
    chunk = {name: i for i, name in enumerate(CHUNKS)}

    loads = {}

    def load(name, src, dst):
        loads[name] = (src, dst, len(loads))
        pltpu.make_async_copy(src, dst, load_sem.at[loads[name][2]]).start()

    def ready(*names):
        for name in names:
            src, dst, i = loads[name]
            pltpu.make_async_copy(src, dst, load_sem.at[i]).wait()

    def token_copies(t, half, b):
        c = layer_rows(pc, 0) if half == 0 else layer_rows(pc, 1)
        d = pc.k * 2 + pc.pack % 2
        m = pc.pack // 2
        src = (kept["out"], gb_v)[t].at[pl.ds(pl.multiple_of(half * BLK + b * slot, slot), slot)]
        dst = tok.at[t, m, pl.ds(pl.multiple_of(d * slot, slot), slot)]
        rs = tok_rs.at[t, m, d]
        same = (b == pc.dp) & (c == pc.ctx)
        return (
            same,
            pltpu.make_async_copy(src, dst, rs),
            remote(src, dst, tok_ss.at[t, half, b], rs, (b, c)),
        )

    def send_tokens(t):
        for half in range(2):

            def one(b, carry):
                same, near, far = token_copies(t, half, b)

                @pl.when(same)
                def _():
                    near.start()

                @pl.when(jnp.logical_not(same))
                def _():
                    far.start()

                return carry

            lax.fori_loop(0, ndp, one, 0)

    def place_tokens(t):
        for half in range(2):

            def sent(b, carry):
                same, _near, far = token_copies(t, half, b)

                @pl.when(jnp.logical_not(same))
                def _():
                    far.wait_send()

                return carry

            lax.fori_loop(0, ndp, sent, 0)
        for m in range(2):

            def arrived(d, carry):
                dst = tok.at[t, m, pl.ds(pl.multiple_of(d * slot, slot), slot)]
                pltpu.make_async_copy(dst, dst, tok_rs.at[t, m, d]).wait()
                return carry

            lax.fori_loop(0, ndp, arrived, 0)
            hot = (lax.broadcasted_iota(jnp.int32, (BLK, BLK), 0) == order_ref[m]).astype(BF16)
            fin[t][m] = jnp.dot(hot, tok[t, m], preferred_element_type=F32).astype(BF16)

    load("dy", kept["dy"], dy_v)

    def feed_forward(inner_t, wdown, slope, act, wgate, wup, n2_t, gn2):
        load("inner_t", kept["inner_t"], inner_t)
        load("wdown", wdown_h, wdown)
        load("slope", kept["slope"], slope)
        load("act", kept["act"], act)
        load("n2_t", kept["n2_t"], n2_t)
        load("wgate", wgate_h, wgate)
        load("wup", wup_h, wup)
        load("hidden", kept["hidden"], hid_v)
        load("att_t", kept["att_t"], att_t)
        load("wout", wout_h, wout)
        load("gain", kept["gain"], gain_v)
        entry_barrier(pc)
        send_tokens(0)
        ready("dy", "inner_t")
        per = BLK // b_down0.shape[1]

        def down(c, carry):
            d = jnp.dot(inner_t[cols(c), :], dy_v[...], preferred_element_type=F32)
            d = d.reshape(per, BLK // per, width)
            for i, buf in enumerate((b_down0, b_down1, b_down2)):
                buf[pl.ds(c * per, per)] = d[:, :, i * third : (i + 1) * third].astype(BF16)
            return carry

        lax.fori_loop(0, ff // BLK, down, 0)
        for i in range(3):
            rounds.begin(chunk[f"down{i}"])
        ready("wdown", "slope", "act", "n2_t", "wgate", "wup")
        gn2[...] = jnp.zeros_like(gn2)
        n_half = half_ff // BLK

        def part(which, c):
            cc = cols(which * n_half + c)
            gi = lax.dot_general(dy_v[...], wdown[cc, :], NT, preferred_element_type=F32)
            gg = (gi * slope[:, cc].astype(F32)).astype(BF16)
            gu = (gi * act[:, cc].astype(F32)).astype(BF16)
            for buf, value in (((b_gate0, b_gate1)[which], gg), ((b_up0, b_up1)[which], gu)):
                d = jnp.dot(n2_t[...], value, preferred_element_type=F32)
                buf[:, :, cols(c)] = d.reshape(n_blocks, -1, BLK).astype(BF16)
            gn2[...] += lax.dot_general(
                gg, wgate[:, cc], NT, preferred_element_type=F32
            ) + lax.dot_general(gu, wup[:, cc], NT, preferred_element_type=F32)

        loop_with_steps(n_half, functools.partial(part, 0), [rounds.take(1) for _ in range(n_half)])
        rounds.begin(chunk["gate0"])
        rounds.begin(chunk["up0"])
        loop_with_steps(n_half, functools.partial(part, 1), [rounds.take(1) for _ in range(n_half)])
        rounds.begin(chunk["gate1"])
        rounds.begin(chunk["up1"])
        ready("hidden", "gain")
        hid = hid_v[...]
        back, d_gain = norm_back(gn2[...], hid, inverse_rms(hid), gain_v[1:2])
        dg_v[1:2] = d_gain.reshape(1, width)
        gh = dy_v[...].astype(F32) + back
        hid_v[...] = gh
        gb_v[...] = gh.astype(BF16)

    pl.run_scoped(
        feed_forward,
        pltpu.VMEM((ff, rows), BF16), pltpu.VMEM((ff, width), BF16), pltpu.VMEM((rows, ff), BF16),
        pltpu.VMEM((rows, ff), BF16), pltpu.VMEM((width, ff), BF16), pltpu.VMEM((width, ff), BF16),
        pltpu.VMEM((width, rows), BF16), pltpu.VMEM((rows, width), F32),
    )

    def head_pairs(kv_v, rope_v, gqkv, q_v, bias_v, lse_v, acc):
        load("q", kept["q"], q_v)
        load("bias", kept["bias"], bias_v)
        load("lse", kept["lse"], lse_v)
        ready("att_t", "wout")

        def out_part(c, carry):
            d = jnp.dot(att_t[...], gb_v[:, cols(c)], preferred_element_type=F32)
            b_out[:, :, cols(c)] = d.reshape(n_blocks, -1, BLK).astype(BF16)
            gatt_v[:, cols(c)] = lax.dot_general(
                gb_v[...], wout[cols(c), :], NT, preferred_element_type=F32
            ).astype(BF16)
            return carry

        lax.fori_loop(0, width // BLK, out_part, 0)
        rounds.begin(chunk["out"])
        ready("q", "kv", "bias", "lse", "rope")
        cos_t, sin_t = rope_v[:, 0:128], rope_v[:, 128:256]

        def pair(hp):
            hc = cols(hp, 128)
            vc = pl.ds(pl.multiple_of(width + hp * 128, 128), 128)
            acc[...] = jnp.zeros_like(acc)
            at = 0
            for half in range(2):
                nk = (half + 1) * pc.g * BLK
                rr = slice(half * BLK, (half + 1) * BLK)
                qp, dop = q_v[rr, hc], gatt_v[rr, hc]
                both = []
                for h in range(2):
                    qm = (jnp.where(lane_mask(h), qp, 0) * 0.125).astype(BF16)
                    dom = jnp.where(lane_mask(h), dop, 0).astype(BF16)
                    s = lax.dot_general(kv_v[0:nk, hc], qm, NT, preferred_element_type=F32)
                    p = jnp.exp(s + bias_v[at : at + nk] - lse_v[hp, h : h + 1, rr])
                    dp = lax.dot_general(kv_v[0:nk, vc], dom, NT, preferred_element_type=F32)
                    weighted = jnp.sum(p * dp, axis=0, keepdims=True)
                    ds = (p * (dp - weighted)).astype(BF16)
                    acc[0:nk, 0:128] += jnp.dot(ds, qm, preferred_element_type=F32)
                    acc[0:nk, 128:256] += jnp.dot(
                        p.astype(BF16), dom, preferred_element_type=F32
                    )
                    both.append(
                        lax.dot_general(kv_v[0:nk, hc], ds, TN, preferred_element_type=F32)
                    )
                sub = lax.broadcasted_iota(jnp.int32, (128, BLK), 0)
                dq = (jnp.where(sub < 64, both[0], both[1]) * 0.125).T
                gqkv[rr, hc] = turned(dq, cos_t[rr], -sin_t[rr]).astype(BF16)
                at += nk
            kv_v[:, hc] = acc[:, 0:128].astype(BF16)
            kv_v[:, vc] = acc[:, 128:256].astype(BF16)

        loop_with_steps(HEADS // 2, pair, [rounds.take(3) for _ in range(HEADS // 2)])

    def attention(kv_v, n1_t, rope_v, gqkv):
        load("kv", kept["kv"], kv_v)
        load("rope", kept["rope"], rope_v)
        load("n1_t", kept["n1_t"], n1_t)
        pl.run_scoped(
            functools.partial(head_pairs, kv_v, rope_v, gqkv),
            pltpu.VMEM((rows, width), BF16), pltpu.VMEM((3 * pc.g * BLK, BLK), F32),
            pltpu.VMEM((HEADS // 2, 2, rows), F32), pltpu.VMEM((pc.g * rows, 256), F32),
        )
        pl.run_scoped(
            functools.partial(last_part, kv_v, n1_t, rope_v, gqkv),
            pltpu.VMEM((rows, width), BF16), pltpu.VMEM((width, 3 * width), BF16),
        )

    def last_part(dkv_v, n1_t, rope_v, gqkv, x_v, wqkv):
        load("wqkv", wqkv_h, wqkv)
        load("x", kept["x"], x_v)
        cos_t, sin_t = rope_v[:, 0:128], rope_v[:, 128:256]
        copies = []
        for o in range(1, pc.g):
            to = (pc.j + o) % pc.g
            for half in range(2):
                where = to if half == 0 else 2 * pc.g - 1 - to
                copies.append(
                    remote(
                        block_at(dkv_v, where), dkv_in.at[o - 1, half],
                        dkv_ss.at[half, o - 1], dkv_rs.at[half, o - 1], pc.member(to),
                    )
                )
        start_all(copies)
        ready("n1_t")

        def weight_grad(name, base, buf):
            def one(c, carry):
                d = jnp.dot(
                    n1_t[...], gqkv[:, pl.ds(pl.multiple_of(base + c * BLK, BLK), BLK)],
                    preferred_element_type=F32,
                )
                buf[:, :, cols(c)] = d.reshape(n_blocks, -1, BLK).astype(BF16)
                return carry

            lax.fori_loop(0, width // BLK, one, 0)
            rounds.begin(chunk[name])

        while any(t in (chunk["gate0"], chunk["up0"], chunk["gate1"]) and s < 3 for t, s in rounds.todo):
            rounds.run()
        weight_grad("q", 0, b_gate0)
        rounds.run(1)
        wait_arrived(copies)
        for half in range(2):
            own = pl.ds(pl.multiple_of(layer_rows(pc, half) * BLK, BLK), BLK)
            rr = slice(half * BLK, (half + 1) * BLK)
            for i in range(2 * width // BLK):
                cc = slice(i * BLK, (i + 1) * BLK)
                total = dkv_v[own, cc].astype(F32)
                for o in range(1, pc.g):
                    total = total + dkv_in[o - 1, half, :, cc].astype(F32)
                if i < width // BLK:
                    total = turned(total, cos_t[rr], -sin_t[rr])
                gqkv[rr, width + i * BLK : width + (i + 1) * BLK] = total.astype(BF16)
        weight_grad("k", width, b_up0)
        weight_grad("v", 2 * width, b_gate1)
        rounds.run(1)
        ready("wqkv", "x")
        gn1 = lax.dot_general(gqkv[...], wqkv[...], NT, preferred_element_type=F32)
        x = x_v[...].astype(F32)
        back, d_gain = norm_back(gn1, x, inverse_rms(x), gain_v[0:1])
        dg_v[0:1] = d_gain.reshape(1, width)
        gb_v[...] = (hid_v[...] + back).astype(BF16)
        send_tokens(1)
        place_tokens(0)
        for cp in copies:
            cp.wait_send()

    pl.run_scoped(
        attention,
        pltpu.VMEM((pc.g * rows, 2 * width), BF16), pltpu.VMEM((width, rows), BF16),
        pltpu.VMEM((rows, 256), F32), pltpu.VMEM((rows, 3 * width), BF16),
    )
    row = lax.broadcasted_iota(jnp.int32, (b_gain.shape[0] * b_gain.shape[1], width), 0)
    col = lax.broadcasted_iota(jnp.int32, row.shape, 1)
    spread = jnp.where(row % SLOTS == 0, dg_v[0:1], jnp.where(row % SLOTS == 1, dg_v[1:2], 0.0))
    spread = jnp.where(row // SLOTS == col // share, spread, 0.0).astype(BF16)
    lane = lax.broadcasted_iota(jnp.int32, (width, 128), 1)
    col = lax.broadcasted_iota(jnp.int32, (width, 128), 0)
    tiles = jnp.dot(spread, (col % share == lane).astype(BF16), preferred_element_type=F32)
    b_gain[...] = tiles.reshape(b_gain.shape).astype(BF16)
    rounds.begin(chunk["gain"])
    while rounds.todo:
        rounds.run()
    place_tokens(1)
    scatter.wait_sent()


def backward(ndp, nctx, pre, share, order, kept, weights):
    wqkv, wout, wgate, wup, wdown = weights
    nz, na, nb, g = nctx // pre, ndp // 4, 2, nctx // 2
    n_blocks = ndp * nz
    rows, width = kept["dy"].shape
    ff = wgate.shape[1]
    r = width // n_blocks
    rd = ff // n_blocks
    n_all = ndp * nctx
    rg = SLOTS * pre
    dma = pltpu.SemaphoreType.DMA
    specs = dict(
        down0=(rd, width // 3), down1=(rd, width // 3), down2=(rd, width // 3),
        gate0=(r, ff // 2), up0=(r, ff // 2), gate1=(r, ff // 2), up1=(r, ff // 2), out=(r, width),
        q=(r, width), k=(r, width), v=(r, width), gain=(rg, 128),
    )
    spec = [specs[name] for name in CHUNKS]
    n = len(CHUNKS)
    own = [i for i, name in enumerate(CHUNKS) if name not in ("q", "k", "v")]
    scratch = [pltpu.VMEM((n_blocks,) + spec[i], BF16) for i in own]
    scratch += [pltpu.VMEM((na, nb, nz) + s, BF16) for s in spec]
    scratch += [pltpu.VMEM((na - 1, nb - 1, nz // 2) + s, BF16) for s in spec]
    scratch += [pltpu.VMEM((na - 1, nb - 1, nz // 2) + s, BF16) for s in spec]
    scratch += [pltpu.VMEM((nb - 1, nz) + s, BF16) for s in spec]
    scratch += [pltpu.VMEM((na - 1, nz) + s, BF16) for s in spec]
    scratch += [pltpu.VMEM((nz - 1,) + s, BF16) for s in spec]
    scratch += [
        pltpu.VMEM((2, 2, BLK, width), BF16), pltpu.VMEM((g - 1, 2, BLK, 2 * width), BF16),
        pltpu.VMEM((rows, width), BF16), pltpu.VMEM((rows, width), F32),
        pltpu.VMEM((width, rows), BF16), pltpu.VMEM((width, width), BF16),
        pltpu.VMEM((rows, width), BF16), pltpu.VMEM((rows, width), BF16),
        pltpu.VMEM((8, width), F32), pltpu.VMEM((8, width), F32),
        dma((2, 2, ndp)), dma((2, 2, ndp)), dma((2, g - 1)), dma((2, g - 1)), dma((24,)),
        dma((n, na, nb)), dma((n, na, nb)),
        dma((n, na - 1, nb - 1)), dma((n, na - 1, nb - 1)),
        dma((n, na - 1, nb - 1)), dma((n, na - 1, nb - 1)),
        dma((n, nb - 1)), dma((n, nb - 1)), dma((n, na - 1)), dma((n, na - 1)),
        dma((n, nz - 1)), dma((n, nz - 1)),
    ]
    out_shape = [jax.ShapeDtypeStruct((2, BLK, width), BF16)] * 2
    out_shape += [
        jax.ShapeDtypeStruct(s, F32)
        for s in ((r, 3 * width), (r, width), (r, ff), (r, ff), (rd, width), (rg, 128))
    ]
    return pl.pallas_call(
        functools.partial(backward_kernel, ndp, nctx, pre, share, n),
        out_shape=out_shape,
        in_specs=[VM] + [ANY] * (len(KB_IN) + 5),
        out_specs=[VM] * len(out_shape),
        scratch_shapes=scratch,
        compiler_params=pltpu.CompilerParams(
            collective_id=1, has_side_effects=True, vmem_limit_bytes=63 << 20
        ),
        name="backward",
    )(order, *[kept[k] for k in KB_IN], *weights)


NEG = -1e30


def lane_mask(h):
    lanes = lax.broadcasted_iota(jnp.int32, (1, 128), 1)
    return (lanes < 64) if h == 0 else (lanes >= 64)


def inverse_rms(values):
    return lax.rsqrt(jnp.mean(values * values, axis=-1, keepdims=True) + eps_norm)


def norm_back(grad, values, inverse, gain):
    scaled = grad * gain
    mean = jnp.mean(scaled * values, axis=-1, keepdims=True)
    return (
        inverse * scaled - values * (inverse * inverse * inverse) * mean,
        jnp.sum(grad * values * inverse, axis=0),
    )


def per_device(
    inputs, cotangent, lengths, send_order,
    norm1_gain, qkv_weight, out_weight, norm2_gain, gate_weight, up_weight, down_weight,
):
    ndp, nctx = lax.axis_size("dp"), lax.axis_size("ctx")
    n_all = ndp * nctx
    width = inputs.shape[2]
    head = width // HEADS
    pc = Place(ndp, nctx)
    share = norm1_gain.shape[0]
    pre = 1
    while (share * pre) % 8:
        pre *= 2
    pad = jnp.zeros((SLOTS, 128), BF16).at[0, :share].set(norm1_gain).at[1, :share].set(norm2_gain)
    lens = jnp.zeros((8, 128), jnp.int32).at[:2, : lengths.shape[2]].set(lengths[:, 0])
    shards = [pad, qkv_weight, out_weight, gate_weight, up_weight, down_weight]
    teams = [[t * pre + i for i in range(pre)] for t in range(nctx // pre)]
    if pre > 1:
        shards = [
            lax.all_gather(w, "ctx", axis_index_groups=teams, axis=0, tiled=True) for w in shards
        ]
    half = head // 2
    frequency = rope_base ** (-(jnp.arange(half, dtype=F32) * 2.0 / head))
    frequency = jnp.broadcast_to(jnp.tile(frequency, 128 // half)[None], (8, 128))
    full, kept = forward(
        ndp, nctx, pre, share, inputs, cotangent, jnp.swapaxes(send_order, 1, 2), lens, frequency, shards
    )
    _, wqkv, wout, wgate, wup, wdown = full
    fin_out, fin_gin, *owned = backward(
        ndp, nctx, pre, share, send_order, kept, (wqkv, wout, wgate, wup, wdown)
    )
    if pre > 1:
        owned = [
            lax.psum_scatter(w, "ctx", axis_index_groups=teams, scatter_dimension=0, tiled=True)
            for w in owned
        ]
    s_qkv, s_out, s_gate, s_up, s_down, s_gains = owned
    return (
        fin_out, fin_gin, s_gains[0, :share], s_qkv, s_out, s_gains[1, :share],
        s_gate, s_up, s_down,
    )


def solution(mesh):
    both = ("dp", "ctx")
    in_specs = (
        P(None, both, None), P(None, both, None), P(None, "dp", None), P(None, both, None),
        P(both), P(both, None), P(both, None), P(both), P(both, None), P(both, None), P(both, None),
    )
    out_specs = (
        P(None, both, None), P(None, both, None),
        P(both), P(both, None), P(both, None), P(both), P(both, None), P(both, None), P(both, None),
    )
    return jax.shard_map(
        per_device, mesh=mesh, in_specs=in_specs, out_specs=out_specs, check_vma=False
    )
```

```python
import functools

import jax
import jax.numpy as jnp
import numpy as np
from jax import lax
from jax.experimental import pallas as pl
from jax.experimental.pallas import tpu as pltpu
from jax.sharding import PartitionSpec as P

HEADS = 12
BLK = 256
SLOTS = 8
eps_norm = 1e-05
rope_base = 10000.0
MESH = pl.DeviceIdType.MESH
F32, BF16 = jnp.float32, jnp.bfloat16
NT = (((1,), (1,)), ((), ()))
TN = (((0,), (0,)), ((), ()))
ANY = pl.BlockSpec(memory_space=pl.ANY)
VM = pl.BlockSpec(memory_space=pltpu.VMEM)
SM = pl.BlockSpec(memory_space=pltpu.SMEM)


class Place:
    def __init__(self, ndp, nctx, pre=1):
        self.ndp, self.nctx, self.pre = ndp, nctx, pre
        self.nz = nctx // pre
        self.nb = 2
        self.na = ndp // 4
        self.g = nctx // 2
        self.gz = nctx // 4
        self.dp = lax.axis_index("dp")
        self.ctx = lax.axis_index("ctx")
        self.k, self.core = self.dp // 2, self.dp % 2
        self.ya, self.xb = self.k // self.nb, self.k % self.nb
        self.me = self.dp * nctx + self.ctx
        self.zi = self.ctx // pre
        self.pack = self.ctx // self.gz
        self.j = self.core * self.gz + self.ctx % self.gz

    def member(self, j):
        return (self.k * 2 + j // self.gz, self.pack * self.gz + j % self.gz)

    def holder(self, m, d, c):
        j = jnp.where(c < self.g, c, 2 * self.g - 1 - c)
        return ((d // 2) * 2 + j // self.gz, (m * 2 + d % 2) * self.gz + j % self.gz)

    def dp_of(self, ya, xb, core):
        return (ya * self.nb + xb) * 2 + core


def greet_all(pc):
    total = pc.ndp * pc.nctx
    barrier = pltpu.get_barrier_semaphore()

    def greet(i, carry):
        other = (pc.me + i) % total
        pl.semaphore_signal(
            barrier, inc=1, device_id=(other // pc.nctx, other % pc.nctx), device_id_type=MESH
        )
        return carry

    lax.fori_loop(1, total, greet, 0)


def met_all(pc):
    pl.semaphore_wait(pltpu.get_barrier_semaphore(), pc.ndp * pc.nctx - 1)


def remote(src, dst, ss, rs, dev):
    return pltpu.make_async_remote_copy(
        src_ref=src, dst_ref=dst, send_sem=ss, recv_sem=rs, device_id=dev, device_id_type=MESH
    )


class Gather:
    def __init__(self, pc, shards, full, chunks, sems):
        self.pc, self.shards, self.full, self.chunks = pc, shards, full, chunks
        (
            self.own_sem, self.z_ss, self.z_rs, self.x_ss, self.x_rs, self.y_ss, self.y_rs,
            self.fa_ss, self.fa_rs, self.fb_ss, self.fb_rs, self.c_ss, self.c_rs,
        ) = sems

    def cut(self, ref, t, start, count):
        _, c0, cw = self.chunks[t]
        return ref.at[pl.ds(pl.multiple_of(start, 8), count), pl.ds(c0, cw)]

    def rows(self, t):
        return self.shards[self.chunks[t][0]].shape[0]

    def mine(self, t):
        a, c0, cw = self.chunks[t]
        return self.shards[a].at[:, pl.ds(c0, cw)]

    def place(self, t, zi=None, count=1):
        r = self.rows(t)
        zi = self.pc.zi if zi is None else zi
        return self.cut(self.full[self.chunks[t][0]], t, (self.pc.dp * self.pc.nz + zi) * r, count * r)

    def block(self, t, dp, part=None):
        n = self.pc.nz * self.rows(t)
        ref = self.full[self.chunks[t][0]]
        if part is None:
            return self.cut(ref, t, dp * n, n)
        return self.cut(ref, t, dp * n + part * (n // 2), n // 2)

    def own_copy(self, t):
        return pltpu.make_async_copy(self.mine(t), self.place(t), self.own_sem.at[t])

    def z_copies(self, t):
        pc = self.pc
        return [
            remote(
                self.mine(t), self.place(t), self.z_ss.at[t, d - 1], self.z_rs.at[t, d - 1],
                (pc.dp, (pc.ctx + d * pc.pre) % pc.nctx),
            )
            for d in range(1, pc.nz)
        ]


    def paired(self, t):
        return self.pc.nz == 4 and t >= STRAIGHT

    def pair_copies(self, t):
        pc = self.pc
        pair = pc.zi + 1 - 2 * (pc.zi % 2)
        near, far = pc.zi // 2 * 2, 2 - pc.zi // 2 * 2

        def at(z):
            return (pc.dp, pc.ctx + (z - pc.zi) * pc.pre)

        def copy(src, dst, i, z):
            return remote(src, dst, self.z_ss.at[t, i], self.z_rs.at[t, i], at(z))

        return (
            copy(self.mine(t), self.place(t), 0, pair),
            copy(self.place(t, near, 2), self.place(t, near, 2), 1, 3 - pc.zi),
            copy(self.place(t, far, 2), self.place(t, far, 2), 2, pair),
        )

    def inner(self):
        return (self.pc.zi == 1) | (self.pc.zi == 2)

    def z_start(self, t):
        if self.paired(t):
            self.pair_copies(t)[0].start()
        else:
            start_all(self.z_copies(t))

    def z_middle(self, t):
        self.own_copy(t).wait()
        if self.paired(t):
            own, both, _on = self.pair_copies(t)

            @pl.when(self.inner())
            def _():
                own.wait_recv()
                both.start()

    def z_finish(self, t):
        if self.paired(t):
            own, both, on = self.pair_copies(t)

            @pl.when(self.inner())
            def _():
                both.wait_recv()
                on.start()

            @pl.when(jnp.logical_not(self.inner()))
            def _():
                own.wait_recv()
                on.wait_recv()

        else:
            wait_arrived(self.z_copies(t))

    def z_sent(self, t):
        if self.paired(t):
            own, both, on = self.pair_copies(t)
            own.wait_send()

            @pl.when(self.inner())
            def _():
                both.wait_send()
                on.wait_send()

        else:
            for cp in self.z_copies(t):
                cp.wait_send()

    def xy_copies(self, t):
        pc = self.pc
        out = []
        for d in range(1, pc.nb):
            to = (pc.dp_of(pc.ya, (pc.xb + d) % pc.nb, pc.core), pc.ctx)
            out.append(
                remote(
                    self.block(t, pc.dp), self.block(t, pc.dp),
                    self.x_ss.at[t, d - 1], self.x_rs.at[t, d - 1], to,
                )
            )
        for d in range(1, pc.na):
            to = (pc.dp_of((pc.ya + d) % pc.na, pc.xb, pc.core), pc.ctx)
            out.append(
                remote(
                    self.block(t, pc.dp), self.block(t, pc.dp),
                    self.y_ss.at[t, d - 1], self.y_rs.at[t, d - 1], to,
                )
            )
        return out

    def forward_copies(self, t):
        pc = self.pc
        out = []
        for dx in range(1, pc.nb):
            for dy in range(1, pc.na):
                src = pc.dp_of(pc.ya, (pc.xb + pc.nb - dx) % pc.nb, pc.core)
                out.append(
                    remote(
                        self.block(t, src, 0), self.block(t, src, 0),
                        self.fa_ss.at[t, dx - 1, dy - 1], self.fa_rs.at[t, dx - 1, dy - 1],
                        (pc.dp_of((pc.ya + dy) % pc.na, pc.xb, pc.core), pc.ctx),
                    )
                )
                src = pc.dp_of((pc.ya + pc.na - dy) % pc.na, pc.xb, pc.core)
                out.append(
                    remote(
                        self.block(t, src, 1), self.block(t, src, 1),
                        self.fb_ss.at[t, dx - 1, dy - 1], self.fb_rs.at[t, dx - 1, dy - 1],
                        (pc.dp_of(pc.ya, (pc.xb + dx) % pc.nb, pc.core), pc.ctx),
                    )
                )
        return out

    def core_copy(self, t, dy, dx):
        pc = self.pc
        src = pc.dp_of((pc.ya + pc.na - dy) % pc.na, (pc.xb + pc.nb - dx) % pc.nb, pc.core)
        return remote(
            self.block(t, src), self.block(t, src), self.c_ss.at[t, dy, dx], self.c_rs.at[t, dy, dx],
            (pc.k * 2 + 1 - pc.core, pc.ctx),
        )

    def core_copies(self, t, which):
        pc = self.pc
        pairs = {
            "own": [(0, 0)],
            "xy": [(0, dx) for dx in range(1, pc.nb)] + [(dy, 0) for dy in range(1, pc.na)],
            "diag": [(dy, dx) for dy in range(1, pc.na) for dx in range(1, pc.nb)],
        }[which]
        return [self.core_copy(t, dy, dx) for dy, dx in pairs]

    def step(self, t, stage):
        if stage == 0:
            self.z_start(t)
        elif stage == -1:
            self.z_middle(t)
        elif stage == 1:
            self.z_finish(t)
            start_all(self.xy_copies(t) + self.core_copies(t, "own"))
        elif stage == 2:
            wait_arrived(self.xy_copies(t))
            start_all(self.forward_copies(t) + self.core_copies(t, "xy"))
        elif stage == 3:
            wait_arrived(self.forward_copies(t))
            start_all(self.core_copies(t, "diag"))
        else:
            wait_arrived([cp for w in ("own", "xy", "diag") for cp in self.core_copies(t, w)])

    def wait_sent(self):
        for t in range(len(self.chunks)):
            self.z_sent(t)
            for cp in self.xy_copies(t) + self.forward_copies(t):
                cp.wait_send()
            for w in ("own", "xy", "diag"):
                for cp in self.core_copies(t, w):
                    cp.wait_send()


def start_all(copies):
    for cp in copies:
        cp.start()


def wait_arrived(copies):
    for cp in copies:
        cp.wait_recv()


class Steps:
    def __init__(self):
        self.todo = []
        self.done = set()

    def add(self, name, fn):
        self.todo.append((name, fn))

    def run(self, count=1):
        for _ in range(count):
            if self.todo:
                name, fn = self.todo.pop(0)
                fn()
                self.done.add(name)

    def until(self, name):
        while name not in self.done:
            self.run()

    def take(self, count):
        out, self.todo = self.todo[:count], self.todo[count:]
        for name, _ in out:
            self.done.add(name)
        return [fn for _, fn in out]


def loop_with_steps(n, body, groups):
    def one(i, carry):
        body(i)
        for at, group in enumerate(groups):
            if group:

                @pl.when(i == at)
                def _():
                    for fn in group:
                        fn()

        return carry

    lax.fori_loop(0, n, one, 0)


def lane_swap(u):
    lane = lax.broadcasted_iota(jnp.int32, (1, 128), 1) % 64
    return jnp.where(lane < 32, pltpu.roll(u, 96, 1), pltpu.roll(u, 32, 1))


def turned(u, cos_t, sin_t):
    parts = []
    for i in range(u.shape[1] // 128):
        v = u[:, i * 128 : (i + 1) * 128]
        parts.append(v * cos_t + lane_swap(v) * sin_t)
    return jnp.concatenate(parts, axis=1)


def cols(i, size=256):
    return pl.ds(pl.multiple_of(i * size, size), size)


def layer_rows(pc, half):
    return pc.j if half == 0 else 2 * pc.g - 1 - pc.j


def gain_row(tiles, which, share, width):
    lane = lax.broadcasted_iota(jnp.int32, (128, width), 0)
    col = lax.broadcasted_iota(jnp.int32, (128, width), 1)
    spread = (lane == col % share).astype(BF16)
    wide = jnp.dot(tiles, spread, preferred_element_type=F32)
    row = lax.broadcasted_iota(jnp.int32, wide.shape, 0)
    col = lax.broadcasted_iota(jnp.int32, wide.shape, 1)
    keep = row == SLOTS * (col // share) + which
    return jnp.sum(jnp.where(keep, wide, 0.0), axis=0, keepdims=True)


class Scatter:
    def __init__(self, pc, grads, shares, bufs, sems):
        self.pc, self.grads, self.shares = pc, grads, shares
        self.core_in, self.diag_a, self.diag_b, self.x_in, self.y_in, self.z_in = bufs
        (
            self.c_ss, self.c_rs, self.da_ss, self.da_rs, self.db_ss, self.db_rs,
            self.x_ss, self.x_rs, self.y_ss, self.y_rs, self.z_ss, self.z_rs,
        ) = sems
        self.yx = [(dy, dx) for dy in range(1, pc.na) for dx in range(1, pc.nb)]
        self.yx += [(0, dx) for dx in range(1, pc.nb)] + [(dy, 0) for dy in range(1, pc.na)]
        self.yx += [(0, 0)]

    def first(self, dy, dx, core):
        pc = self.pc
        k = ((pc.ya + dy) % pc.na) * pc.nb + (pc.xb + dx) % pc.nb
        return (k * 2 + core) * pc.nz

    def core_copies(self, t):
        pc = self.pc
        return [
            remote(
                self.grads[t].at[pl.ds(self.first(dy, dx, 1 - pc.core), pc.nz)],
                self.core_in[t].at[dy, dx], self.c_ss.at[t, dy, dx], self.c_rs.at[t, dy, dx],
                (pc.k * 2 + 1 - pc.core, pc.ctx),
            )
            for dy, dx in self.yx
        ]

    def diag_copies(self, t):
        pc = self.pc
        h = pc.nz // 2
        out = []
        for dy in range(1, pc.na):
            for dx in range(1, pc.nb):
                out.append(
                    remote(
                        self.core_in[t].at[dy, dx, pl.ds(0, h)], self.diag_a[t].at[dy - 1, dx - 1],
                        self.da_ss.at[t, dy - 1, dx - 1], self.da_rs.at[t, dy - 1, dx - 1],
                        (pc.dp_of((pc.ya + dy) % pc.na, pc.xb, pc.core), pc.ctx),
                    )
                )
                out.append(
                    remote(
                        self.core_in[t].at[dy, dx, pl.ds(h, h)], self.diag_b[t].at[dy - 1, dx - 1],
                        self.db_ss.at[t, dy - 1, dx - 1], self.db_rs.at[t, dy - 1, dx - 1],
                        (pc.dp_of(pc.ya, (pc.xb + dx) % pc.nb, pc.core), pc.ctx),
                    )
                )
        return out

    def xy_copies(self, t):
        pc = self.pc
        out = []
        for dx in range(1, pc.nb):
            out.append(
                remote(
                    self.core_in[t].at[0, dx], self.x_in[t].at[dx - 1],
                    self.x_ss.at[t, dx - 1], self.x_rs.at[t, dx - 1],
                    (pc.dp_of(pc.ya, (pc.xb + dx) % pc.nb, pc.core), pc.ctx),
                )
            )
        for dy in range(1, pc.na):
            out.append(
                remote(
                    self.core_in[t].at[dy, 0], self.y_in[t].at[dy - 1],
                    self.y_ss.at[t, dy - 1], self.y_rs.at[t, dy - 1],
                    (pc.dp_of((pc.ya + dy) % pc.na, pc.xb, pc.core), pc.ctx),
                )
            )
        return out

    def z_copies(self, t):
        pc = self.pc
        return [
            remote(
                self.core_in[t].at[0, 0, (pc.zi + d) % pc.nz], self.z_in[t].at[d - 1],
                self.z_ss.at[t, d - 1], self.z_rs.at[t, d - 1],
                (pc.dp, (pc.ctx + d * pc.pre) % pc.nctx),
            )
            for d in range(1, pc.nz)
        ]

    def step(self, t, stage):
        pc = self.pc
        h = pc.nz // 2
        if stage == 0:
            start_all(self.core_copies(t))
        elif stage == 1:
            wait_arrived(self.core_copies(t))
            for dy, dx in self.yx:
                first = self.first(dy, dx, pc.core)
                self.accumulate(t, dy, dx, 0, pc.nz, [lambda z, f=first: self.grads[t][f + z]])
            start_all(self.diag_copies(t))
        elif stage == 2:
            for cp in self.core_copies(t):
                cp.wait_send()
            wait_arrived(self.diag_copies(t))
            for dx in range(1, pc.nb):
                self.accumulate(
                    t, 0, dx, 0, h,
                    [lambda z, dy=dy: self.diag_a[t][dy - 1, dx - 1, z] for dy in range(1, pc.na)],
                )
            for dy in range(1, pc.na):
                self.accumulate(
                    t, dy, 0, h, h,
                    [lambda z, dx=dx: self.diag_b[t][dy - 1, dx - 1, z] for dx in range(1, pc.nb)],
                )
            start_all(self.xy_copies(t))
        elif stage == 3:
            wait_arrived(self.xy_copies(t))
            self.accumulate(
                t, 0, 0, 0, pc.nz,
                [lambda z, i=i: self.x_in[t][i, z] for i in range(pc.nb - 1)]
                + [lambda z, i=i: self.y_in[t][i, z] for i in range(pc.na - 1)],
            )
            start_all(self.z_copies(t))
        else:
            wait_arrived(self.z_copies(t))
            total = self.core_in[t][0, 0, pc.zi].astype(F32)
            for i in range(pc.nz - 1):
                total = total + self.z_in[t][i].astype(F32)
            self.shares[t][...] = total

    def accumulate(self, t, dy, dx, z0, count, others):
        ref = self.core_in[t]

        def one(z, carry):
            total = ref[dy, dx, z0 + z].astype(F32)
            for other in others:
                total = total + other(z).astype(F32)
            ref[dy, dx, z0 + z] = total.astype(BF16)
            return carry

        lax.fori_loop(0, count, one, 0)

    def wait_sent(self):
        for t in range(len(self.grads)):
            for cp in self.diag_copies(t) + self.xy_copies(t) + self.z_copies(t):
                cp.wait_send()


class Rounds(Steps):
    def __init__(self, scatter, stages):
        super().__init__()
        self.scatter, self.stages = scatter, stages
        self.last = []

    def begin(self, t):
        self.scatter.step(t, 0)
        self.todo.append((t, 1))

    def take(self, count):
        out = []
        for _ in range(count):
            if self.todo:
                t, stage = self.todo.pop(0)
                out.append(functools.partial(self.scatter.step, t, stage))
                if stage + 1 < self.stages - 1:
                    self.todo.append((t, stage + 1))
                else:
                    self.last.append(t)
        return out

    def finish(self):
        while self.todo:
            self.run()
        for t in self.last:
            self.scatter.step(t, self.stages - 1)

    def run(self, count=1):
        for fn in self.take(count):
            fn()

    def push(self, *chunks):
        for t in chunks:
            i = [c for c, _ in self.todo].index(t)
            self.todo.insert(0, self.todo.pop(i))
            self.run(1)


def block_at(ref, index, size=BLK):
    return ref.at[pl.ds(pl.multiple_of(index * size, size), size)]


NEG = -1e30


def lane_mask(h):
    lanes = lax.broadcasted_iota(jnp.int32, (1, 128), 1)
    return (lanes < 64) if h == 0 else (lanes >= 64)


def inverse_rms(values):
    return lax.rsqrt(jnp.mean(values * values, axis=-1, keepdims=True) + eps_norm)


def norm_back(grad, values, inverse, gain):
    scaled = grad * gain
    mean = jnp.mean(scaled * values, axis=-1, keepdims=True)
    return (
        inverse * scaled - values * (inverse * inverse * inverse) * mean,
        jnp.sum(grad * values * inverse, axis=0),
    )


AHEAD = 5
BEFORE_X = ('xy', 4)
STRAIGHT = 4
LOOP_ROUNDS = (2, 2, 2, 1, 1, 1)
ORDER_BEFORE = ()
ORDER_AT = {0: (0,), 1: (1,), 2: (2,), 3: (3,), 4: (4,), 5: (5,), 6: (6,), 7: (7,)}
CHUNKS = ("gate0", "up0", "gate1", "up1", "down0", "down1", "down2", "out", "q", "k", "v", "gain")


def layer_kernel(
    ndp, nctx, pre, share, chunks, order_ref, len_ref, freq_ref, x_hbm, dy_hbm, *refs
):
    nt, nch = 6, len(CHUNKS)
    shards, refs = refs[:nt], refs[nt:]
    full, refs = refs[:nt], refs[nt:]
    fin, refs = refs[:2], refs[2:]
    (s_qkv, s_out, s_gate, s_up, s_down, s_gain), refs = refs[:6], refs[6:]
    (b_gate0, b_up0, b_gate1, b_up1, b_down, b_out, b_gain), refs = refs[:7], refs[7:]
    bufs = [refs[i * nch : (i + 1) * nch] for i in range(6)]
    refs = refs[6 * nch :]
    (
        x_v, dy_v, kv_v, dkv_in, tok, plen, hid_v, q_v, lse_v, att_t, n1_t, rope_v, bias_v, gb_v, out_v,
        gain_v, dg_v, tiles_v,
        tok_ss, tok_rs, ret_ss, ret_rs, len_ss, len_rs, kv_ss, kv_rs, dkv_ss, dkv_rs, load_sem, fin_sem,
        *sems,
    ) = refs
    pc = Place(ndp, nctx, pre)
    rows, width = x_v.shape
    ff = s_gate.shape[1]
    half_ff, third = ff // 2, width // 3
    slot = BLK // ndp
    n_blocks = ndp * pc.nz
    gather = Gather(pc, shards, full, chunks, sems[:13])
    narrow = slice(0, width)
    grads = [b_gate0, b_up0, b_gate1, b_up1]
    grads += [b_down.at[:, :, i * third : (i + 1) * third] for i in range(3)] + [b_out]
    grads += [b.at[:, :, narrow] for b in (b_gate0, b_up0, b_gate1)] + [b_gain]
    shares = [s_gate.at[:, pl.ds(0, half_ff)], s_up.at[:, pl.ds(0, half_ff)]]
    shares += [s_gate.at[:, pl.ds(half_ff, half_ff)], s_up.at[:, pl.ds(half_ff, half_ff)]]
    shares += [s_down.at[:, pl.ds(i * third, third)] for i in range(3)] + [s_out]
    shares += [s_qkv.at[:, pl.ds(i * width, width)] for i in range(3)] + [s_gain]
    scatter = Scatter(pc, grads, shares, bufs, sems[13:])
    rounds = Rounds(scatter, 5)
    chunk = {name: i for i, name in enumerate(CHUNKS)}
    partner = (pc.k * 2 + 1 - pc.core, pc.ctx)
    last_of = {a: max(t for t in range(len(chunks)) if chunks[t][0] == a) for a in range(nt)}
    loads = {}

    def load(name, src, dst):
        loads[name] = (src, dst, len(loads))
        pltpu.make_async_copy(src, dst, load_sem.at[loads[name][2]]).start()

    def ready(*names):
        for name in names:
            src, dst, i = loads[name]
            pltpu.make_async_copy(src, dst, load_sem.at[i]).wait()


    def to_pack(perm, t, m, d):
        dp_to, ctx_to = pc.holder(m, d, pc.ctx)
        half = jnp.where(pc.ctx < pc.g, 0, 1)
        src = perm.at[t, m, pl.ds(pl.multiple_of(d * slot, slot), slot)]
        dst = (x_v, dy_v)[t].at[pl.ds(pl.multiple_of(half * BLK + pc.dp * slot, slot), slot)]
        rs = tok_rs.at[t, half, pc.dp]
        same = (dp_to == pc.dp) & (ctx_to == pc.ctx)
        return same, src, dst, tok_ss.at[t, m, d], rs, (dp_to, ctx_to)

    def to_loader(t, half, b):
        c = layer_rows(pc, half)
        d = pc.k * 2 + pc.pack % 2
        m = pc.pack // 2
        src = (out_v, gb_v)[t].at[pl.ds(pl.multiple_of(half * BLK + b * slot, slot), slot)]
        dst = tok.at[t, m, pl.ds(pl.multiple_of(d * slot, slot), slot)]
        same = (b == pc.dp) & (c == pc.ctx)
        return same, src, dst, ret_ss.at[t, half, b], ret_rs.at[t, m, d], (b, c)

    def send_group(find, gy, gx):
        k = ((pc.ya + gy) % pc.na) * pc.nb + (pc.xb + gx) % pc.nb
        for first in range(2):
            for e in range(2):
                same, src, dst, ss, rs, to = find(first, 2 * k + e)

                @pl.when(same)
                def _():
                    pltpu.make_async_copy(src, dst, rs).start()

                @pl.when(jnp.logical_not(same))
                def _():
                    remote(src, dst, ss, rs, to).start()

    def tokens_sent(find):
        def one(d, carry):
            same, src, dst, ss, rs, to = find(d)

            @pl.when(jnp.logical_not(same))
            def _():
                remote(src, dst, ss, rs, to).wait_send()

            return carry

        lax.fori_loop(0, ndp, one, 0)

    def tokens_arrived(ref, sem_of, base):
        def one(b, carry):
            dst = ref.at[pl.ds(pl.multiple_of(base + b * slot, slot), slot)]
            pltpu.make_async_copy(dst, dst, sem_of(b)).wait()
            return carry

        lax.fori_loop(0, ndp, one, 0)

    def send_back(t):
        for gy, gx in offsets:
            send_group(functools.partial(to_loader, t), gy, gx)

    offsets = [(gy, gx) for gy in range(pc.na) for gx in range(pc.nb)]

    def fin_copy(t):
        return pltpu.make_async_copy(tok.at[t], fin[t], fin_sem.at[t])

    def place_tokens(t):
        for half in range(2):
            tokens_sent(functools.partial(to_loader, t, half))
        for m in range(2):
            tokens_arrived(tok.at[t, m], lambda d, m=m: ret_rs.at[t, m, d], 0)
            hot = (lax.broadcasted_iota(jnp.int32, (BLK, BLK), 0) == order_ref[m]).astype(BF16)
            tok[t, m] = jnp.dot(hot, tok[t, m], preferred_element_type=F32).astype(BF16)
        fin_copy(t).start()

    steps = Steps()
    len_copy = functools.partial(remote, len_ref, plen, len_ss, len_rs, partner)

    def plan(perm):
        n = len(chunks)
        groups = [(t, gy, gx) for t in range(2) for gy, gx in offsets]

        def tokens(i):
            t, gy, gx = groups[i]
            steps.add(("tok", i), functools.partial(send_group, functools.partial(to_pack, perm, t), gy, gx))

        each = len(offsets) // 4

        def some_tokens(q):
            for i in range(q * each, (q + 1) * each):
                tokens(i)

        def middle(i):
            steps.add(("mid", i), functools.partial(gather.step, i, -1))

        for i in range(2):
            middle(i)
        for i in ORDER_BEFORE:
            some_tokens(i)
        for i in range(n + 3):
            if i >= 3:
                steps.add(("c", i - 3), functools.partial(gather.step, i - 3, 4))
            if i < n:
                steps.add(("z", i), functools.partial(gather.step, i, 1))
                if i + 2 < n:
                    middle(i + 2)
                if i + AHEAD < n:
                    steps.add(("start", i + AHEAD), functools.partial(gather.step, i + AHEAD, 0))
                for q in ORDER_AT.get(i, ()):
                    some_tokens(q)
            if 1 <= i <= n:
                steps.add(("xy", i - 1), functools.partial(gather.step, i - 1, 2))
            if 2 <= i <= n + 1:
                steps.add(("f", i - 2), functools.partial(gather.step, i - 2, 3))
        return len(groups)

    def index(shape, axis):
        return lax.broadcasted_iota(jnp.int32, shape, axis).astype(F32)

    def attention_forward(perm, wqkv, wout, n1_v, att_v):
        load("x_in", x_hbm, perm.at[0])
        load("dy_in", dy_hbm, perm.at[1])
        for t in range(len(chunks)):
            gather.own_copy(t).start()
        greet_all(pc)
        for t, name in enumerate(("x_in", "dy_in")):
            ready(name)
            for m in range(2):
                hot = (lax.broadcasted_iota(jnp.int32, (BLK, BLK), 0) == order_ref[m]).astype(BF16)
                perm[t, m] = lax.dot_general(
                    hot, perm[t, m], TN, preferred_element_type=F32
                ).astype(BF16)
        met_all(pc)
        for t in range(AHEAD):
            gather.step(t, 0)
        len_copy().start()
        n_groups = plan(perm)
        steps.until(("xy", 0))

        len_copy().wait_recv()
        lens = jnp.where(pc.pack % 2 == pc.core, len_ref[...], plen[...]).astype(F32)
        lens = jnp.where(pc.pack // 2 == 0, lens[0:1], lens[1:2])
        lane = lax.broadcasted_iota(jnp.int32, (1, 128), 1)
        ends = [jnp.sum(jnp.where(lane <= i, lens, 0.0), axis=1, keepdims=True) for i in range(4)]
        sizes = [jnp.sum(jnp.where(lane == i, lens, 0.0), axis=1, keepdims=True) for i in range(4)]

        def segment(at):
            seg = jnp.zeros(at.shape, F32)
            start = jnp.zeros(at.shape, F32)
            for end, size in zip(ends, sizes):
                passed = (at >= end).astype(F32)
                seg = seg + passed
                start = start + passed * size
            return seg, start

        sign = jnp.where(lane % 64 < 32, -1.0, 1.0)
        at = 0
        for half in range(2):
            base = (layer_rows(pc, half) * BLK).astype(F32)
            here = base + index((BLK, 128), 0)
            _, start = segment(here)
            angle = (here - start) * freq_ref[0:1]
            rope_v[half * BLK : (half + 1) * BLK, 0:128] = jnp.cos(angle)
            rope_v[half * BLK : (half + 1) * BLK, 128:256] = jnp.sin(angle) * sign
            qrow = base + index((1, BLK), 1)
            segq, _ = segment(qrow)
            for kb in range((half + 1) * pc.g):
                krow = kb * BLK + index((BLK, BLK), 0)
                segk, _ = segment(kb * BLK + index((BLK, 1), 0))
                bias_v[at : at + BLK] = jnp.where((segk == segq) & (krow <= qrow), 0.0, NEG).astype(BF16)
                at += BLK
        steps.until(("c", 0))
        load("tiles", full[0], tiles_v)
        ready("tiles")
        gain_v[0:1] = gain_row(tiles_v[...], 0, share, width)
        gain_v[1:2] = gain_row(tiles_v[...], 1, share, width)
        steps.until(("tok", n_groups // 2 - 1))
        steps.until(BEFORE_X)
        for half in range(2):
            tokens_arrived(x_v, lambda b, half=half: tok_rs.at[0, half, b], half * BLK)
        x = x_v[...].astype(F32)
        n1_v[...] = (x * inverse_rms(x) * gain_v[0:1]).astype(BF16)
        n1_t[...] = n1_v[...].T
        steps.run(2)

        cos_t, sin_t = rope_v[:, 0:128], rope_v[:, 128:256]

        def kv_copies(part):
            copies = []
            for half in range(2):
                ref = kv_v.at[
                    pl.ds(pl.multiple_of(layer_rows(pc, half) * BLK, BLK), BLK),
                    pl.ds(part * width, width),
                ]
                for o in range(1, pc.g):
                    copies.append(
                        remote(
                            ref, ref, kv_ss.at[part, half, o - 1], kv_rs.at[part, half, o - 1],
                            pc.member((pc.j + o) % pc.g),
                        )
                    )
            return copies

        def project(base, put, rope):
            def one(i, carry):
                u = jnp.dot(
                    n1_v[...], wqkv[:, pl.ds(pl.multiple_of(base + i * BLK, BLK), BLK)],
                    preferred_element_type=F32,
                )
                if rope:
                    u = turned(u, cos_t, sin_t)
                put(i, u.astype(BF16))
                return carry

            lax.fori_loop(0, width // BLK, one, 0)

        def to_kv(part):
            def put(i, u):
                for half in range(2):
                    kv_v[
                        pl.ds(pl.multiple_of(layer_rows(pc, half) * BLK, BLK), BLK),
                        pl.ds(pl.multiple_of(part * width + i * BLK, BLK), BLK),
                    ] = u[half * BLK : (half + 1) * BLK]

            return put

        def to_q(i, u):
            q_v[:, cols(i)] = u

        steps.until(("c", last_of[1]))
        load("wqkv", full[1], wqkv)
        ready("wqkv")
        project(width, to_kv(0), True)
        start_all(kv_copies(0))
        steps.run(1)
        project(2 * width, to_kv(1), False)
        start_all(kv_copies(1))
        steps.run(1)
        project(0, to_q, True)
        steps.run(2)
        wait_arrived(kv_copies(0) + kv_copies(1))

        def pair(hp):
            hc = cols(hp, 128)
            vc = pl.ds(pl.multiple_of(width + hp * 128, 128), 128)
            at = 0
            for half in range(2):
                nk = (half + 1) * pc.g * BLK
                rr = slice(half * BLK, (half + 1) * BLK)
                qp = q_v[rr, hc]
                both = []
                for h in range(2):
                    qm = (jnp.where(lane_mask(h), qp, 0) * 0.125).astype(BF16)
                    s = lax.dot_general(kv_v[0:nk, hc], qm, NT, preferred_element_type=F32)
                    s = s + bias_v[at : at + nk].astype(F32)
                    top = jnp.max(s, axis=0, keepdims=True)
                    p = jnp.exp(s - top)
                    total = jnp.sum(p, axis=0, keepdims=True)
                    p = (p * (1.0 / total)).astype(BF16)
                    both.append(
                        lax.dot_general(kv_v[0:nk, vc], p, TN, preferred_element_type=F32)
                    )
                    lse_v[hp, h : h + 1, rr] = top + jnp.log(total)
                sub = lax.broadcasted_iota(jnp.int32, (128, BLK), 0)
                o = jnp.where(sub < 64, both[0], both[1])
                att_v[rr, hc] = o.T.astype(BF16)
                att_t[hc, rr] = o.astype(BF16)
                at += nk

        loop_with_steps(HEADS // 2, pair, [steps.take(2) for _ in range(HEADS // 2)])
        steps.until(("c", last_of[2]))
        load("wout", full[2], wout)
        ready("wout")
        hid_v[...] = x_v[...].astype(F32) + jnp.dot(
            att_v[...], wout[...], preferred_element_type=F32
        )
        steps.until(("tok", n_groups - 1))
        for t in range(2):
            for m in range(2):
                tokens_sent(functools.partial(to_pack, perm, t, m))
        for half in range(2):
            tokens_arrived(dy_v, lambda b, half=half: tok_rs.at[1, half, b], half * BLK)
        for cp in kv_copies(0) + kv_copies(1):
            cp.wait_send()

    pl.run_scoped(
        attention_forward,
        pltpu.VMEM((2, 2, BLK, width), BF16), pltpu.VMEM((width, 3 * width), BF16),
        pltpu.VMEM((width, width), BF16), pltpu.VMEM((rows, width), BF16),
        pltpu.VMEM((rows, width), BF16),
    )


    def feed_forward(wdown, wgate, wup, n2_v, n2_t, gn2, res):
        hid = hid_v[...]
        n2_v[...] = (hid * inverse_rms(hid) * gain_v[1:2]).astype(BF16)
        n2_t[...] = n2_v[...].T
        res[...] = hid
        gn2[...] = jnp.zeros_like(gn2)
        steps.run(2)
        steps.until(("c", last_of[5]))
        load("wdown", full[5], wdown)
        n_half = half_ff // BLK
        per = BLK // b_down.shape[1]

        def part(which, c):
            cc = cols(c)
            rr = cols(which * n_half + c)
            g = jnp.dot(n2_v[...], wgate[:, cc], preferred_element_type=F32)
            u = jnp.dot(n2_v[...], wup[:, cc], preferred_element_type=F32)
            gi = lax.dot_general(dy_v[...], wdown[rr, :], NT, preferred_element_type=F32)
            sig = 1.0 / (1.0 + jnp.exp(-g))
            act = g * sig
            inner = (act * u).astype(BF16)
            gg = (gi * u * (sig * (1.0 + g * (1.0 - sig)))).astype(BF16)
            gu = (gi * act).astype(BF16)
            res[...] += jnp.dot(inner, wdown[rr, :], preferred_element_type=F32)
            gn2[...] += lax.dot_general(
                gg, wgate[:, cc], NT, preferred_element_type=F32
            ) + lax.dot_general(gu, wup[:, cc], NT, preferred_element_type=F32)
            for buf, value in (((b_gate0, b_gate1)[which], gg), ((b_up0, b_up1)[which], gu)):
                d = jnp.dot(n2_t[...], value, preferred_element_type=F32)
                buf[:, :, cc] = d.reshape(n_blocks, -1, BLK).astype(BF16)
            d = jnp.dot(inner.T, dy_v[...], preferred_element_type=F32)
            b_down[pl.ds((which * n_half + c) * per, per)] = d.reshape(per, -1, width).astype(BF16)

        def load_half(which):
            n = len(chunks)
            steps.until(("c", n - 3 if which == 0 else n - 1))
            cc = pl.ds(which * half_ff, half_ff)
            load(f"wgate{which}", full[3].at[:, cc], wgate)
            load(f"wup{which}", full[4].at[:, cc], wup)
            ready(f"wgate{which}", f"wup{which}")

        load_half(0)
        ready("wdown")
        loop_with_steps(n_half, functools.partial(part, 0), [steps.take(2) for _ in range(n_half)])
        rounds.begin(chunk["gate0"])
        rounds.begin(chunk["up0"])
        load_half(1)
        while steps.todo:
            steps.run()
        loop_with_steps(n_half, functools.partial(part, 1), [rounds.take(2) if i < 2 else [] for i in range(n_half)])
        for name in ("gate1", "up1", "down0", "down1", "down2"):
            rounds.begin(chunk[name])
        out_v[...] = res[...].astype(BF16)
        hid = hid_v[...]
        back, d_gain = norm_back(gn2[...], hid, inverse_rms(hid), gain_v[1:2])
        dg_v[1:2] = d_gain.reshape(1, width)
        gh = dy_v[...].astype(F32) + back
        hid_v[...] = gh
        gb_v[...] = gh.astype(BF16)
        rounds.push(*[chunk[name] for name in ("gate1", "up1", "down0", "down1", "down2")])

    pl.run_scoped(
        feed_forward,
        pltpu.VMEM((ff, width), BF16), pltpu.VMEM((width, half_ff), BF16),
        pltpu.VMEM((width, half_ff), BF16), pltpu.VMEM((rows, width), BF16),
        pltpu.VMEM((width, rows), BF16), pltpu.VMEM((rows, width), F32), pltpu.VMEM((rows, width), F32),
    )


    def head_pairs(gqkv, wout, gatt_v, acc):
        load("wout_back", full[2], wout)
        ready("wout_back")

        def out_part(c, carry):
            d = jnp.dot(att_t[...], gb_v[:, cols(c)], preferred_element_type=F32)
            b_out[:, :, cols(c)] = d.reshape(n_blocks, -1, BLK).astype(BF16)
            gatt_v[:, cols(c)] = lax.dot_general(
                gb_v[...], wout[cols(c), :], NT, preferred_element_type=F32
            ).astype(BF16)
            return carry

        lax.fori_loop(0, width // BLK, out_part, 0)
        rounds.begin(chunk["out"])
        cos_t, sin_t = rope_v[:, 0:128], rope_v[:, 128:256]

        def pair(hp):
            hc = cols(hp, 128)
            vc = pl.ds(pl.multiple_of(width + hp * 128, 128), 128)
            acc[...] = jnp.zeros_like(acc)
            at = 0
            for half in range(2):
                nk = (half + 1) * pc.g * BLK
                rr = slice(half * BLK, (half + 1) * BLK)
                qp, dop = q_v[rr, hc], gatt_v[rr, hc]
                both = []
                for h in range(2):
                    qm = (jnp.where(lane_mask(h), qp, 0) * 0.125).astype(BF16)
                    dom = jnp.where(lane_mask(h), dop, 0).astype(BF16)
                    s = lax.dot_general(kv_v[0:nk, hc], qm, NT, preferred_element_type=F32)
                    p = jnp.exp(s + bias_v[at : at + nk].astype(F32) - lse_v[hp, h : h + 1, rr])
                    dp = lax.dot_general(kv_v[0:nk, vc], dom, NT, preferred_element_type=F32)
                    weighted = jnp.sum(p * dp, axis=0, keepdims=True)
                    ds = (p * (dp - weighted)).astype(BF16)
                    acc[0:nk, 0:128] += jnp.dot(ds, qm, preferred_element_type=F32)
                    acc[0:nk, 128:256] += jnp.dot(
                        p.astype(BF16), dom, preferred_element_type=F32
                    )
                    both.append(
                        lax.dot_general(kv_v[0:nk, hc], ds, TN, preferred_element_type=F32)
                    )
                sub = lax.broadcasted_iota(jnp.int32, (128, BLK), 0)
                dq = (jnp.where(sub < 64, both[0], both[1]) * 0.125).T
                gqkv[rr, hc] = turned(dq, cos_t[rr], -sin_t[rr]).astype(BF16)
                at += nk
            kv_v[:, hc] = acc[:, 0:128].astype(BF16)
            kv_v[:, vc] = acc[:, 128:256].astype(BF16)

        groups = [rounds.take(n) for n in LOOP_ROUNDS]
        for i, (gy, gx) in enumerate(offsets):
            groups[min(1 + i, 5)].append(
                functools.partial(send_group, functools.partial(to_loader, 0), gy, gx)
            )
        loop_with_steps(HEADS // 2, pair, groups)

    def last_part(gqkv, wqkv):
        load("wqkv_back", full[1], wqkv)
        cos_t, sin_t = rope_v[:, 0:128], rope_v[:, 128:256]
        copies = []
        for o in range(1, pc.g):
            to = (pc.j + o) % pc.g
            for half in range(2):
                where = to if half == 0 else 2 * pc.g - 1 - to
                copies.append(
                    remote(
                        block_at(kv_v, where), dkv_in.at[o - 1, half],
                        dkv_ss.at[half, o - 1], dkv_rs.at[half, o - 1], pc.member(to),
                    )
                )
        start_all(copies)

        def weight_grad(name, base, buf):
            def one(c, carry):
                d = jnp.dot(
                    n1_t[...], gqkv[:, pl.ds(pl.multiple_of(base + c * BLK, BLK), BLK)],
                    preferred_element_type=F32,
                )
                buf[:, :, cols(c)] = d.reshape(n_blocks, -1, BLK).astype(BF16)
                return carry

            lax.fori_loop(0, width // BLK, one, 0)
            rounds.begin(chunk[name])

        while any(t in (chunk["gate0"], chunk["up0"], chunk["gate1"]) and st < 3 for t, st in rounds.todo):
            rounds.run()
        weight_grad("q", 0, b_gate0)
        rounds.run(2)
        wait_arrived(copies)
        rounds.push(chunk["q"])
        for half in range(2):
            own = pl.ds(pl.multiple_of(layer_rows(pc, half) * BLK, BLK), BLK)
            rr = slice(half * BLK, (half + 1) * BLK)
            for i in range(2 * width // BLK):
                cc = slice(i * BLK, (i + 1) * BLK)
                total = kv_v[own, cc].astype(F32)
                for o in range(1, pc.g):
                    total = total + dkv_in[o - 1, half, :, cc].astype(F32)
                if i < width // BLK:
                    total = turned(total, cos_t[rr], -sin_t[rr])
                gqkv[rr, width + i * BLK : width + (i + 1) * BLK] = total.astype(BF16)
        weight_grad("k", width, b_up0)
        weight_grad("v", 2 * width, b_gate1)
        rounds.push(chunk["k"])
        rounds.run(2)
        ready("wqkv_back")
        gn1 = lax.dot_general(gqkv[...], wqkv[...], NT, preferred_element_type=F32)
        x = x_v[...].astype(F32)
        back, d_gain = norm_back(gn1, x, inverse_rms(x), gain_v[0:1])
        dg_v[0:1] = d_gain.reshape(1, width)
        gb_v[...] = (hid_v[...] + back).astype(BF16)
        send_back(1)
        rounds.push(chunk["v"])
        row = lax.broadcasted_iota(jnp.int32, (b_gain.shape[0] * b_gain.shape[1], width), 0)
        col = lax.broadcasted_iota(jnp.int32, row.shape, 1)
        spread = jnp.where(row % SLOTS == 0, dg_v[0:1], jnp.where(row % SLOTS == 1, dg_v[1:2], 0.0))
        spread = jnp.where(row // SLOTS == col // share, spread, 0.0).astype(BF16)
        lane = lax.broadcasted_iota(jnp.int32, (width, 128), 1)
        col = lax.broadcasted_iota(jnp.int32, (width, 128), 0)
        tiles = jnp.dot(spread, (col % share == lane).astype(BF16), preferred_element_type=F32)
        b_gain[...] = tiles.reshape(b_gain.shape).astype(BF16)
        rounds.begin(chunk["gain"])
        rounds.run(4)
        rounds.push(chunk["gain"])
        place_tokens(0)
        for cp in copies:
            cp.wait_send()

    def attention_backward(gqkv):
        pl.run_scoped(
            functools.partial(head_pairs, gqkv),
            pltpu.VMEM((width, width), BF16), pltpu.VMEM((rows, width), BF16),
            pltpu.VMEM((pc.g * rows, 256), F32),
        )
        pl.run_scoped(
            functools.partial(last_part, gqkv), pltpu.VMEM((width, 3 * width), BF16)
        )

    pl.run_scoped(attention_backward, pltpu.VMEM((rows, 3 * width), BF16))
    rounds.finish()
    place_tokens(1)
    len_copy().wait_send()
    gather.wait_sent()
    scatter.wait_sent()
    for t in range(2):
        fin_copy(t).wait()


def layer(ndp, nctx, pre, share, order, lens, freq, x, dy, shards):
    nz, na, nb, g = nctx // pre, ndp // 4, 2, nctx // 2
    n_blocks = ndp * nz
    rows, width = 2 * BLK, x.shape[-1]
    ff = shards[3].shape[1]
    r, rd, rg = width // n_blocks, ff // n_blocks, SLOTS * pre
    dma = pltpu.SemaphoreType.DMA
    chunks = [(0, 0, 128)]
    chunks += [(1, width, width), (1, 2 * width, width), (1, 0, width), (2, 0, width)]
    chunks += [(5, 0, width // 2), (5, width // 2, width // 2)]
    chunks += [(a, c * (ff // 2), ff // 2) for c in range(2) for a in (3, 4)]
    m = len(chunks)
    full = [jax.ShapeDtypeStruct((n_blocks * s.shape[0], s.shape[1]), BF16) for s in shards]
    out_shape = full + [jax.ShapeDtypeStruct((2, BLK, width), BF16)] * 2
    out_shape += [
        jax.ShapeDtypeStruct(s, F32)
        for s in ((r, 3 * width), (r, width), (r, ff), (r, ff), (rd, width), (rg, 128))
    ]
    specs = dict(
        gate0=(r, ff // 2), up0=(r, ff // 2), gate1=(r, ff // 2), up1=(r, ff // 2),
        down0=(rd, width // 3), down1=(rd, width // 3), down2=(rd, width // 3), out=(r, width),
        q=(r, width), k=(r, width), v=(r, width), gain=(rg, 128),
    )
    spec = [specs[name] for name in CHUNKS]
    n = len(CHUNKS)
    scratch = [pltpu.VMEM((n_blocks, r, ff // 2), BF16)] * 4
    scratch += [
        pltpu.VMEM((n_blocks, rd, width), BF16), pltpu.VMEM((n_blocks, r, width), BF16),
        pltpu.VMEM((n_blocks, rg, 128), BF16),
    ]
    scratch += [pltpu.VMEM((na, nb, nz) + s, BF16) for s in spec]
    scratch += [pltpu.VMEM((na - 1, nb - 1, nz // 2) + s, BF16) for s in spec]
    scratch += [pltpu.VMEM((na - 1, nb - 1, nz // 2) + s, BF16) for s in spec]
    scratch += [pltpu.VMEM((nb - 1, nz) + s, BF16) for s in spec]
    scratch += [pltpu.VMEM((na - 1, nz) + s, BF16) for s in spec]
    scratch += [pltpu.VMEM((nz - 1,) + s, BF16) for s in spec]
    scratch += [
        pltpu.VMEM((rows, width), BF16), pltpu.VMEM((rows, width), BF16),
        pltpu.VMEM((g * rows, 2 * width), BF16), pltpu.VMEM((g - 1, 2, BLK, 2 * width), BF16),
        pltpu.VMEM((2, 2, BLK, width), BF16), pltpu.VMEM(lens.shape, lens.dtype),
        pltpu.VMEM((rows, width), F32), pltpu.VMEM((rows, width), BF16),
        pltpu.VMEM((HEADS // 2, 2, rows), F32), pltpu.VMEM((width, rows), BF16),
        pltpu.VMEM((width, rows), BF16), pltpu.VMEM((rows, 256), F32),
        pltpu.VMEM((3 * g * BLK, BLK), BF16), pltpu.VMEM((rows, width), BF16),
        pltpu.VMEM((rows, width), BF16), pltpu.VMEM((8, width), F32), pltpu.VMEM((8, width), F32),
        pltpu.VMEM(full[0].shape, BF16),
        dma((2, 2, ndp)), dma((2, 2, ndp)), dma((2, 2, ndp)), dma((2, 2, ndp)), dma, dma,
        dma((2, 2, g - 1)), dma((2, 2, g - 1)), dma((2, g - 1)), dma((2, g - 1)),
        dma((16,)), dma((2,)),
        dma((m,)), dma((m, nz - 1)), dma((m, nz - 1)),
        dma((m, nb - 1)), dma((m, nb - 1)), dma((m, na - 1)), dma((m, na - 1)),
        dma((m, nb - 1, na - 1)), dma((m, nb - 1, na - 1)),
        dma((m, nb - 1, na - 1)), dma((m, nb - 1, na - 1)),
        dma((m, na, nb)), dma((m, na, nb)),
        dma((n, na, nb)), dma((n, na, nb)),
        dma((n, na - 1, nb - 1)), dma((n, na - 1, nb - 1)),
        dma((n, na - 1, nb - 1)), dma((n, na - 1, nb - 1)),
        dma((n, nb - 1)), dma((n, nb - 1)), dma((n, na - 1)), dma((n, na - 1)),
        dma((n, nz - 1)), dma((n, nz - 1)),
    ]
    res = pl.pallas_call(
        functools.partial(layer_kernel, ndp, nctx, pre, share, chunks),
        out_shape=out_shape,
        in_specs=[VM] * 3 + [ANY] * (2 + len(shards)),
        out_specs=[ANY] * (len(shards) + 2) + [VM] * 6,
        scratch_shapes=scratch,
        compiler_params=pltpu.CompilerParams(
            collective_id=0, has_side_effects=True, vmem_limit_bytes=63 << 20
        ),
        name="layer",
    )(order, lens, freq, x, dy, *shards)
    return res[len(shards) :]


def per_device(
    inputs, cotangent, lengths, send_order,
    norm1_gain, qkv_weight, out_weight, norm2_gain, gate_weight, up_weight, down_weight,
):
    ndp, nctx = lax.axis_size("dp"), lax.axis_size("ctx")
    head = inputs.shape[2] // HEADS
    share = norm1_gain.shape[0]
    pre = 1
    while (share * pre) % 8:
        pre *= 2
    pad = jnp.pad(jnp.stack([norm1_gain, norm2_gain]), ((0, SLOTS - 2), (0, 128 - share)))
    lens = jnp.pad(lengths[:, 0], ((0, 6), (0, 128 - lengths.shape[2])))
    shards = [pad, qkv_weight, out_weight, gate_weight, up_weight, down_weight]
    teams = [[t * pre + i for i in range(pre)] for t in range(nctx // pre)]
    if pre > 1:
        shards = [
            lax.all_gather(w, "ctx", axis_index_groups=teams, axis=0, tiled=True) for w in shards
        ]
    half = head // 2
    frequency = np.float32(rope_base) ** (-(np.arange(half, dtype=np.float32) * 2.0 / head))
    frequency = np.tile(frequency.astype(np.float32), (8, 128 // half))
    fin_out, fin_gin, *owned = layer(
        ndp, nctx, pre, share, send_order, lens, frequency, inputs, cotangent, shards
    )
    if pre > 1:
        owned = [
            lax.psum_scatter(w, "ctx", axis_index_groups=teams, scatter_dimension=0, tiled=True)
            for w in owned
        ]
    s_qkv, s_out, s_gate, s_up, s_down, s_gains = owned
    return (
        fin_out, fin_gin, s_gains[0, :share], s_qkv, s_out, s_gains[1, :share],
        s_gate, s_up, s_down,
    )


def solution(mesh):
    both = ("dp", "ctx")
    in_specs = (
        P(None, both, None), P(None, both, None), P(None, "dp", None), P(None, both, None),
        P(both), P(both, None), P(both, None), P(both), P(both, None), P(both, None), P(both, None),
    )
    out_specs = (
        P(None, both, None), P(None, both, None),
        P(both), P(both, None), P(both, None), P(both), P(both, None), P(both, None), P(both, None),
    )
    return jax.shard_map(
        per_device, mesh=mesh, in_specs=in_specs, out_specs=out_specs, check_vma=False
    )
```

```python
import functools

import jax
import jax.numpy as jnp
import numpy as np
from jax import lax
from jax.experimental import pallas as pl
from jax.experimental.pallas import tpu as pltpu
from jax.sharding import PartitionSpec as P

HEADS = 12
BLK = 256
SLOTS = 8
eps_norm = 1e-05
rope_base = 10000.0
MESH = pl.DeviceIdType.MESH
F32, BF16 = jnp.float32, jnp.bfloat16
NT = (((1,), (1,)), ((), ()))
TN = (((0,), (0,)), ((), ()))
ANY = pl.BlockSpec(memory_space=pl.ANY)
VM = pl.BlockSpec(memory_space=pltpu.VMEM)
SM = pl.BlockSpec(memory_space=pltpu.SMEM)


class Place:
    def __init__(self, ndp, nctx, pre=1):
        self.ndp, self.nctx, self.pre = ndp, nctx, pre
        self.nz = nctx // pre
        self.nb = 2
        self.na = ndp // 4
        self.g = nctx // 2
        self.gz = nctx // 4
        self.dp = lax.axis_index("dp")
        self.ctx = lax.axis_index("ctx")
        self.k, self.core = self.dp // 2, self.dp % 2
        self.ya, self.xb = self.k // self.nb, self.k % self.nb
        self.me = self.dp * nctx + self.ctx
        self.zi = self.ctx // pre
        self.pack = self.ctx // self.gz
        self.j = self.core * self.gz + self.ctx % self.gz

    def member(self, j):
        return (self.k * 2 + j // self.gz, self.pack * self.gz + j % self.gz)

    def holder(self, m, d, c):
        j = jnp.where(c < self.g, c, 2 * self.g - 1 - c)
        return ((d // 2) * 2 + j // self.gz, (m * 2 + d % 2) * self.gz + j % self.gz)

    def dp_of(self, ya, xb, core):
        return (ya * self.nb + xb) * 2 + core


def greet_all(pc):
    total = pc.ndp * pc.nctx
    barrier = pltpu.get_barrier_semaphore()

    def greet(i, carry):
        other = (pc.me + i) % total
        pl.semaphore_signal(
            barrier, inc=1, device_id=(other // pc.nctx, other % pc.nctx), device_id_type=MESH
        )
        return carry

    lax.fori_loop(1, total, greet, 0)


def met_all(pc):
    pl.semaphore_wait(pltpu.get_barrier_semaphore(), pc.ndp * pc.nctx - 1)


def remote(src, dst, ss, rs, dev):
    return pltpu.make_async_remote_copy(
        src_ref=src, dst_ref=dst, send_sem=ss, recv_sem=rs, device_id=dev, device_id_type=MESH
    )


class Gather:
    def __init__(self, pc, shards, full, chunks, sems):
        self.pc, self.shards, self.full, self.chunks = pc, shards, full, chunks
        (
            self.own_sem, self.z_ss, self.z_rs, self.x_ss, self.x_rs, self.y_ss, self.y_rs,
            self.fa_ss, self.fa_rs, self.fb_ss, self.fb_rs, self.c_ss, self.c_rs,
        ) = sems

    def cut(self, ref, t, start, count):
        _, c0, cw = self.chunks[t]
        return ref.at[pl.ds(pl.multiple_of(start, 8), count), pl.ds(c0, cw)]

    def rows(self, t):
        return self.shards[self.chunks[t][0]].shape[0]

    def mine(self, t):
        a, c0, cw = self.chunks[t]
        return self.shards[a].at[:, pl.ds(c0, cw)]

    def place(self, t, zi=None, count=1):
        r = self.rows(t)
        zi = self.pc.zi if zi is None else zi
        return self.cut(self.full[self.chunks[t][0]], t, (self.pc.dp * self.pc.nz + zi) * r, count * r)

    def block(self, t, dp, part=None):
        n = self.pc.nz * self.rows(t)
        ref = self.full[self.chunks[t][0]]
        if part is None:
            return self.cut(ref, t, dp * n, n)
        return self.cut(ref, t, dp * n + part * (n // 2), n // 2)

    def own_copy(self, t):
        return pltpu.make_async_copy(self.mine(t), self.place(t), self.own_sem.at[t])

    def z_copies(self, t):
        pc = self.pc
        return [
            remote(
                self.mine(t), self.place(t), self.z_ss.at[t, d - 1], self.z_rs.at[t, d - 1],
                (pc.dp, (pc.ctx + d * pc.pre) % pc.nctx),
            )
            for d in range(1, pc.nz)
        ]


    def paired(self, t):
        return self.pc.nz == 4 and t >= STRAIGHT

    def pair_copies(self, t):
        pc = self.pc
        pair = pc.zi + 1 - 2 * (pc.zi % 2)
        near, far = pc.zi // 2 * 2, 2 - pc.zi // 2 * 2

        def at(z):
            return (pc.dp, pc.ctx + (z - pc.zi) * pc.pre)

        def copy(src, dst, i, z):
            return remote(src, dst, self.z_ss.at[t, i], self.z_rs.at[t, i], at(z))

        return (
            copy(self.mine(t), self.place(t), 0, pair),
            copy(self.place(t, near, 2), self.place(t, near, 2), 1, 3 - pc.zi),
            copy(self.place(t, far, 2), self.place(t, far, 2), 2, pair),
        )

    def inner(self):
        return (self.pc.zi == 1) | (self.pc.zi == 2)

    def z_start(self, t):
        if self.paired(t):
            self.pair_copies(t)[0].start()
        else:
            start_all(self.z_copies(t))

    def z_middle(self, t):
        self.own_copy(t).wait()
        if self.paired(t):
            own, both, _on = self.pair_copies(t)

            @pl.when(self.inner())
            def _():
                own.wait_recv()
                both.start()

    def z_finish(self, t):
        if self.paired(t):
            own, both, on = self.pair_copies(t)

            @pl.when(self.inner())
            def _():
                both.wait_recv()
                on.start()

            @pl.when(jnp.logical_not(self.inner()))
            def _():
                own.wait_recv()
                on.wait_recv()

        else:
            wait_arrived(self.z_copies(t))

    def z_sent(self, t):
        if self.paired(t):
            own, both, on = self.pair_copies(t)
            own.wait_send()

            @pl.when(self.inner())
            def _():
                both.wait_send()
                on.wait_send()

        else:
            for cp in self.z_copies(t):
                cp.wait_send()

    def xy_copies(self, t):
        pc = self.pc
        out = []
        for d in range(1, pc.nb):
            to = (pc.dp_of(pc.ya, (pc.xb + d) % pc.nb, pc.core), pc.ctx)
            out.append(
                remote(
                    self.block(t, pc.dp), self.block(t, pc.dp),
                    self.x_ss.at[t, d - 1], self.x_rs.at[t, d - 1], to,
                )
            )
        for d in range(1, pc.na):
            to = (pc.dp_of((pc.ya + d) % pc.na, pc.xb, pc.core), pc.ctx)
            out.append(
                remote(
                    self.block(t, pc.dp), self.block(t, pc.dp),
                    self.y_ss.at[t, d - 1], self.y_rs.at[t, d - 1], to,
                )
            )
        return out

    def forward_copies(self, t):
        pc = self.pc
        out = []
        for dx in range(1, pc.nb):
            for dy in range(1, pc.na):
                src = pc.dp_of(pc.ya, (pc.xb + pc.nb - dx) % pc.nb, pc.core)
                out.append(
                    remote(
                        self.block(t, src, 0), self.block(t, src, 0),
                        self.fa_ss.at[t, dx - 1, dy - 1], self.fa_rs.at[t, dx - 1, dy - 1],
                        (pc.dp_of((pc.ya + dy) % pc.na, pc.xb, pc.core), pc.ctx),
                    )
                )
                src = pc.dp_of((pc.ya + pc.na - dy) % pc.na, pc.xb, pc.core)
                out.append(
                    remote(
                        self.block(t, src, 1), self.block(t, src, 1),
                        self.fb_ss.at[t, dx - 1, dy - 1], self.fb_rs.at[t, dx - 1, dy - 1],
                        (pc.dp_of(pc.ya, (pc.xb + dx) % pc.nb, pc.core), pc.ctx),
                    )
                )
        return out

    def core_copy(self, t, dy, dx):
        pc = self.pc
        src = pc.dp_of((pc.ya + pc.na - dy) % pc.na, (pc.xb + pc.nb - dx) % pc.nb, pc.core)
        return remote(
            self.block(t, src), self.block(t, src), self.c_ss.at[t, dy, dx], self.c_rs.at[t, dy, dx],
            (pc.k * 2 + 1 - pc.core, pc.ctx),
        )

    def core_copies(self, t, which):
        pc = self.pc
        pairs = {
            "own": [(0, 0)],
            "xy": [(0, dx) for dx in range(1, pc.nb)] + [(dy, 0) for dy in range(1, pc.na)],
            "diag": [(dy, dx) for dy in range(1, pc.na) for dx in range(1, pc.nb)],
        }[which]
        return [self.core_copy(t, dy, dx) for dy, dx in pairs]

    def step(self, t, stage):
        if stage == 0:
            self.z_start(t)
        elif stage == -1:
            self.z_middle(t)
        elif stage == 1:
            self.z_finish(t)
            start_all(self.xy_copies(t) + self.core_copies(t, "own"))
        elif stage == 2:
            wait_arrived(self.xy_copies(t))
            start_all(self.forward_copies(t) + self.core_copies(t, "xy"))
        elif stage == 3:
            wait_arrived(self.forward_copies(t))
            start_all(self.core_copies(t, "diag"))
        else:
            wait_arrived([cp for w in ("own", "xy", "diag") for cp in self.core_copies(t, w)])

    def wait_sent(self):
        for t in range(len(self.chunks)):
            self.z_sent(t)
            for cp in self.xy_copies(t) + self.forward_copies(t):
                cp.wait_send()
            for w in ("own", "xy", "diag"):
                for cp in self.core_copies(t, w):
                    cp.wait_send()


def start_all(copies):
    for cp in copies:
        cp.start()


def wait_arrived(copies):
    for cp in copies:
        cp.wait_recv()


class Steps:
    def __init__(self):
        self.todo = []
        self.done = set()

    def add(self, name, fn):
        self.todo.append((name, fn))

    def run(self, count=1):
        for _ in range(count):
            if self.todo:
                name, fn = self.todo.pop(0)
                fn()
                self.done.add(name)

    def until(self, name):
        while name not in self.done:
            self.run()

    def take(self, count):
        out, self.todo = self.todo[:count], self.todo[count:]
        for name, _ in out:
            self.done.add(name)
        return [fn for _, fn in out]


def loop_with_steps(n, body, groups):
    def one(i, carry):
        body(i)
        for at, group in enumerate(groups):
            if group:

                @pl.when(i == at)
                def _():
                    for fn in group:
                        fn()

        return carry

    lax.fori_loop(0, n, one, 0)


def lane_swap(u):
    lane = lax.broadcasted_iota(jnp.int32, (1, 128), 1) % 64
    return jnp.where(lane < 32, pltpu.roll(u, 96, 1), pltpu.roll(u, 32, 1))


def turned(u, cos_t, sin_t):
    parts = []
    for i in range(u.shape[1] // 128):
        v = u[:, i * 128 : (i + 1) * 128]
        parts.append(v * cos_t + lane_swap(v) * sin_t)
    return jnp.concatenate(parts, axis=1)


def cols(i, size=256):
    return pl.ds(pl.multiple_of(i * size, size), size)


def layer_rows(pc, half):
    return pc.j if half == 0 else 2 * pc.g - 1 - pc.j


def gain_row(tiles, which, share, width):
    lane = lax.broadcasted_iota(jnp.int32, (128, width), 0)
    col = lax.broadcasted_iota(jnp.int32, (128, width), 1)
    spread = (lane == col % share).astype(BF16)
    wide = jnp.dot(tiles, spread, preferred_element_type=F32)
    row = lax.broadcasted_iota(jnp.int32, wide.shape, 0)
    col = lax.broadcasted_iota(jnp.int32, wide.shape, 1)
    keep = row == SLOTS * (col // share) + which
    return jnp.sum(jnp.where(keep, wide, 0.0), axis=0, keepdims=True)


class Scatter:
    def __init__(self, pc, grads, shares, bufs, sems):
        self.pc, self.grads, self.shares = pc, grads, shares
        self.core_in, self.diag_a, self.diag_b, self.x_in, self.y_in, self.z_in = bufs
        (
            self.c_ss, self.c_rs, self.da_ss, self.da_rs, self.db_ss, self.db_rs,
            self.x_ss, self.x_rs, self.y_ss, self.y_rs, self.z_ss, self.z_rs,
        ) = sems
        self.yx = [(dy, dx) for dy in range(1, pc.na) for dx in range(1, pc.nb)]
        self.yx += [(0, dx) for dx in range(1, pc.nb)] + [(dy, 0) for dy in range(1, pc.na)]
        self.yx += [(0, 0)]

    def first(self, dy, dx, core):
        pc = self.pc
        k = ((pc.ya + dy) % pc.na) * pc.nb + (pc.xb + dx) % pc.nb
        return (k * 2 + core) * pc.nz

    def core_copies(self, t):
        pc = self.pc
        return [
            remote(
                self.grads[t].at[pl.ds(self.first(dy, dx, 1 - pc.core), pc.nz)],
                self.core_in[t].at[dy, dx], self.c_ss.at[t, dy, dx], self.c_rs.at[t, dy, dx],
                (pc.k * 2 + 1 - pc.core, pc.ctx),
            )
            for dy, dx in self.yx
        ]

    def diag_copies(self, t):
        pc = self.pc
        h = pc.nz // 2
        out = []
        for dy in range(1, pc.na):
            for dx in range(1, pc.nb):
                out.append(
                    remote(
                        self.core_in[t].at[dy, dx, pl.ds(0, h)], self.diag_a[t].at[dy - 1, dx - 1],
                        self.da_ss.at[t, dy - 1, dx - 1], self.da_rs.at[t, dy - 1, dx - 1],
                        (pc.dp_of((pc.ya + dy) % pc.na, pc.xb, pc.core), pc.ctx),
                    )
                )
                out.append(
                    remote(
                        self.core_in[t].at[dy, dx, pl.ds(h, h)], self.diag_b[t].at[dy - 1, dx - 1],
                        self.db_ss.at[t, dy - 1, dx - 1], self.db_rs.at[t, dy - 1, dx - 1],
                        (pc.dp_of(pc.ya, (pc.xb + dx) % pc.nb, pc.core), pc.ctx),
                    )
                )
        return out

    def xy_copies(self, t):
        pc = self.pc
        out = []
        for dx in range(1, pc.nb):
            out.append(
                remote(
                    self.core_in[t].at[0, dx], self.x_in[t].at[dx - 1],
                    self.x_ss.at[t, dx - 1], self.x_rs.at[t, dx - 1],
                    (pc.dp_of(pc.ya, (pc.xb + dx) % pc.nb, pc.core), pc.ctx),
                )
            )
        for dy in range(1, pc.na):
            out.append(
                remote(
                    self.core_in[t].at[dy, 0], self.y_in[t].at[dy - 1],
                    self.y_ss.at[t, dy - 1], self.y_rs.at[t, dy - 1],
                    (pc.dp_of((pc.ya + dy) % pc.na, pc.xb, pc.core), pc.ctx),
                )
            )
        return out

    def z_copies(self, t):
        pc = self.pc
        return [
            remote(
                self.core_in[t].at[0, 0, (pc.zi + d) % pc.nz], self.z_in[t].at[d - 1],
                self.z_ss.at[t, d - 1], self.z_rs.at[t, d - 1],
                (pc.dp, (pc.ctx + d * pc.pre) % pc.nctx),
            )
            for d in range(1, pc.nz)
        ]

    def step(self, t, stage):
        pc = self.pc
        h = pc.nz // 2
        if stage == 0:
            start_all(self.core_copies(t))
        elif stage == 1:
            wait_arrived(self.core_copies(t))
            for dy, dx in self.yx:
                first = self.first(dy, dx, pc.core)
                self.accumulate(t, dy, dx, 0, pc.nz, [lambda z, f=first: self.grads[t][f + z]])
            start_all(self.diag_copies(t))
        elif stage == 2:
            for cp in self.core_copies(t):
                cp.wait_send()
            wait_arrived(self.diag_copies(t))
            for dx in range(1, pc.nb):
                self.accumulate(
                    t, 0, dx, 0, h,
                    [lambda z, dy=dy: self.diag_a[t][dy - 1, dx - 1, z] for dy in range(1, pc.na)],
                )
            for dy in range(1, pc.na):
                self.accumulate(
                    t, dy, 0, h, h,
                    [lambda z, dx=dx: self.diag_b[t][dy - 1, dx - 1, z] for dx in range(1, pc.nb)],
                )
            start_all(self.xy_copies(t))
        elif stage == 3:
            wait_arrived(self.xy_copies(t))
            self.accumulate(
                t, 0, 0, 0, pc.nz,
                [lambda z, i=i: self.x_in[t][i, z] for i in range(pc.nb - 1)]
                + [lambda z, i=i: self.y_in[t][i, z] for i in range(pc.na - 1)],
            )
            start_all(self.z_copies(t))
        else:
            wait_arrived(self.z_copies(t))
            total = self.core_in[t][0, 0, pc.zi].astype(F32)
            for i in range(pc.nz - 1):
                total = total + self.z_in[t][i].astype(F32)
            self.shares[t][...] = total

    def accumulate(self, t, dy, dx, z0, count, others):
        ref = self.core_in[t]

        def one(z, carry):
            total = ref[dy, dx, z0 + z].astype(F32)
            for other in others:
                total = total + other(z).astype(F32)
            ref[dy, dx, z0 + z] = total.astype(BF16)
            return carry

        lax.fori_loop(0, count, one, 0)

    def wait_sent(self):
        for t in range(len(self.grads)):
            for cp in self.diag_copies(t) + self.xy_copies(t) + self.z_copies(t):
                cp.wait_send()


class Rounds(Steps):
    def __init__(self, scatter, stages):
        super().__init__()
        self.scatter, self.stages = scatter, stages
        self.last = []

    def begin(self, t):
        self.scatter.step(t, 0)
        self.todo.append((t, 1))

    def take(self, count):
        out = []
        for _ in range(count):
            if self.todo:
                t, stage = self.todo.pop(0)
                out.append(functools.partial(self.scatter.step, t, stage))
                if stage + 1 < self.stages - 1:
                    self.todo.append((t, stage + 1))
                else:
                    self.last.append(t)
        return out

    def finish(self):
        while self.todo:
            self.run()
        for t in self.last:
            self.scatter.step(t, self.stages - 1)

    def run(self, count=1):
        for fn in self.take(count):
            fn()

    def push(self, *chunks):
        for t in chunks:
            i = [c for c, _ in self.todo].index(t)
            self.todo.insert(0, self.todo.pop(i))
            self.run(1)


def block_at(ref, index, size=BLK):
    return ref.at[pl.ds(pl.multiple_of(index * size, size), size)]


NEG = -1e30


def lane_mask(h):
    lanes = lax.broadcasted_iota(jnp.int32, (1, 128), 1)
    return (lanes < 64) if h == 0 else (lanes >= 64)


def inverse_rms(values):
    return lax.rsqrt(jnp.mean(values * values, axis=-1, keepdims=True) + eps_norm)


def norm_back(grad, values, inverse, gain):
    scaled = grad * gain
    mean = jnp.mean(scaled * values, axis=-1, keepdims=True)
    return (
        inverse * scaled - values * (inverse * inverse * inverse) * mean,
        jnp.sum(grad * values * inverse, axis=0),
    )


FF_STEPS = (((2, 0), (2, 0)), ((2, 1), (2, 1), (2, 0)), ((0, 2), (0, 2), (0, 1)))
AHEAD = 6
BEFORE_X = ("xy", 5)
STRAIGHT = 4
LOOP_ROUNDS = (2, 2, 2, 2, 3, 2)
ORDER_BEFORE = ()
ORDER_AT = {0: (0,), 2: (1,), 3: (2,), 4: (3,), 5: (4,), 6: (5,), 7: (6,), 8: (7,)}
PARTS = ((0, 2), (2, 3), (5, 3))
CHUNKS = ("gate0", "up0", "gate1", "up1", "gate2", "up2")
CHUNKS += ("down0", "down1", "down2", "out", "q", "k", "v", "gain")


def layer_kernel(
    ndp, nctx, pre, share, chunks, order_ref, raw_len_ref, freq_ref, gain1_ref, gain2_ref, x_hbm, dy_hbm, *refs
):
    nt, nch = 6, len(CHUNKS)
    made_here = pre == 1
    shards, refs = refs[: nt - made_here], refs[nt - made_here :]
    full, refs = refs[:nt], refs[nt:]
    fin, refs = refs[:2], refs[2:]
    (s_qkv, s_out, s_gate, s_up, s_down, s_gain), refs = refs[:6], refs[6:]
    (b_gate0, b_up0, b_gate1, b_up1, b_gate2, b_up2, b_down, b_out, b_gain), refs = refs[:9], refs[9:]
    bufs = [refs[i * nch : (i + 1) * nch] for i in range(6)]
    refs = refs[6 * nch :]
    (
        x_v, dy_v, kv_v, dkv_in, tok, plen, hid_v, q_v, lse_v, att_t, n1_t, rope_v, bias_v, gb_v, out_v,
        gain_v, dg_v, tiles_v, len_ref, pad_v,
        tok_ss, tok_rs, ret_ss, ret_rs, len_ss, len_rs, kv_ss, kv_rs, dkv_ss, dkv_rs, load_sem, fin_sem,
        *sems,
    ) = refs
    pc = Place(ndp, nctx, pre)
    rows, width = x_v.shape
    ff = s_gate.shape[1]
    third = width // 3
    slot = BLK // ndp
    n_blocks = ndp * pc.nz
    len_ref[...] = jnp.zeros_like(len_ref)
    len_ref[0 : raw_len_ref.shape[0], 0 : raw_len_ref.shape[1]] = raw_len_ref[...]
    if made_here:
        gain_v[...] = jnp.zeros_like(gain_v)
        gain_v[0:1, 0:share] = gain1_ref[...].astype(F32)
        gain_v[1:2, 0:share] = gain2_ref[...].astype(F32)
        pad_v[...] = gain_v[:, 0:128].astype(BF16)
        shards = (pad_v,) + tuple(shards)
    gather = Gather(pc, shards, full, chunks, sems[:13])
    narrow = slice(0, width)
    grads = [b_gate0, b_up0, b_gate1, b_up1, b_gate2, b_up2]
    grads += [b_down.at[:, :, i * third : (i + 1) * third] for i in range(3)] + [b_out]
    grads += [b.at[:, :, narrow] for b in (b_gate1, b_up1, b_gate2)] + [b_gain]
    shares = [ref.at[:, pl.ds(u * BLK, n * BLK)] for u, n in PARTS for ref in (s_gate, s_up)]
    shares += [s_down.at[:, pl.ds(i * third, third)] for i in range(3)] + [s_out]
    shares += [s_qkv.at[:, pl.ds(i * width, width)] for i in range(3)] + [s_gain]
    scatter = Scatter(pc, grads, shares, bufs, sems[13:])
    rounds = Rounds(scatter, 5)
    chunk = {name: i for i, name in enumerate(CHUNKS)}
    partner = (pc.k * 2 + 1 - pc.core, pc.ctx)
    last_of = {a: max(t for t in range(len(chunks)) if chunks[t][0] == a) for a in range(nt)}
    loads = {}

    def load(name, src, dst):
        loads[name] = (src, dst, len(loads))
        pltpu.make_async_copy(src, dst, load_sem.at[loads[name][2]]).start()

    def ready(*names):
        for name in names:
            src, dst, i = loads[name]
            pltpu.make_async_copy(src, dst, load_sem.at[i]).wait()


    def to_pack(perm, t, m, d):
        dp_to, ctx_to = pc.holder(m, d, pc.ctx)
        half = jnp.where(pc.ctx < pc.g, 0, 1)
        src = perm.at[t, m, pl.ds(pl.multiple_of(d * slot, slot), slot)]
        dst = (x_v, dy_v)[t].at[pl.ds(pl.multiple_of(half * BLK + pc.dp * slot, slot), slot)]
        rs = tok_rs.at[t, half, pc.dp]
        same = (dp_to == pc.dp) & (ctx_to == pc.ctx)
        return same, src, dst, tok_ss.at[t, m, d], rs, (dp_to, ctx_to)

    def to_loader(t, half, b):
        c = layer_rows(pc, half)
        d = pc.k * 2 + pc.pack % 2
        m = pc.pack // 2
        src = (out_v, gb_v)[t].at[pl.ds(pl.multiple_of(half * BLK + b * slot, slot), slot)]
        dst = tok.at[t, m, pl.ds(pl.multiple_of(d * slot, slot), slot)]
        same = (b == pc.dp) & (c == pc.ctx)
        return same, src, dst, ret_ss.at[t, half, b], ret_rs.at[t, m, d], (b, c)

    def send_group(find, gy, gx):
        k = ((pc.ya + gy) % pc.na) * pc.nb + (pc.xb + gx) % pc.nb
        for first in range(2):
            for e in range(2):
                same, src, dst, ss, rs, to = find(first, 2 * k + e)

                @pl.when(same)
                def _():
                    pltpu.make_async_copy(src, dst, rs).start()

                @pl.when(jnp.logical_not(same))
                def _():
                    remote(src, dst, ss, rs, to).start()

    def tokens_sent(find):
        def one(d, carry):
            same, src, dst, ss, rs, to = find(d)

            @pl.when(jnp.logical_not(same))
            def _():
                remote(src, dst, ss, rs, to).wait_send()

            return carry

        lax.fori_loop(0, ndp, one, 0)

    def tokens_arrived(ref, sem_of, base):
        def one(b, carry):
            dst = ref.at[pl.ds(pl.multiple_of(base + b * slot, slot), slot)]
            pltpu.make_async_copy(dst, dst, sem_of(b)).wait()
            return carry

        lax.fori_loop(0, ndp, one, 0)

    def send_back(t):
        for gy, gx in offsets:
            send_group(functools.partial(to_loader, t), gy, gx)

    offsets = [(gy, gx) for gy in range(pc.na) for gx in range(pc.nb)]

    def fin_copy(t):
        return pltpu.make_async_copy(tok.at[t], fin[t], fin_sem.at[t])

    def place_tokens(t):
        for half in range(2):
            tokens_sent(functools.partial(to_loader, t, half))
        for m in range(2):
            tokens_arrived(tok.at[t, m], lambda d, m=m: ret_rs.at[t, m, d], 0)
        fin_copy(t).start()

    steps = Steps()
    len_copy = functools.partial(remote, len_ref, plen, len_ss, len_rs, partner)

    def plan(perm):
        n = len(chunks)
        groups = [(t, gy, gx) for t in range(2) for gy, gx in offsets]

        def tokens(i):
            t, gy, gx = groups[i]
            steps.add(("tok", i), functools.partial(send_group, functools.partial(to_pack, perm, t), gy, gx))

        each = len(offsets) // 4

        def some_tokens(q):
            for i in range(q * each, (q + 1) * each):
                tokens(i)

        def middle(i):
            steps.add(("mid", i), functools.partial(gather.step, i, -1))

        for i in range(2):
            middle(i)
        for i in ORDER_BEFORE:
            some_tokens(i)
        for i in range(n + 3):
            if i >= 3:
                steps.add(("c", i - 3), functools.partial(gather.step, i - 3, 4))
            if i < n:
                steps.add(("z", i), functools.partial(gather.step, i, 1))
                if i + 2 < n:
                    middle(i + 2)
                if i + AHEAD < n:
                    steps.add(("start", i + AHEAD), functools.partial(gather.step, i + AHEAD, 0))
                for q in ORDER_AT.get(i, ()):
                    some_tokens(q)
            if 1 <= i <= n:
                steps.add(("xy", i - 1), functools.partial(gather.step, i - 1, 2))
            if 2 <= i <= n + 1:
                steps.add(("f", i - 2), functools.partial(gather.step, i - 2, 3))
        return len(groups)

    def index(shape, axis):
        return lax.broadcasted_iota(jnp.int32, shape, axis).astype(F32)

    def attention_forward(perm, wqkv, wout, n1_v, att_v):
        load("x_in", x_hbm, perm.at[0])
        load("dy_in", dy_hbm, perm.at[1])
        for t in range(len(chunks)):
            gather.own_copy(t).start()
        greet_all(pc)
        for t, name in enumerate(("x_in", "dy_in")):
            ready(name)
            for m in range(2):
                hot = (lax.broadcasted_iota(jnp.int32, (BLK, BLK), 0) == order_ref[m]).astype(BF16)
                perm[t, m] = lax.dot_general(
                    hot, perm[t, m], TN, preferred_element_type=F32
                ).astype(BF16)
        met_all(pc)
        for t in range(AHEAD):
            gather.step(t, 0)
        len_copy().start()
        n_groups = plan(perm)
        steps.until(("xy", 0))

        len_copy().wait_recv()
        lens = jnp.where(pc.pack % 2 == pc.core, len_ref[...], plen[...]).astype(F32)
        lens = jnp.where(pc.pack // 2 == 0, lens[0:1], lens[1:2])
        lane = lax.broadcasted_iota(jnp.int32, (1, 128), 1)
        ends = [jnp.sum(jnp.where(lane <= i, lens, 0.0), axis=1, keepdims=True) for i in range(4)]
        sizes = [jnp.sum(jnp.where(lane == i, lens, 0.0), axis=1, keepdims=True) for i in range(4)]

        def segment(at):
            seg = jnp.zeros(at.shape, F32)
            start = jnp.zeros(at.shape, F32)
            for end, size in zip(ends, sizes):
                passed = (at >= end).astype(F32)
                seg = seg + passed
                start = start + passed * size
            return seg, start

        sign = jnp.where(lane % 64 < 32, -1.0, 1.0)
        at = 0
        for half in range(2):
            base = (layer_rows(pc, half) * BLK).astype(F32)
            here = base + index((BLK, 128), 0)
            _, start = segment(here)
            angle = (here - start) * freq_ref[0:1]
            rope_v[half * BLK : (half + 1) * BLK, 0:128] = jnp.cos(angle)
            rope_v[half * BLK : (half + 1) * BLK, 128:256] = jnp.sin(angle) * sign
            qrow = base + index((1, BLK), 1)
            segq, _ = segment(qrow)
            for kb in range((half + 1) * pc.g):
                krow = kb * BLK + index((BLK, BLK), 0)
                segk, _ = segment(kb * BLK + index((BLK, 1), 0))
                bias_v[at : at + BLK] = jnp.where((segk == segq) & (krow <= qrow), 0.0, NEG).astype(BF16)
                at += BLK
        steps.until(("c", 0))
        load("tiles", full[0], tiles_v)
        ready("tiles")
        gain_v[0:1] = gain_row(tiles_v[...], 0, share, width)
        gain_v[1:2] = gain_row(tiles_v[...], 1, share, width)
        steps.until(("tok", n_groups // 2 - 1))
        steps.until(BEFORE_X)
        for half in range(2):
            tokens_arrived(x_v, lambda b, half=half: tok_rs.at[0, half, b], half * BLK)
        x = x_v[...].astype(F32)
        n1_v[...] = (x * inverse_rms(x) * gain_v[0:1]).astype(BF16)
        n1_t[...] = n1_v[...].T
        steps.run(2)

        cos_t, sin_t = rope_v[:, 0:128], rope_v[:, 128:256]

        def kv_copies(part):
            copies = []
            for half in range(2):
                ref = kv_v.at[
                    pl.ds(pl.multiple_of(layer_rows(pc, half) * BLK, BLK), BLK),
                    pl.ds(part * width, width),
                ]
                for o in range(1, pc.g):
                    copies.append(
                        remote(
                            ref, ref, kv_ss.at[part, half, o - 1], kv_rs.at[part, half, o - 1],
                            pc.member((pc.j + o) % pc.g),
                        )
                    )
            return copies

        def project(base, put, rope):
            def one(i, carry):
                u = jnp.dot(
                    n1_v[...], wqkv[:, pl.ds(pl.multiple_of(base + i * BLK, BLK), BLK)],
                    preferred_element_type=F32,
                )
                if rope:
                    u = turned(u, cos_t, sin_t)
                put(i, u.astype(BF16))
                return carry

            lax.fori_loop(0, width // BLK, one, 0)

        def to_kv(part):
            def put(i, u):
                for half in range(2):
                    kv_v[
                        pl.ds(pl.multiple_of(layer_rows(pc, half) * BLK, BLK), BLK),
                        pl.ds(pl.multiple_of(part * width + i * BLK, BLK), BLK),
                    ] = u[half * BLK : (half + 1) * BLK]

            return put

        def to_q(i, u):
            q_v[:, cols(i)] = u

        steps.until(("c", last_of[1]))
        load("wqkv", full[1], wqkv)
        ready("wqkv")
        project(width, to_kv(0), True)
        start_all(kv_copies(0))
        steps.run(1)
        project(2 * width, to_kv(1), False)
        start_all(kv_copies(1))
        steps.run(1)
        project(0, to_q, True)
        steps.run(2)
        wait_arrived(kv_copies(0) + kv_copies(1))

        def pair(hp):
            hc = cols(hp, 128)
            vc = pl.ds(pl.multiple_of(width + hp * 128, 128), 128)
            at = 0
            for half in range(2):
                nk = (half + 1) * pc.g * BLK
                rr = slice(half * BLK, (half + 1) * BLK)
                qp = q_v[rr, hc]
                both = []
                for h in range(2):
                    qm = (jnp.where(lane_mask(h), qp, 0) * 0.125).astype(BF16)
                    s = lax.dot_general(kv_v[0:nk, hc], qm, NT, preferred_element_type=F32)
                    s = s + bias_v[at : at + nk].astype(F32)
                    top = jnp.max(s, axis=0, keepdims=True)
                    p = jnp.exp(s - top)
                    total = jnp.sum(p, axis=0, keepdims=True)
                    p = (p * (1.0 / total)).astype(BF16)
                    both.append(
                        lax.dot_general(kv_v[0:nk, vc], p, TN, preferred_element_type=F32)
                    )
                    lse_v[hp, h : h + 1, rr] = top + jnp.log(total)
                sub = lax.broadcasted_iota(jnp.int32, (128, BLK), 0)
                o = jnp.where(sub < 64, both[0], both[1])
                att_v[rr, hc] = o.T.astype(BF16)
                att_t[hc, rr] = o.astype(BF16)
                at += nk

        loop_with_steps(HEADS // 2, pair, [steps.take(2) for _ in range(HEADS // 2)])
        steps.until(("c", last_of[2]))
        load("wout", full[2], wout)
        ready("wout")
        hid_v[...] = x_v[...].astype(F32) + jnp.dot(
            att_v[...], wout[...], preferred_element_type=F32
        )
        steps.until(("tok", n_groups - 1))
        for t in range(2):
            for m in range(2):
                tokens_sent(functools.partial(to_pack, perm, t, m))
        for half in range(2):
            tokens_arrived(dy_v, lambda b, half=half: tok_rs.at[1, half, b], half * BLK)
        for cp in kv_copies(0) + kv_copies(1):
            cp.wait_send()

    pl.run_scoped(
        attention_forward,
        pltpu.VMEM((2, 2, BLK, width), BF16), pltpu.VMEM((width, 3 * width), BF16),
        pltpu.VMEM((width, width), BF16), pltpu.VMEM((rows, width), BF16),
        pltpu.VMEM((rows, width), BF16),
    )


    def feed_forward(wdown, wgate, wup, n2_v, n2_t, gn2, res):
        hid = hid_v[...]
        n2_v[...] = (hid * inverse_rms(hid) * gain_v[1:2]).astype(BF16)
        n2_t[...] = n2_v[...].T
        res[...] = hid
        gn2[...] = jnp.zeros_like(gn2)
        steps.run(2)
        steps.until(("c", last_of[5]))
        load("wdown", full[5], wdown)
        per = BLK // b_down.shape[1]

        def part(which, c):
            cc = cols(c)
            rr = cols(PARTS[which][0] + c)
            g = jnp.dot(n2_v[...], wgate[:, cc], preferred_element_type=F32)
            u = jnp.dot(n2_v[...], wup[:, cc], preferred_element_type=F32)
            gi = lax.dot_general(dy_v[...], wdown[rr, :], NT, preferred_element_type=F32)
            sig = 1.0 / (1.0 + jnp.exp(-g))
            act = g * sig
            inner = (act * u).astype(BF16)
            gg = (gi * u * (sig * (1.0 + g * (1.0 - sig)))).astype(BF16)
            gu = (gi * act).astype(BF16)
            res[...] += jnp.dot(inner, wdown[rr, :], preferred_element_type=F32)
            gn2[...] += lax.dot_general(
                gg, wgate[:, cc], NT, preferred_element_type=F32
            ) + lax.dot_general(gu, wup[:, cc], NT, preferred_element_type=F32)
            for buf, value in (((b_gate0, b_gate1, b_gate2)[which], gg), ((b_up0, b_up1, b_up2)[which], gu)):
                d = jnp.dot(n2_t[...], value, preferred_element_type=F32)
                buf[:, :, cc] = d.reshape(n_blocks, -1, BLK).astype(BF16)
            d = jnp.dot(inner.T, dy_v[...], preferred_element_type=F32)
            b_down[pl.ds((PARTS[which][0] + c) * per, per)] = d.reshape(per, -1, width).astype(BF16)

        def load_part(which):
            n = len(chunks)
            steps.until(("c", n - 5 + 2 * which))
            at, count = PARTS[which]
            src, dst = pl.ds(at * BLK, count * BLK), pl.ds(0, count * BLK)
            load(f"wgate{which}", full[3].at[:, src], wgate.at[:, dst])
            load(f"wup{which}", full[4].at[:, src], wup.at[:, dst])
            ready(f"wgate{which}", f"wup{which}")

        for which, (_at, count) in enumerate(PARTS):
            load_part(which)
            if which == 0:
                ready("wdown")
            groups = []
            for i in range(count):
                gathers, sums = FF_STEPS[which][i]
                groups.append(steps.take(gathers) + rounds.take(sums))
            loop_with_steps(count, functools.partial(part, which), groups)
            rounds.begin(chunk[f"gate{which}"])
            rounds.begin(chunk[f"up{which}"])
        while steps.todo:
            steps.run()
        for name in ("down0", "down1", "down2"):
            rounds.begin(chunk[name])
        out_v[...] = res[...].astype(BF16)
        hid = hid_v[...]
        back, d_gain = norm_back(gn2[...], hid, inverse_rms(hid), gain_v[1:2])
        dg_v[1:2] = d_gain.reshape(1, width)
        gh = dy_v[...].astype(F32) + back
        hid_v[...] = gh
        gb_v[...] = gh.astype(BF16)
        rounds.push(*[chunk[name] for name in ("gate2", "up2", "down0", "down1", "down2")])

    pl.run_scoped(
        feed_forward,
        pltpu.VMEM((ff, width), BF16), pltpu.VMEM((width, 3 * BLK), BF16),
        pltpu.VMEM((width, 3 * BLK), BF16), pltpu.VMEM((rows, width), BF16),
        pltpu.VMEM((width, rows), BF16), pltpu.VMEM((rows, width), F32), pltpu.VMEM((rows, width), F32),
    )


    def head_pairs(gqkv, wout, gatt_v, acc):
        load("wout_back", full[2], wout)
        ready("wout_back")

        def out_part(c, carry):
            d = jnp.dot(att_t[...], gb_v[:, cols(c)], preferred_element_type=F32)
            b_out[:, :, cols(c)] = d.reshape(n_blocks, -1, BLK).astype(BF16)
            gatt_v[:, cols(c)] = lax.dot_general(
                gb_v[...], wout[cols(c), :], NT, preferred_element_type=F32
            ).astype(BF16)
            return carry

        lax.fori_loop(0, width // BLK, out_part, 0)
        rounds.begin(chunk["out"])
        cos_t, sin_t = rope_v[:, 0:128], rope_v[:, 128:256]

        def pair(hp):
            hc = cols(hp, 128)
            vc = pl.ds(pl.multiple_of(width + hp * 128, 128), 128)
            acc[...] = jnp.zeros_like(acc)
            at = 0
            for half in range(2):
                nk = (half + 1) * pc.g * BLK
                rr = slice(half * BLK, (half + 1) * BLK)
                qp, dop = q_v[rr, hc], gatt_v[rr, hc]
                both = []
                for h in range(2):
                    qm = (jnp.where(lane_mask(h), qp, 0) * 0.125).astype(BF16)
                    dom = jnp.where(lane_mask(h), dop, 0).astype(BF16)
                    s = lax.dot_general(kv_v[0:nk, hc], qm, NT, preferred_element_type=F32)
                    p = jnp.exp(s + bias_v[at : at + nk].astype(F32) - lse_v[hp, h : h + 1, rr])
                    dp = lax.dot_general(kv_v[0:nk, vc], dom, NT, preferred_element_type=F32)
                    weighted = jnp.sum(p * dp, axis=0, keepdims=True)
                    ds = (p * (dp - weighted)).astype(BF16)
                    acc[0:nk, 0:128] += jnp.dot(ds, qm, preferred_element_type=F32)
                    acc[0:nk, 128:256] += jnp.dot(
                        p.astype(BF16), dom, preferred_element_type=F32
                    )
                    both.append(
                        lax.dot_general(kv_v[0:nk, hc], ds, TN, preferred_element_type=F32)
                    )
                sub = lax.broadcasted_iota(jnp.int32, (128, BLK), 0)
                dq = (jnp.where(sub < 64, both[0], both[1]) * 0.125).T
                gqkv[rr, hc] = turned(dq, cos_t[rr], -sin_t[rr]).astype(BF16)
                at += nk
            kv_v[:, hc] = acc[:, 0:128].astype(BF16)
            kv_v[:, vc] = acc[:, 128:256].astype(BF16)

        groups = [rounds.take(n) for n in LOOP_ROUNDS]
        for i, (gy, gx) in enumerate(offsets):
            groups[min(1 + i, 5)].append(
                functools.partial(send_group, functools.partial(to_loader, 0), gy, gx)
            )
        loop_with_steps(HEADS // 2, pair, groups)

    def last_part(gqkv, wqkv):
        load("wqkv_back", full[1], wqkv)
        cos_t, sin_t = rope_v[:, 0:128], rope_v[:, 128:256]
        copies = []
        for o in range(1, pc.g):
            to = (pc.j + o) % pc.g
            for half in range(2):
                where = to if half == 0 else 2 * pc.g - 1 - to
                copies.append(
                    remote(
                        block_at(kv_v, where), dkv_in.at[o - 1, half],
                        dkv_ss.at[half, o - 1], dkv_rs.at[half, o - 1], pc.member(to),
                    )
                )
        start_all(copies)

        def weight_grad(name, base, buf):
            def one(c, carry):
                d = jnp.dot(
                    n1_t[...], gqkv[:, pl.ds(pl.multiple_of(base + c * BLK, BLK), BLK)],
                    preferred_element_type=F32,
                )
                buf[:, :, cols(c)] = d.reshape(n_blocks, -1, BLK).astype(BF16)
                return carry

            lax.fori_loop(0, width // BLK, one, 0)
            rounds.begin(chunk[name])

        while any(t in (chunk["gate1"], chunk["up1"], chunk["gate2"]) and st < 3 for t, st in rounds.todo):
            rounds.run()
        weight_grad("q", 0, b_gate1)
        rounds.run(2)
        wait_arrived(copies)
        rounds.push(chunk["q"])
        for half in range(2):
            own = pl.ds(pl.multiple_of(layer_rows(pc, half) * BLK, BLK), BLK)
            rr = slice(half * BLK, (half + 1) * BLK)
            for i in range(2 * width // BLK):
                cc = slice(i * BLK, (i + 1) * BLK)
                total = kv_v[own, cc].astype(F32)
                for o in range(1, pc.g):
                    total = total + dkv_in[o - 1, half, :, cc].astype(F32)
                if i < width // BLK:
                    total = turned(total, cos_t[rr], -sin_t[rr])
                gqkv[rr, width + i * BLK : width + (i + 1) * BLK] = total.astype(BF16)
        weight_grad("k", width, b_up1)
        weight_grad("v", 2 * width, b_gate2)
        rounds.push(chunk["k"])
        rounds.run(2)
        ready("wqkv_back")
        gn1 = lax.dot_general(gqkv[...], wqkv[...], NT, preferred_element_type=F32)
        x = x_v[...].astype(F32)
        back, d_gain = norm_back(gn1, x, inverse_rms(x), gain_v[0:1])
        dg_v[0:1] = d_gain.reshape(1, width)
        gb_v[...] = (hid_v[...] + back).astype(BF16)
        send_back(1)
        rounds.push(chunk["v"])
        row = lax.broadcasted_iota(jnp.int32, (b_gain.shape[0] * b_gain.shape[1], width), 0)
        col = lax.broadcasted_iota(jnp.int32, row.shape, 1)
        spread = jnp.where(row % SLOTS == 0, dg_v[0:1], jnp.where(row % SLOTS == 1, dg_v[1:2], 0.0))
        spread = jnp.where(row // SLOTS == col // share, spread, 0.0).astype(BF16)
        lane = lax.broadcasted_iota(jnp.int32, (width, 128), 1)
        col = lax.broadcasted_iota(jnp.int32, (width, 128), 0)
        tiles = jnp.dot(spread, (col % share == lane).astype(BF16), preferred_element_type=F32)
        b_gain[...] = tiles.reshape(b_gain.shape).astype(BF16)
        rounds.begin(chunk["gain"])
        rounds.run(4)
        rounds.push(chunk["gain"])
        place_tokens(0)
        for cp in copies:
            cp.wait_send()

    def attention_backward(gqkv):
        pl.run_scoped(
            functools.partial(head_pairs, gqkv),
            pltpu.VMEM((width, width), BF16), pltpu.VMEM((rows, width), BF16),
            pltpu.VMEM((pc.g * rows, 256), F32),
        )
        pl.run_scoped(
            functools.partial(last_part, gqkv), pltpu.VMEM((width, 3 * width), BF16)
        )

    pl.run_scoped(attention_backward, pltpu.VMEM((rows, 3 * width), BF16))
    rounds.finish()
    place_tokens(1)
    len_copy().wait_send()
    gather.wait_sent()
    scatter.wait_sent()
    for t in range(2):
        fin_copy(t).wait()


def finish_kernel(n, share, order_ref, *refs):
    tokens, kept, refs = refs[:2], refs[2 : 2 + n], refs[2 + n :]
    outs, copies, refs = refs[:2], refs[2 : 2 + n + (n > 0)], refs[2 + n + (n > 0) :]
    tok, fin, in_sem, out_sem, *held = refs
    moves = [pltpu.make_async_copy(tokens[t], tok.at[t], in_sem.at[t]) for t in range(2)]
    moves += [pltpu.make_async_copy(kept[i], held[i], in_sem.at[2 + i]) for i in range(n)]
    start_all(moves)
    away = []
    for t in range(2):
        moves[t].wait()
        for m in range(2):
            hot = (lax.broadcasted_iota(jnp.int32, (BLK, BLK), 0) == order_ref[m]).astype(BF16)
            fin[t, m] = jnp.dot(hot, tok[t, m], preferred_element_type=F32).astype(BF16)
        away.append(pltpu.make_async_copy(fin.at[t], outs[t], out_sem.at[t]))
        away[-1].start()
    for i in range(n - 1):
        moves[2 + i].wait()
        away.append(pltpu.make_async_copy(held[i], copies[i], out_sem.at[2 + i]))
        away[-1].start()
    if n:
        moves[1 + n].wait()
        for i, dst in enumerate(copies[n - 1 :]):
            dst[...] = held[n - 1][i : i + 1, 0:share]
    for cp in away:
        cp.wait()


def finish(share, order, tokens, kept):
    n = len(kept)
    out = [jax.ShapeDtypeStruct(v.shape, v.dtype) for v in list(tokens) + list(kept[:-1])]
    specs = [ANY] * len(out)
    if n:
        out += [jax.ShapeDtypeStruct((1, share), F32)] * 2
        specs += [VM] * 2
    return pl.pallas_call(
        functools.partial(finish_kernel, n, share),
        out_shape=out,
        in_specs=[VM] + [ANY] * (2 + n),
        out_specs=specs,
        scratch_shapes=[
            pltpu.VMEM((2,) + tokens[0].shape, BF16), pltpu.VMEM((2,) + tokens[0].shape, BF16),
            pltpu.SemaphoreType.DMA((2 + n,)), pltpu.SemaphoreType.DMA((2 + n,)),
        ]
        + [pltpu.VMEM(v.shape, v.dtype) for v in kept],
        compiler_params=pltpu.CompilerParams(vmem_limit_bytes=63 << 20),
        name="finish",
    )(order, *tokens, *kept)


def layer(ndp, nctx, pre, share, order, lens, freq, gains, x, dy, shards):
    nz, na, nb, g = nctx // pre, ndp // 4, 2, nctx // 2
    n_blocks = ndp * nz
    rows, width = 2 * BLK, x.shape[-1]
    ff = shards[3].shape[1]
    r, rd, rg = width // n_blocks, ff // n_blocks, SLOTS * pre
    dma = pltpu.SemaphoreType.DMA
    chunks = [(0, 0, 128)]
    chunks += [(1, width, width), (1, 2 * width, width), (1, 0, width), (2, 0, width)]
    chunks += [(5, 0, width // 2), (5, width // 2, width // 2)]
    chunks += [(a, u * BLK, n * BLK) for u, n in PARTS for a in (3, 4)]
    m = len(chunks)
    given = shards[1:] if pre == 1 else shards
    full = [jax.ShapeDtypeStruct((n_blocks * s.shape[0], s.shape[1]), BF16) for s in shards]
    out_shape = full + [jax.ShapeDtypeStruct((2, BLK, width), BF16)] * 2
    out_shape += [
        jax.ShapeDtypeStruct(s, F32)
        for s in ((r, 3 * width), (r, width), (r, ff), (r, ff), (rd, width), (rg, 128))
    ]
    specs = dict(
        **{f"{name}{i}": (r, n * BLK) for i, (_u, n) in enumerate(PARTS) for name in ("gate", "up")},
        down0=(rd, width // 3), down1=(rd, width // 3), down2=(rd, width // 3), out=(r, width),
        q=(r, width), k=(r, width), v=(r, width), gain=(rg, 128),
    )
    spec = [specs[name] for name in CHUNKS]
    n = len(CHUNKS)
    scratch = [pltpu.VMEM((n_blocks,) + s, BF16) for s in spec[:6]]
    scratch += [
        pltpu.VMEM((n_blocks, rd, width), BF16), pltpu.VMEM((n_blocks, r, width), BF16),
        pltpu.VMEM((n_blocks, rg, 128), BF16),
    ]
    scratch += [pltpu.VMEM((na, nb, nz) + s, BF16) for s in spec]
    scratch += [pltpu.VMEM((na - 1, nb - 1, nz // 2) + s, BF16) for s in spec]
    scratch += [pltpu.VMEM((na - 1, nb - 1, nz // 2) + s, BF16) for s in spec]
    scratch += [pltpu.VMEM((nb - 1, nz) + s, BF16) for s in spec]
    scratch += [pltpu.VMEM((na - 1, nz) + s, BF16) for s in spec]
    scratch += [pltpu.VMEM((nz - 1,) + s, BF16) for s in spec]
    scratch += [
        pltpu.VMEM((rows, width), BF16), pltpu.VMEM((rows, width), BF16),
        pltpu.VMEM((g * rows, 2 * width), BF16), pltpu.VMEM((g - 1, 2, BLK, 2 * width), BF16),
        pltpu.VMEM((2, 2, BLK, width), BF16), pltpu.VMEM((8, 128), jnp.int32),
        pltpu.VMEM((rows, width), F32), pltpu.VMEM((rows, width), BF16),
        pltpu.VMEM((HEADS // 2, 2, rows), F32), pltpu.VMEM((width, rows), BF16),
        pltpu.VMEM((width, rows), BF16), pltpu.VMEM((rows, 256), F32),
        pltpu.VMEM((3 * g * BLK, BLK), BF16), pltpu.VMEM((rows, width), BF16),
        pltpu.VMEM((rows, width), BF16), pltpu.VMEM((8, width), F32), pltpu.VMEM((8, width), F32),
        pltpu.VMEM(full[0].shape, BF16), pltpu.VMEM((8, 128), jnp.int32), pltpu.VMEM((SLOTS, 128), BF16),
        dma((2, 2, ndp)), dma((2, 2, ndp)), dma((2, 2, ndp)), dma((2, 2, ndp)), dma, dma,
        dma((2, 2, g - 1)), dma((2, 2, g - 1)), dma((2, g - 1)), dma((2, g - 1)),
        dma((20,)), dma((2,)),
        dma((m,)), dma((m, nz - 1)), dma((m, nz - 1)),
        dma((m, nb - 1)), dma((m, nb - 1)), dma((m, na - 1)), dma((m, na - 1)),
        dma((m, nb - 1, na - 1)), dma((m, nb - 1, na - 1)),
        dma((m, nb - 1, na - 1)), dma((m, nb - 1, na - 1)),
        dma((m, na, nb)), dma((m, na, nb)),
        dma((n, na, nb)), dma((n, na, nb)),
        dma((n, na - 1, nb - 1)), dma((n, na - 1, nb - 1)),
        dma((n, na - 1, nb - 1)), dma((n, na - 1, nb - 1)),
        dma((n, nb - 1)), dma((n, nb - 1)), dma((n, na - 1)), dma((n, na - 1)),
        dma((n, nz - 1)), dma((n, nz - 1)),
    ]
    res = pl.pallas_call(
        functools.partial(layer_kernel, ndp, nctx, pre, share, chunks),
        out_shape=out_shape,
        in_specs=[VM] * 5 + [ANY] * (2 + len(given)),
        out_specs=[ANY] * (len(shards) + 2) + [VM] * 6,
        scratch_shapes=scratch,
        compiler_params=pltpu.CompilerParams(
            collective_id=0, has_side_effects=True, vmem_limit_bytes=63 << 20
        ),
        name="layer",
    )(order, lens, freq, *gains, x, dy, *given)
    return res[len(shards) :]


def per_device(
    inputs, cotangent, lengths, send_order,
    norm1_gain, qkv_weight, out_weight, norm2_gain, gate_weight, up_weight, down_weight,
):
    ndp, nctx = lax.axis_size("dp"), lax.axis_size("ctx")
    head = inputs.shape[2] // HEADS
    share = norm1_gain.shape[0]
    pre = 1
    while (share * pre) % 8:
        pre *= 2
    gains = (norm1_gain.reshape(1, share), norm2_gain.reshape(1, share))
    pad = jax.ShapeDtypeStruct((SLOTS, 128), BF16)
    if pre > 1:
        pad = jnp.pad(jnp.concatenate(gains), ((0, SLOTS - 2), (0, 128 - share)))
    shards = [pad, qkv_weight, out_weight, gate_weight, up_weight, down_weight]
    teams = [[t * pre + i for i in range(pre)] for t in range(nctx // pre)]
    if pre > 1:
        shards = [
            lax.all_gather(w, "ctx", axis_index_groups=teams, axis=0, tiled=True) for w in shards
        ]
    half = head // 2
    frequency = np.float32(rope_base) ** (-(np.arange(half, dtype=np.float32) * 2.0 / head))
    frequency = np.tile(frequency.astype(np.float32), (8, 128 // half))
    back_out, back_gin, *owned = layer(
        ndp, nctx, pre, share, send_order, lengths[:, 0], frequency, gains, inputs, cotangent, shards
    )
    if pre > 1:
        owned = [
            lax.psum_scatter(w, "ctx", axis_index_groups=teams, scatter_dimension=0, tiled=True)
            for w in owned
        ]
        fin_out, fin_gin = finish(share, send_order, (back_out, back_gin), [])
        s_qkv, s_out, s_gate, s_up, s_down, s_gains = owned
        g1, g2 = s_gains[0:1, :share], s_gains[1:2, :share]
    else:
        fin_out, fin_gin, s_qkv, s_out, s_gate, s_up, s_down, g1, g2 = finish(
            share, send_order, (back_out, back_gin), owned
        )
    return (
        fin_out, fin_gin, g1.reshape(share), s_qkv, s_out, g2.reshape(share), s_gate, s_up, s_down,
    )


def solution(mesh):
    both = ("dp", "ctx")
    in_specs = (
        P(None, both, None), P(None, both, None), P(None, "dp", None), P(None, both, None),
        P(both), P(both, None), P(both, None), P(both), P(both, None), P(both, None), P(both, None),
    )
    out_specs = (
        P(None, both, None), P(None, both, None),
        P(both), P(both, None), P(both, None), P(both), P(both, None), P(both, None), P(both, None),
    )
    return jax.shard_map(
        per_device, mesh=mesh, in_specs=in_specs, out_specs=out_specs, check_vma=False
    )
```
